32 devices in a mesh: dp: 4 (over x, core), fsdp: 8 (over z, y).
Axes of the slice: x: 2, y: 2, z: 4, core: 2. Of those that a mesh axis runs over, the one named last changes fastest.
Arguments:
- inputs: bfloat16 [8192, 384], P(('dp', 'fsdp')), may hold values from -6 to 6
- cotangent: bfloat16 [8192, 384], P(('dp', 'fsdp')), may hold values from -6 to 6
- master: float32 [1774848], P(('dp', 'fsdp'))
- first_moment: float32 [1774848], P(('dp', 'fsdp')), may hold values from -1.5 to 1.5
- second_moment: float32 [1774848], P(('dp', 'fsdp')), may hold values from 0.005 to 0.2
- image_ids: int32 [8192], replicated, may hold values from 0 to 6, as said below
- spans: int32 [32, 2], replicated, may hold values from 0 to 31, as said below
Outputs:
- block_out: bfloat16 [8192, 384], P(('dp', 'fsdp'))
- input_grad: float32 [8192, 384], P(('dp', 'fsdp'))
- weight_grad: float32 [1774848], P(('dp', 'fsdp'))
- grad_norm: float32 [1], replicated
- new_first: float32 [1774848], P(('dp', 'fsdp'))
- new_second: float32 [1774848], P(('dp', 'fsdp'))
- new_master: float32 [1774848], P(('dp', 'fsdp'))
The draws below stay inside these ranges and needn't reach their ends.
Inputs may be any that keep to these rules, and one draw needn't show every extreme that they name: `image_ids`: image numbers start at 0 and never fall; they rise by one at the first token of each image; every image has exactly 1370 tokens except the first and the last, which may have fewer; the largest image number is the same in every draw. `spans`: row d holds the first and the last device whose tokens belong to an image that also has tokens on device d.
All inputs are finite; a program needn't handle non-finite values.
Results may differ from the reference program's by a relative error of at most 0.011.
Values may be sent and summed in bfloat16 or wider, within the bound.
No kernel may reach another device: no remote copies, remote signals or barrier semaphores. Data moves between devices by JAX's collectives and lax.ppermute only.
A program may use at most 192 MiB of HBM per device.

```python
import math
import jax
import jax.numpy as jnp
from jax import lax

D = 384
HEADS = 6
HEAD_DIM = 64
FF = 1536
TOK_DEV = 256
IMG = 1370
TOKENS = 8192
P_SIZE = 1774848


def image_phase(key):
    remain = (TOKENS - 1) % IMG
    upper = 2 * remain // IMG
    lowest = upper * (IMG - remain)
    highest = IMG - remain + upper * remain
    return jax.random.randint(jax.random.fold_in(key, 7), (), lowest, highest, dtype=jnp.int32)


def draw_image_ids(key, part):
    phase = image_phase(key)
    positions = jnp.arange(TOKENS, dtype=jnp.int32)
    return ((positions + phase) // IMG).astype(jnp.int32)


def draw_spans(key, part):
    phase = image_phase(key)
    count = TOKENS // TOK_DEV
    first = jnp.arange(count, dtype=jnp.int32) * TOK_DEV
    last = first + TOK_DEV - 1
    first_image = (first + phase) // IMG
    last_image = (last + phase) // IMG
    begin = jnp.maximum(first_image * IMG - phase, 0)
    finish = jnp.minimum((last_image + 1) * IMG - phase - 1, TOKENS - 1)
    return jnp.stack([begin // TOK_DEV, finish // TOK_DEV], axis=1).astype(jnp.int32)


def draw_master(key, part):
    root_width = D ** (-0.5)
    root_hidden = FF ** (-0.5)
    specs = [(D, 1.0, 0.15, 0), (D, 0.0, 0.1, 0), (3 * D * D, 0.0, root_width, 0), (2 * D, 0.0, 0.1, 0), (D * D, 0.0, 8.0 * root_width, 0), (D, 0.0, 0.1, 0), (D, 1.0, 0.4, 1), (D, 1.0, 0.15, 0), (D, 0.0, 0.1, 0), (D * FF, 0.0, root_width, 0), (FF, 0.0, 0.2, 0), (FF * D, 0.0, 1.5 * root_hidden, 0), (D, 0.0, 0.1, 0), (D, 1.0, 0.4, 1)]
    pieces = []
    for index, spec in enumerate(specs):
        count, center, spread, kind = spec
        subkey = jax.random.fold_in(key, 100 + index)
        if kind == 0:
            normal = jnp.clip(jax.random.normal(subkey, (count,), jnp.float32), -5.0, 5.0)
            pieces.append(center + spread * normal)
        else:
            pieces.append(jax.random.uniform(subkey, (count,), jnp.float32, center - spread, center + spread))
    return jnp.concatenate(pieces).astype(jnp.float32)


def shard_levels(own_key, dims, shards, low, top_value):
    def one(position, shards_of):
        steps = jax.random.uniform(jax.random.fold_in(jax.random.fold_in(own_key, 6), position), (shards_of,), jnp.float32, low / len(shards), top_value / len(shards))
        return jnp.repeat(jnp.exp(steps), dims[position] // shards_of).reshape((-1,) + (1,) * (len(dims) - position - 1))

    loudness = one(*shards[0])
    for cut in shards[1:]:
        loudness = loudness * one(*cut)
    return loudness


def centred(own_key, dims, scale, reach, shards=(), kind=jnp.bfloat16):
    drawn = scale * jax.random.normal(own_key, dims, jnp.float32)
    if shards:
        drawn = drawn * shard_levels(own_key, dims, shards, -0.22, 0.18)
    return jnp.clip(drawn, -reach, reach).astype(kind)


def setup_inputs(seed: int = 0) -> dict:
    key_list = jax.random.split(jax.random.key(seed), 8)
    return {
        "inputs": centred(key_list[0], (TOKENS, D), 1.0, 6.0, ((0, 32),)),
        "cotangent": centred(key_list[1], (TOKENS, D), 1.0, 6.0, ((0, 32),)),
        "master": draw_master(jax.random.fold_in(key_list[7], 71), 0),
        "first_moment": centred(key_list[3], (P_SIZE,), 0.25, 1.5, ((0, 32),), jnp.float32),
        "second_moment": jnp.clip(jnp.exp(math.log(0.2) - 3.6888795 * jax.random.uniform(key_list[4], (P_SIZE,), jnp.float32) ** shard_levels(key_list[4], (P_SIZE,), ((0, 32),), -0.2, 0.2)), 0.005, 0.2),
        "image_ids": draw_image_ids(jax.random.fold_in(key_list[7], 71), 0),
        "spans": draw_spans(jax.random.fold_in(key_list[7], 71), 0),
    }


@jax.custom_vjp
def low(v):
    return lax.optimization_barrier(v.astype(jnp.bfloat16)).astype(jnp.float32)

@jax.custom_vjp
def low_back(v):
    return v

def low_keep(v):
    return (low(v), None)

def low_pass(kept, grad):
    return (grad,)

def back_keep(v):
    return (v, None)

def back_low(kept, grad):
    return (low(grad),)
low.defvjp(low_keep, low_pass)
low_back.defvjp(back_keep, back_low)
HIGH = lax.Precision.HIGHEST
LN_EPS = 1e-06
BETA_ONE = 0.5
BETA_TWO = 0.6
LEARN_RATE = 0.01
WEIGHT_DECAY = 0.05
ADAM_EPS = 1e-08
CLIP_RATIO = 0.25
MASKED = -1e+30

def shapes(width, hidden):
    return [(width,), (width,), (width, 3 * width), (2 * width,), (width, width), (width,), (width,), (width,), (width,), (width, hidden), (hidden,), (hidden, width), (width,), (width,)]

def unpack(flat, width, hidden):
    pieces = []
    offset = 0
    for shape in shapes(width, hidden):
        count = math.prod(shape)
        pieces.append(flat[offset:offset + count].reshape(shape))
        offset += count
    return pieces

def layer_norm(values, gain, shift):
    center = values - lax.optimization_barrier(jnp.mean(values, axis=-1, keepdims=True))
    spread = lax.optimization_barrier(jnp.mean(center * center, axis=-1, keepdims=True))
    return center * lax.rsqrt(spread + LN_EPS) * gain + shift

def attention(query, keys, values, image_ids, spans):
    rows = TOK_DEV
    count = TOKENS // rows
    span_len = rows + 2 * IMG
    heads = query.reshape(TOKENS, HEADS, HEAD_DIM)
    pad_keys = jnp.pad(keys.reshape(TOKENS, HEADS, HEAD_DIM), ((IMG, IMG), (0, 0), (0, 0)))
    pad_values = jnp.pad(values.reshape(TOKENS, HEADS, HEAD_DIM), ((IMG, IMG), (0, 0), (0, 0)))
    pad_ids = jnp.pad(image_ids, (IMG, IMG), constant_values=-1)
    scale = HEAD_DIM ** (-0.5)

    def block(device):
        start = (device * rows).astype(jnp.int32)
        query_block = lax.dynamic_slice_in_dim(heads, start, rows, 0)
        key_block = lax.dynamic_slice_in_dim(pad_keys, start, span_len, 0)
        value_block = lax.dynamic_slice_in_dim(pad_values, start, span_len, 0)
        query_ids = lax.dynamic_slice_in_dim(image_ids, start, rows, 0)
        key_ids = lax.dynamic_slice_in_dim(pad_ids, start, span_len, 0)
        key_device = (start - IMG + jnp.arange(span_len, dtype=jnp.int32)) // rows
        bounds = lax.dynamic_index_in_dim(spans, device, 0, keepdims=False)
        mask = (query_ids[:, None] == key_ids[None, :]) & (key_device >= bounds[0])[None, :] & (key_device <= bounds[1])[None, :]
        scores = low_back(jnp.einsum('thd,khd->htk', query_block, key_block, precision=HIGH) * scale)
        scores = jnp.where(mask[None], scores, MASKED)
        weights = low(jax.nn.softmax(scores, axis=-1))
        return jnp.einsum('htk,khd->thd', weights, value_block, precision=HIGH)
    mixed = lax.map(jax.checkpoint(block), jnp.arange(count, dtype=jnp.int32))
    return mixed.reshape(TOKENS, HEADS * HEAD_DIM)

def make_layer(image_ids, spans):

    def layer(params, values):
        first_gain, first_shift, triple_weight, triple_bias, output_weight, output_bias, first_scale, second_gain, second_shift, up_weight, up_bias, down_weight, down_bias, second_scale = unpack(low(params), D, FF)
        normed_one = low(layer_norm(values, first_gain, first_shift))
        bias_full = jnp.concatenate([triple_bias[:D], jnp.zeros((D,), jnp.float32), triple_bias[D:]])
        triple = low(low_back(jnp.dot(normed_one, triple_weight, precision=HIGH) + bias_full))
        attended = attention(triple[:, :D], triple[:, D:2 * D], triple[:, 2 * D:], image_ids, spans)
        attended = low(low_back(attended))
        branch_one = low_back(jnp.dot(attended, output_weight, precision=HIGH) + output_bias)
        middle = values + first_scale * branch_one
        normed_two = low(layer_norm(middle, second_gain, second_shift))
        pre_act = low_back(jnp.dot(normed_two, up_weight, precision=HIGH) + up_bias)
        activated = low(jax.nn.gelu(pre_act, approximate=False))
        branch_two = low_back(jnp.dot(activated, down_weight, precision=HIGH) + down_bias)
        return middle + second_scale * branch_two
    return layer

def reference(inputs, cotangent, master, first_moment, second_moment, image_ids, spans):
    values = inputs.astype(jnp.float32)
    upstream = cotangent.astype(jnp.float32)
    layer = make_layer(image_ids, spans)
    result, pull = jax.vjp(layer, master, values)
    weight_grad, input_grad = pull(upstream)
    grad_norm = jnp.sqrt(jnp.sum(weight_grad * weight_grad))
    ceiling = CLIP_RATIO * math.sqrt(P_SIZE)
    factor = ceiling / jnp.maximum(grad_norm, ceiling)
    clipped = weight_grad * factor
    new_first = BETA_ONE * first_moment + (1.0 - BETA_ONE) * clipped
    new_second = BETA_TWO * second_moment + (1.0 - BETA_TWO) * clipped * clipped
    new_master = master - LEARN_RATE * (new_first / (jnp.sqrt(new_second) + ADAM_EPS) + WEIGHT_DECAY * master)
    return (result.astype(jnp.bfloat16), input_grad, weight_grad, grad_norm.reshape(1), new_first, new_second, new_master)
```

```python
import math

import jax
import jax.numpy as jnp
from jax import lax
from jax.experimental import pallas as pl
from jax.experimental.pallas import tpu as pltpu
from jax.sharding import PartitionSpec as P

D = 384
HEADS = 6
HEAD_DIM = 64
FF = 1536
IMG = 1370
LANES = 128

LN_EPS = 1e-06
BETA_ONE = 0.5
BETA_TWO = 0.6
LEARN_RATE = 0.01
WEIGHT_DECAY = 0.05
ADAM_EPS = 1e-08
CLIP_RATIO = 0.25
MASKED = -1e30
BOTH = ("dp", "fsdp")
LOW = jnp.bfloat16
WIDE = jnp.float32
SCALE = HEAD_DIM ** (-0.5)

NT = (((1,), (1,)), ((), ()))
NN = (((1,), (0,)), ((), ()))
TN = (((0,), (0,)), ((), ()))

PIECES = [
    ("gain1", D),
    ("shift1", D),
    ("triple", 3 * D * D),
    ("tbias", 2 * D),
    ("out", D * D),
    ("obias", D),
    ("scale1", D),
    ("gain2", D),
    ("shift2", D),
    ("up", D * FF),
    ("ubias", FF),
    ("down", FF * D),
    ("dbias", D),
    ("scale2", D),
]
AT = {}
_row = 0
for _name, _count in PIECES:
    AT[_name] = _row
    _row += _count // LANES
ALL_ROWS = _row


def dot(a, b, dims):
    return lax.dot_general(a, b, dims, preferred_element_type=WIDE)


class Plan:
    def __init__(self, dp, fsdp, share, tokens):
        self.count = dp * fsdp
        self.share = share
        self.rows = -(-(2 * (LANES - 1) + share) // LANES)
        self.rows = -(-self.rows // 16) * 16
        self.start = [e * share // LANES for e in range(self.count)]
        self.tokens = tokens
        self.reach = (IMG - 2 + tokens) // tokens
        self.window = 2 * self.reach + 1
        self.grouped = dp == 4 and fsdp == 8 and self.reach <= 6
        if self.grouped:
            self.stages = [[2, 4, 6], [16, 1, 17], [8]]
        else:
            bits = [1 << k for k in range(self.count.bit_length() - 1)]
            bits = [b for b in bits if b != fsdp] + [fsdp]
            self.stages = [[b] for b in bits]
        masks = [0]
        for stage in self.stages:
            masks = masks + [m ^ s for s in stage for m in masks]
        self.bits = [masks[1 << k] for k in range(self.count.bit_length() - 1)]
        self.first_late = next(e for e in range(self.count) if self.start[e] >= AT["out"])
        self.flat_rows = -(-(self.start[-1] + self.rows) // 8) * 8

    def send(self, x, mask):
        return lax.ppermute(x, BOTH, [(i, i ^ mask) for i in range(self.count)])

    def spread(self, own):
        buf = own[None]
        for stage in self.stages[:-1]:
            buf = jnp.concatenate([buf] + [self.send(buf, m) for m in stage], axis=0)
        return buf, self.send(buf, self.stages[-1][0])

    def reduce_parts(self, blocks):
        buf = blocks
        for stage in reversed(self.stages):
            split = buf.reshape((len(stage) + 1, -1) + buf.shape[1:])
            parts = [split[0]] + [self.send(split[k + 1], m) for k, m in enumerate(stage)]
            if stage is self.stages[0]:
                return [part[0] for part in parts]
            total = parts[0].astype(WIDE)
            for part in parts[1:]:
                total = total + part.astype(WIDE)
            buf = total.astype(LOW)

    def total(self, value):
        for stage in self.stages:
            got = [value] + [self.send(value, m) for m in stage]
            while len(got) > 1:
                got = [got[k] + got[k + 1] for k in range(0, len(got), 2)]
            value = got[0]
        return value

    def exchange(self, block):
        own = block[None]
        if self.grouped:
            column = jnp.concatenate([own] + [self.send(own, m) for m in (2, 4, 6)], axis=0)
            beside = self.send(column, 1)
            across = [(8 + j, 16 + j) for j in range(8)] + [(16 + j, 8 + j) for j in range(8)]
            far_column = lax.ppermute(column, BOTH, across)
            far_beside = lax.ppermute(beside, BOTH, across)
            row = jnp.concatenate([column, beside], axis=0)
            return [row, self.send(row, 8), far_column, far_beside]
        slots = []
        for slot in range(self.window):
            by = self.reach - slot
            pairs = [(i, i + by) for i in range(self.count) if 0 <= i + by < self.count]
            slots.append(own if by == 0 else lax.ppermute(own, BOTH, pairs))
        return [jnp.concatenate(slots, axis=0)]

    def table(self, device, spans):
        e = jnp.arange(self.count, dtype=jnp.int32)
        rel = e ^ device
        where = jnp.zeros_like(e)
        for k, bit in enumerate(self.bits):
            where = where + jnp.where((rel & bit) != 0, 1 << k, 0)
        slot = jnp.arange(self.window, dtype=jnp.int32)
        if self.grouped:
            other = device - self.reach + slot
            pos = ((other ^ device) & 7) >> 1
            pos = pos + 4 * ((other ^ device) & 1)
            cross = (other >> 3) ^ (device >> 3)
            source = jnp.where(cross == 0, 0, jnp.where(cross == 1, 1, 2 + (pos >> 2)))
            index = jnp.where(source >= 2, pos & 3, pos)
        else:
            source = jnp.zeros_like(slot)
            index = slot
        bounds = lax.dynamic_index_in_dim(spans, device, 0, keepdims=False)
        ends = jnp.clip(bounds - device + self.reach, 0, self.window - 1)
        shift = ((device * self.share) % LANES).reshape(1)
        return jnp.concatenate([where, source, index, ends, shift]).astype(jnp.int32)

    def source_at(self, slot):
        return self.count + slot

    def index_at(self, slot):
        return self.count + self.window + slot

    def low_at(self):
        return self.count + 2 * self.window

    def shift_at(self):
        return self.count + 2 * self.window + 2


def fetch_window(plan, table, sources, dest, sems, lo, hi, wait):
    def step(slot, carry):
        for k, source in enumerate(sources):

            @pl.when(table[plan.source_at(slot)] == k)
            def _(source=source):
                copy = pltpu.make_async_copy(
                    source.at[table[plan.index_at(slot)]], dest.at[slot], sems.at[slot]
                )
                if wait:
                    copy.wait()
                else:
                    copy.start()

        return carry

    lax.fori_loop(lo, hi + 1, step, 0)


def normalized(x):
    center = x - jnp.mean(x, axis=-1, keepdims=True)
    spread = jnp.mean(center * center, axis=-1, keepdims=True)
    r = lax.rsqrt(spread + LN_EPS)
    return center * r, r


def norm_back(grad, gain, n, r):
    g = grad * gain
    inner = jnp.mean(g, axis=-1, keepdims=True)
    outer = jnp.mean(g * n, axis=-1, keepdims=True)
    return r * (g - inner - n * outer)


def vector(ref, row, width):
    return jnp.concatenate([ref[row + j : row + j + 1, :] for j in range(width // LANES)], axis=1)


def put_vector(ref, row, value):
    for j in range(value.shape[1] // LANES):
        ref[row + j : row + j + 1, :] = value[:, LANES * j : LANES * (j + 1)]


def column_sum(x):
    return jnp.sum(x, axis=0, keepdims=True)


def shift_kernel(plan):
    def kernel(table, x_ref, out_ref, pad):
        s = table[plan.shift_at()]
        x = x_ref[...]
        y = pltpu.roll(x, s, 1)
        pad[0:8, :] = jnp.zeros((8, LANES), WIDE)
        pad[8:, :] = y
        lane = lax.broadcasted_iota(jnp.int32, y.shape, 1)
        out_ref[...] = jnp.where(lane >= s, y, pad[7 : 7 + plan.rows, :]).astype(LOW)

    return kernel


def unshift_kernel(plan):
    def kernel(table, *refs):
        parts, (out_ref, sq_ref, pad) = refs[:-3], refs[-3:]
        s = table[plan.shift_at()]
        got = [p[...].astype(WIDE) for p in parts]
        while len(got) > 1:
            got = [got[k] + got[k + 1] for k in range(0, len(got), 2)]
        y = pltpu.roll(got[0], LANES - s, 1)
        pad[0 : plan.rows, :] = y
        pad[plan.rows :, :] = jnp.zeros((8, LANES), WIDE)
        lane = lax.broadcasted_iota(jnp.int32, y.shape, 1)
        row = lax.broadcasted_iota(jnp.int32, y.shape, 0)
        out = jnp.where(lane < LANES - s, y, pad[1 : 1 + plan.rows, :])
        out = jnp.where(row * LANES + lane < plan.share, out, 0.0)
        out_ref[...] = out
        sq = jnp.sum(jnp.sum(out * out, axis=0, keepdims=True), axis=1, keepdims=True)
        sq_ref[...] = jnp.broadcast_to(sq, (8, LANES))

    return kernel


def forward_kernel(plan, sources):
    T = plan.tokens
    W = plan.window
    own = plan.reach
    half = plan.count // 2

    def kernel(table, *refs):
        near, core = refs[:2]
        wins = refs[2 : 2 + sources]
        cot_ref, col_ref, row_ref = refs[2 + sources : 5 + sources]
        (
            out_ref,
            msg_ref,
            q_ref,
            k_ref,
            v_ref,
            triple_ref,
            normed_ref,
            mid_ref,
            act_ref,
            pre_ref,
            gbt_ref,
            n2_ref,
            att_ref,
            gbo_ref,
            vec_ref,
            stat_ref,
            gain_ref,
            kown_ref,
            vown_ref,
        ) = refs[5 + sources : 24 + sources]
        wbuf, flat, xwin, wo, wup, wdn, scores, wsem, xsem = refs[24 + sources :]
        lo = table[plan.low_at()]
        hi = table[plan.low_at() + 1]

        def weight_copy(e, wait):
            t = table[e]

            @pl.when(t < half)
            def _():
                c = pltpu.make_async_copy(near.at[t], wbuf.at[e], wsem.at[e])
                c.wait() if wait else c.start()

            @pl.when(t >= half)
            def _():
                c = pltpu.make_async_copy(core.at[t - half], wbuf.at[e], wsem.at[e])
                c.wait() if wait else c.start()

        def start_one(e, carry):
            weight_copy(e, False)
            return carry

        lax.fori_loop(0, plan.count, start_one, 0)
        fetch_window(plan, table, wins, xwin, xsem, lo, hi, False)

        def wait_one(e, carry):
            weight_copy(e, True)
            return carry

        lax.fori_loop(0, plan.count, wait_one, 0)
        for e in range(plan.count):
            r0 = plan.start[e]
            block = wbuf[e].astype(WIDE)
            if e:
                before = flat[r0 : r0 + 1, :]
                flat[r0 : r0 + plan.rows, :] = block
                flat[r0 : r0 + 1, :] = before + block[0:1, :]
            else:
                flat[r0 : r0 + plan.rows, :] = block

        def unfold(dest, name, height, width):
            wide = width // LANES
            step = min(height, 384)
            for j in range(wide):
                for i in range(0, height, step):
                    dest[i : i + step, LANES * j : LANES * (j + 1)] = flat[
                        pl.ds(AT[name] + i * wide + j, step, stride=wide), :
                    ].astype(LOW)

        unfold(triple_ref, "triple", D, 3 * D)
        gain1 = vector(flat, AT["gain1"], D)
        shift1 = vector(flat, AT["shift1"], D)
        gain_ref[...] = jnp.broadcast_to(gain1, (8, D))
        tbias = vector(flat, AT["tbias"], 2 * D)
        fetch_window(plan, table, wins, xwin, xsem, lo, hi, True)

        def project(w, carry):
            n, _ = normalized(xwin[w].astype(WIDE))
            low = (n * gain1 + shift1).astype(LOW)

            @pl.when(w == own)
            def _():
                normed_ref[...] = low

            q = dot(low, triple_ref[:, :D], NN) + tbias[:, :D]
            q_ref[w] = (q.astype(LOW).astype(WIDE) * SCALE).astype(LOW)
            k_ref[w] = dot(low, triple_ref[:, D : 2 * D], NN).astype(LOW)
            v_ref[w] = (dot(low, triple_ref[:, 2 * D :], NN) + tbias[:, D:]).astype(LOW)
            return carry

        lax.fori_loop(lo, hi + 1, project, 0)
        kown_ref[...] = k_ref[own]
        vown_ref[...] = v_ref[own]

        unfold(wo, "out", D, D)
        unfold(wup, "up", D, FF)
        unfold(wdn, "down", FF, D)

        lane = lax.broadcasted_iota(jnp.int32, (T, LANES), 1)
        left = lane < HEAD_DIM
        ids = jnp.concatenate([col_ref[...]] * (T // LANES), axis=1)
        mixed = []
        stats = jnp.zeros((T, LANES), WIDE)
        for p in range(HEADS // 2):
            cols = slice(LANES * p, LANES * (p + 1))
            q = q_ref[own, :, cols]
            qs = [jnp.where(left, q, 0), jnp.where(left, 0, q)]

            def first(w, tops, qs=qs, cols=cols):
                key = k_ref[w, :, cols]
                seen = ids == row_ref[pl.ds(w, 1), :]
                new = []
                for i in range(2):
                    s = jnp.where(seen, dot(qs[i], key, NT), MASKED)
                    scores[i, w] = s
                    top = tops[i]
                    for c in range(0, T, LANES):
                        top = jnp.maximum(top, s[:, c : c + LANES])
                    new.append(top)
                return tuple(new)

            start = jnp.full((T, LANES), MASKED, WIDE)
            tops = lax.fori_loop(lo, hi + 1, first, (start, start))
            tops = [jnp.max(t, axis=1, keepdims=True) for t in tops]

            def second(w, carry, tops=tops, cols=cols):
                value = v_ref[w, :, cols]
                new = []
                for i in range(2):
                    total, acc = carry[2 * i], carry[2 * i + 1]
                    e = jnp.exp(scores[i, w] - tops[i])
                    for c in range(0, T, LANES):
                        total = total + e[:, c : c + LANES]
                    new += [total, acc + dot(e.astype(LOW), value, NN)]
                return tuple(new)

            zero = jnp.zeros((T, LANES), WIDE)
            got = lax.fori_loop(lo, hi + 1, second, (zero,) * 4)
            sums = [jnp.sum(got[2 * i], axis=1, keepdims=True) for i in range(2)]
            mixed.append(jnp.where(left, got[1] / sums[0], got[3] / sums[1]))
            for i in range(2):
                stats = jnp.where(lane == 2 * p + i, tops[i] + jnp.log(sums[i]), stats)
        att = jnp.concatenate(mixed, axis=1)
        att_low = att.astype(LOW)
        att_ref[...] = att_low
        x = xwin[own].astype(WIDE)
        scale1 = vector(flat, AT["scale1"], D)
        scale2 = vector(flat, AT["scale2"], D)
        gain2 = vector(flat, AT["gain2"], D)
        branch_one = dot(att_low, wo[...], NN) + vector(flat, AT["obias"], D)
        middle = x + scale1 * branch_one
        n2, r2 = normalized(middle)
        n2_low = (n2 * gain2 + vector(flat, AT["shift2"], D)).astype(LOW)
        n2_ref[...] = n2_low
        pre = dot(n2_low, wup[...], NN) + vector(flat, AT["ubias"], FF)
        cdf = 0.5 * (1.0 + lax.erf(pre * math.sqrt(0.5)))
        act_low = (pre * cdf).astype(LOW)
        act_ref[...] = act_low
        slope = cdf + pre * (jnp.exp(-0.5 * pre * pre) * (1.0 / math.sqrt(2.0 * math.pi)))
        branch_two = dot(act_low, wdn[...], NN) + vector(flat, AT["dbias"], D)
        out_ref[...] = (middle + scale2 * branch_two).astype(LOW)

        up = cot_ref[...].astype(WIDE)
        gbt = (scale2 * up).astype(LOW)
        gbt_ref[...] = gbt
        gpre = (dot(gbt, wdn[...], NT) * slope).astype(LOW)
        pre_ref[...] = gpre
        gn2 = dot(gpre, wup[...], NT)
        gmid = up + norm_back(gn2, gain2, n2, r2)
        mid_ref[...] = gmid
        gbo = (scale1 * gmid).astype(LOW)
        gbo_ref[...] = gbo
        gatt = dot(gbo, wo[...], NT).astype(LOW)
        msg_ref[0:T, :] = gatt
        inner = gatt.astype(WIDE) * att
        for p in range(HEADS // 2):
            part = inner[:, LANES * p : LANES * (p + 1)]
            one = jnp.sum(jnp.where(left, part, 0.0), axis=1, keepdims=True)
            two = jnp.sum(jnp.where(left, 0.0, part), axis=1, keepdims=True)
            stats = jnp.where(lane == HEADS + 2 * p, one, stats)
            stats = jnp.where(lane == HEADS + 2 * p + 1, two, stats)
        stat_ref[...] = stats
        flipped = jnp.transpose(stats)[0:16, :]
        hi16 = flipped.astype(LOW)
        rest = flipped - hi16.astype(WIDE)
        mid16 = rest.astype(LOW)
        low16 = (rest - mid16.astype(WIDE)).astype(LOW)
        packed = jnp.concatenate([hi16, mid16[:, : D - T]], axis=1)
        msg_ref[T : T + 16, :] = packed
        packed = jnp.concatenate([mid16[:, D - T :], low16], axis=1)
        msg_ref[T + 16 : T + 32, :] = packed

        vec_ref[...] = jnp.zeros(vec_ref.shape, WIDE)
        vec_ref[0:1, :D] = column_sum(up * branch_two)
        vec_ref[1:2, :D] = column_sum(gbt.astype(WIDE))
        vec_ref[2:3, :] = column_sum(gpre.astype(WIDE))
        vec_ref[3:4, :D] = column_sum(gn2 * n2)
        vec_ref[4:5, :D] = column_sum(gn2)
        vec_ref[5:6, :D] = column_sum(gmid * branch_one)
        vec_ref[6:7, :D] = column_sum(gbo.astype(WIDE))

    return kernel


def fold(dest, row, left, right, width):
    wide = width // LANES
    height = left.shape[1]
    for i in range(0, height, 384):
        part = dot(left[:, i : i + 384], right[...], TN)
        for j in range(wide):
            dest[pl.ds(row + i * wide + j, 384, stride=wide), :] = part[
                :, LANES * j : LANES * (j + 1)
            ]


def middle_kernel(plan):
    T = plan.tokens
    own = plan.reach
    base = AT["out"]

    def kernel(
        table,
        q_ref,
        k_ref,
        v_ref,
        msg_ref,
        stat_ref,
        col_ref,
        row_ref,
        act_ref,
        pre_ref,
        gbt_ref,
        n2_ref,
        att_ref,
        gbo_ref,
        vec_ref,
        gq_ref,
        blocks_ref,
        tail_ref,
        flat,
    ):
        lo = table[plan.low_at()]
        hi = table[plan.low_at() + 1]
        fold(flat, AT["down"] - base, act_ref, gbt_ref, D)
        fold(flat, AT["up"] - base, n2_ref, pre_ref, FF)
        fold(flat, AT["out"] - base, att_ref, gbo_ref, D)
        put_vector(flat, AT["scale2"] - base, vec_ref[0:1, :D])
        put_vector(flat, AT["dbias"] - base, vec_ref[1:2, :D])
        put_vector(flat, AT["ubias"] - base, vec_ref[2:3, :])
        put_vector(flat, AT["gain2"] - base, vec_ref[3:4, :D])
        put_vector(flat, AT["shift2"] - base, vec_ref[4:5, :D])
        put_vector(flat, AT["scale1"] - base, vec_ref[5:6, :D])
        put_vector(flat, AT["obias"] - base, vec_ref[6:7, :D])
        end = ALL_ROWS - base
        flat[end:, :] = jnp.zeros((flat.shape[0] - end, LANES), WIDE)
        tail_ref[...] = flat[0 : plan.rows, :]
        for e in range(plan.first_late, plan.count):
            r0 = plan.start[e] - base
            blocks_ref[table[e]] = flat[r0 : r0 + plan.rows, :].astype(LOW)

        lane = lax.broadcasted_iota(jnp.int32, (T, LANES), 1)
        left = lane < HEAD_DIM
        ids = jnp.concatenate([col_ref[...]] * (T // LANES), axis=1)
        for p in range(HEADS // 2):
            cols = slice(LANES * p, LANES * (p + 1))
            q = q_ref[own, :, cols]
            g = msg_ref[0:T, cols]
            qs = [jnp.where(left, q, 0), jnp.where(left, 0, q)]
            gs = [jnp.where(left, g, 0), jnp.where(left, 0, g)]
            logs = [stat_ref[:, 2 * p + i : 2 * p + i + 1] for i in range(2)]
            inner = [stat_ref[:, HEADS + 2 * p + i : HEADS + 2 * p + i + 1] for i in range(2)]

            def step(w, carry, qs=qs, gs=gs, logs=logs, inner=inner, cols=cols):
                key = k_ref[w, :, cols]
                value = v_ref[w, :, cols]
                seen = ids == row_ref[pl.ds(w, 1), :]
                new = []
                for i in range(2):
                    s = jnp.where(seen, dot(qs[i], key, NT), MASKED)
                    prob = jnp.exp(s - logs[i])
                    gs_i = prob * (dot(gs[i], value, NT) - inner[i])
                    new.append(carry[i] + dot(gs_i.astype(LOW), key, NN))
                return tuple(new)

            zero = jnp.zeros((T, LANES), WIDE)
            got = lax.fori_loop(lo, hi + 1, step, (zero, zero))
            gq_ref[:, cols] = (jnp.where(left, got[0], got[1]) * SCALE).astype(LOW)

    return kernel


def last_kernel(plan, sources):
    T = plan.tokens
    own = plan.reach
    early = plan.first_late

    def kernel(table, *refs):
        wins = refs[:sources]
        (
            q_ref,
            k_ref,
            v_ref,
            col_ref,
            row_ref,
            gq_ref,
            normed_ref,
            triple_ref,
            x_ref,
            mid_ref,
            gain_ref,
            tail_ref,
            _,
            grad_ref,
            blocks_ref,
        ) = refs[sources : sources + 15]
        mwin, flat, gt, stage, msem, osem = refs[sources + 15 :]
        lo = table[plan.low_at()]
        hi = table[plan.low_at() + 1]
        fetch_window(plan, table, wins, mwin, msem, lo, hi, False)
        fetch_window(plan, table, wins, mwin, msem, lo, hi, True)
        lane = lax.broadcasted_iota(jnp.int32, (T, LANES), 1)
        left = lane < HEAD_DIM
        ids = jnp.concatenate([col_ref[...]] * (T // LANES), axis=1)
        for p in range(HEADS // 2):
            cols = slice(LANES * p, LANES * (p + 1))
            k = k_ref[:, cols]
            v = v_ref[:, cols]
            ks = [jnp.where(left, k, 0), jnp.where(left, 0, k)]
            vs = [jnp.where(left, v, 0), jnp.where(left, 0, v)]

            def step(w, carry, ks=ks, vs=vs, cols=cols, p=p):
                q = q_ref[w, :, cols]
                g = mwin[w, 0:T, cols]
                one = mwin[w, T : T + 16, :].astype(WIDE)
                two = mwin[w, T + 16 : T + 32, :].astype(WIDE)
                stats = one[:, :T] + jnp.concatenate(
                    [one[:, T:], two[:, : 2 * T - D]], axis=1
                )
                stats = stats + two[:, 2 * T - D :]
                seen = ids == row_ref[pl.ds(w, 1), :]
                new = []
                for i in range(2):
                    h = 2 * p + i
                    s = jnp.where(seen, dot(ks[i], q, NT), MASKED)
                    prob = jnp.exp(s - stats[h : h + 1, :])
                    gs_i = prob * (dot(vs[i], g, NT) - stats[HEADS + h : HEADS + h + 1, :])
                    new.append(carry[2 * i] + dot(gs_i.astype(LOW), q, NN))
                    new.append(carry[2 * i + 1] + dot(prob.astype(LOW), g, NN))
                return tuple(new)

            zero = jnp.zeros((T, LANES), WIDE)
            got = lax.fori_loop(lo, hi + 1, step, (zero,) * 4)
            gt[:, D + LANES * p : D + LANES * (p + 1)] = jnp.where(left, got[0], got[2]).astype(LOW)
            gt[:, 2 * D + LANES * p : 2 * D + LANES * (p + 1)] = jnp.where(
                left, got[1], got[3]
            ).astype(LOW)
        gt[:, :D] = gq_ref[...]
        fold(flat, AT["triple"], normed_ref, gt, 3 * D)
        put_vector(flat, AT["tbias"], column_sum(gt[:, :D].astype(WIDE)))
        put_vector(flat, AT["tbias"] + D // LANES, column_sum(gt[:, 2 * D :].astype(WIDE)))
        gn = dot(gt[...], triple_ref[...], NT)
        n, r = normalized(x_ref[...].astype(WIDE))
        put_vector(flat, AT["gain1"], column_sum(gn * n))
        put_vector(flat, AT["shift1"], column_sum(gn))
        flat[AT["out"] : AT["out"] + plan.rows, :] = tail_ref[...]
        for e in range(early):
            r0 = plan.start[e]
            stage[e] = flat[r0 : r0 + plan.rows, :].astype(LOW)
            pltpu.make_async_copy(stage.at[e], blocks_ref.at[table[e]], osem.at[e]).start()
        grad_ref[...] = mid_ref[...] + norm_back(gn, gain_ref[0:1, :], n, r)
        for e in range(early):
            pltpu.make_async_copy(stage.at[e], blocks_ref.at[table[e]], osem.at[e]).wait()

    return kernel


def shape(dims, kind):
    return jax.ShapeDtypeStruct(dims, kind)


SMEM = pl.BlockSpec(memory_space=pltpu.SMEM)
VMEM = pl.BlockSpec(memory_space=pltpu.VMEM)
ANY = pl.BlockSpec(memory_space=pl.ANY)


def build(plan):
    T = plan.tokens
    W = plan.window
    R = plan.rows
    N = plan.count
    limit = pltpu.CompilerParams(vmem_limit_bytes=60 * 1024 * 1024)

    def per_device(inputs, cotangent, master, first_moment, second_moment, image_ids, spans):
        device = lax.axis_index(BOTH).astype(jnp.int32)
        table = plan.table(device, spans)
        padded = jnp.pad(image_ids, (plan.reach * T, plan.reach * T), constant_values=-1)
        key_ids = lax.dynamic_slice_in_dim(padded, device * T, W * T, 0).reshape(W, T)
        own_ids = key_ids[plan.reach]
        columns = jnp.broadcast_to(own_ids[:, None], (T, LANES))

        shifted = pl.pallas_call(
            shift_kernel(plan),
            in_specs=[SMEM, VMEM],
            out_specs=VMEM,
            out_shape=shape((R, LANES), LOW),
            scratch_shapes=[pltpu.VMEM((R + 8, LANES), WIDE)],
            name="shift",
        )(table, jnp.pad(master, (0, R * LANES - plan.share)).reshape(R, LANES))
        near, core = plan.spread(shifted)
        wins = plan.exchange(inputs)
        sources = len(wins)

        outs = pl.pallas_call(
            forward_kernel(plan, sources),
            in_specs=[SMEM, ANY, ANY] + [ANY] * sources + [VMEM] * 3,
            out_specs=[VMEM] * 19,
            out_shape=[
                shape((T, D), LOW),
                shape((T + 32, D), LOW),
                shape((W, T, D), LOW),
                shape((W, T, D), LOW),
                shape((W, T, D), LOW),
                shape((D, 3 * D), LOW),
                shape((T, D), LOW),
                shape((T, D), WIDE),
                shape((T, FF), LOW),
                shape((T, FF), LOW),
                shape((T, D), LOW),
                shape((T, D), LOW),
                shape((T, D), LOW),
                shape((T, D), LOW),
                shape((8, FF), WIDE),
                shape((T, LANES), WIDE),
                shape((8, D), WIDE),
                shape((T, D), LOW),
                shape((T, D), LOW),
            ],
            scratch_shapes=[
                pltpu.VMEM((N, R, LANES), LOW),
                pltpu.VMEM((plan.flat_rows, LANES), WIDE),
                pltpu.VMEM((W, T, D), LOW),
                pltpu.VMEM((D, D), LOW),
                pltpu.VMEM((D, FF), LOW),
                pltpu.VMEM((FF, D), LOW),
                pltpu.VMEM((2, W, T, T), WIDE),
                pltpu.SemaphoreType.DMA((N,)),
                pltpu.SemaphoreType.DMA((W,)),
            ],
            compiler_params=limit,
            name="forward",
        )(table, near, core, *wins, cotangent, columns, key_ids)
        (
            result,
            message,
            q,
            k,
            v,
            triple,
            normed,
            gmid,
            act,
            gpre,
            gbt,
            n2,
            att,
            gbo,
            vec,
            stat,
            gain,
            k_own,
            v_own,
        ) = outs
        messages = plan.exchange(message)

        gq, blocks, tail = pl.pallas_call(
            middle_kernel(plan),
            in_specs=[SMEM] + [VMEM] * 14,
            out_specs=[VMEM] * 3,
            out_shape=[
                shape((T, D), LOW),
                shape((N, R, LANES), LOW),
                shape((R, LANES), WIDE),
            ],
            scratch_shapes=[
                pltpu.VMEM((plan.flat_rows - AT["out"] + 8, LANES), WIDE),
            ],
            compiler_params=limit,
            name="middle",
        )(table, q, k, v, message, stat, columns, key_ids, act, gpre, gbt, n2, att, gbo, vec)

        late = plan.first_late
        input_grad, blocks = pl.pallas_call(
            last_kernel(plan, sources),
            in_specs=[SMEM]
            + [ANY] * sources
            + [VMEM] * 12
            + [ANY],
            out_specs=[VMEM, ANY],
            out_shape=[shape((T, D), WIDE), shape((N, R, LANES), LOW)],
            scratch_shapes=[
                pltpu.VMEM((W, T + 32, D), LOW),
                pltpu.VMEM((AT["out"] + R + 8, LANES), WIDE),
                pltpu.VMEM((T, 3 * D), LOW),
                pltpu.VMEM((late, R, LANES), LOW),
                pltpu.SemaphoreType.DMA((W,)),
                pltpu.SemaphoreType.DMA((late,)),
            ],
            input_output_aliases={13 + sources: 1},
            compiler_params=limit,
            name="last",
        )(
            table,
            *messages,
            q,
            k_own,
            v_own,
            columns,
            key_ids,
            gq,
            normed,
            triple,
            inputs,
            gmid,
            gain,
            tail,
            blocks,
        )

        parts = plan.reduce_parts(blocks)
        grad, square = pl.pallas_call(
            unshift_kernel(plan),
            in_specs=[SMEM] + [VMEM] * len(parts),
            out_specs=[VMEM, VMEM],
            out_shape=[shape((R, LANES), WIDE), shape((8, LANES), WIDE)],
            scratch_shapes=[pltpu.VMEM((R + 8, LANES), WIDE)],
            name="unshift",
        )(table, *parts)
        grad_shard = grad.reshape(-1)[: plan.share]
        grad_norm = jnp.sqrt(plan.total(square)[0, 0])
        ceiling = CLIP_RATIO * math.sqrt(plan.share * N)
        factor = ceiling / jnp.maximum(grad_norm, ceiling)
        clipped = grad_shard * factor
        new_first = BETA_ONE * first_moment + (1.0 - BETA_ONE) * clipped
        new_second = BETA_TWO * second_moment + (1.0 - BETA_TWO) * clipped * clipped
        new_master = master - LEARN_RATE * (
            new_first / (jnp.sqrt(new_second) + ADAM_EPS) + WEIGHT_DECAY * master
        )
        return (
            result,
            input_grad,
            grad_shard,
            grad_norm.reshape(1),
            new_first,
            new_second,
            new_master,
        )

    return per_device


def solution(mesh):
    dp = mesh.shape["dp"]
    fsdp = mesh.shape["fsdp"]
    row = P(BOTH, None)
    flat = P(BOTH)
    in_specs = (row, row, flat, flat, flat, P(), P())
    out_specs = (row, row, flat, P(), flat, flat, flat)

    def per_device(*args):
        inputs, master = args[0], args[2]
        plan = Plan(dp, fsdp, master.shape[0], inputs.shape[0])
        return build(plan)(*args)

    return jax.shard_map(
        per_device, mesh=mesh, in_specs=in_specs, out_specs=out_specs, check_vma=False
    )
```

```python
import math

import jax
import jax.numpy as jnp
from jax import lax
from jax.experimental import pallas as pl
from jax.experimental.pallas import tpu as pltpu
from jax.sharding import PartitionSpec as P


D = 384
HEADS = 6
HEAD_DIM = 64
FF = 1536
IMG = 1370
LANES = 128

LN_EPS = 1e-06
BETA_ONE = 0.5
BETA_TWO = 0.6
LEARN_RATE = 0.01
WEIGHT_DECAY = 0.05
ADAM_EPS = 1e-08
CLIP_RATIO = 0.25
MASKED = -1e30
BOTH = ("dp", "fsdp")
LOW = jnp.bfloat16
WIDE = jnp.float32
SCALE = HEAD_DIM ** (-0.5)

NT = (((1,), (1,)), ((), ()))
NN = (((1,), (0,)), ((), ()))
TN = (((0,), (0,)), ((), ()))

PIECES = [
    ("gain1", D),
    ("shift1", D),
    ("triple", 3 * D * D),
    ("tbias", 2 * D),
    ("out", D * D),
    ("obias", D),
    ("scale1", D),
    ("gain2", D),
    ("shift2", D),
    ("up", D * FF),
    ("ubias", FF),
    ("down", FF * D),
    ("dbias", D),
    ("scale2", D),
]
AT = {}
_row = 0
for _name, _count in PIECES:
    AT[_name] = _row
    _row += _count // LANES
ALL_ROWS = _row


def dot(a, b, dims):
    return lax.dot_general(a, b, dims, preferred_element_type=WIDE)


class Plan:
    def __init__(self, dp, fsdp, share, tokens):
        self.count = dp * fsdp
        self.share = share
        self.rows = -(-(2 * (LANES - 1) + share) // LANES)
        self.rows = -(-self.rows // 16) * 16
        self.start = [e * share // LANES for e in range(self.count)]
        self.tokens = tokens
        self.part = tokens
        self.reach = (IMG - 2 + tokens) // tokens
        self.window = 2 * self.reach + 1
        self.grouped = dp == 4 and fsdp == 8 and self.reach <= 6
        if self.grouped:
            self.stages = [[2, 4, 6], [16, 1, 17], [8]]
        else:
            bits = [1 << k for k in range(self.count.bit_length() - 1)]
            bits = [b for b in bits if b != fsdp] + [fsdp]
            self.stages = [[b] for b in bits]
        masks = [0]
        for stage in self.stages:
            masks = masks + [m ^ s for s in stage for m in masks]
        self.bits = [masks[1 << k] for k in range(self.count.bit_length() - 1)]
        self.first_late = next(e for e in range(self.count) if self.start[e] >= AT["out"])
        self.flat_rows = -(-(self.start[-1] + self.rows) // 8) * 8

    def send(self, x, mask):
        return lax.ppermute(x, BOTH, [(i, i ^ mask) for i in range(self.count)])

    def spread(self, own):
        buf = own[None]
        for stage in self.stages[:-1]:
            buf = jnp.concatenate([buf] + [self.send(buf, m) for m in stage], axis=0)
        return buf, self.send(buf, self.stages[-1][0])

    def reduce_parts(self, blocks):
        buf = blocks
        for stage in reversed(self.stages):
            split = buf.reshape((len(stage) + 1, -1) + buf.shape[1:])
            parts = [split[0]] + [self.send(split[k + 1], m) for k, m in enumerate(stage)]
            if stage is self.stages[0]:
                return [part[0] for part in parts]
            total = parts[0].astype(WIDE)
            for part in parts[1:]:
                total = total + part.astype(WIDE)
            buf = total.astype(LOW)

    def total(self, value):
        for stage in self.stages:
            got = [value] + [self.send(value, m) for m in stage]
            while len(got) > 1:
                got = [got[k] + got[k + 1] for k in range(0, len(got), 2)]
            value = got[0]
        return value

    def exchange(self, block, extra=()):
        own = block[None]
        if self.grouped:
            hops = []
            for m in (1, 2, 3, 4, 6):
                hops.append(self.send(own, m))
            one, two, three, four, six = hops
            pair = jnp.concatenate([four, six], axis=0)
            quad = jnp.concatenate([two, three, four, six], axis=0)
            pair, quad, extra = lax.optimization_barrier((pair, quad, extra))
            across = [(8 + j, 16 + j) for j in range(8)] + [(16 + j, 8 + j) for j in range(8)]
            skew = [(a, b ^ 1) for a, b in across]
            far = lax.ppermute(quad, BOTH, across)
            far_beside = lax.ppermute(pair, BOTH, skew)
            beside = self.send(pair, 1)
            row = jnp.concatenate([own, one, quad, beside], axis=0)
            return [row, self.send(row, 8), far, far_beside], extra
        slots = []
        for slot in range(self.window):
            by = self.reach - slot
            pairs = [(i, i + by) for i in range(self.count) if 0 <= i + by < self.count]
            slots.append(own if by == 0 else lax.ppermute(own, BOTH, pairs))
        return [jnp.concatenate(slots, axis=0)], extra

    def table(self, device, spans, key_ids):
        e = jnp.arange(self.count, dtype=jnp.int32)
        rel = e ^ device
        where = jnp.zeros_like(e)
        for k, bit in enumerate(self.bits):
            where = where + jnp.where((rel & bit) != 0, 1 << k, 0)
        slot = jnp.arange(self.window, dtype=jnp.int32)
        if self.grouped:
            other = device - self.reach + slot
            mask = (other ^ device) & 7
            pos = jnp.where(mask == 6, 5, jnp.where(mask == 5, 6, mask))
            cross = (other >> 3) ^ (device >> 3)
            late = pos >= 6
            source = jnp.where(cross == 0, 0, jnp.where(cross == 1, 1, jnp.where(late, 3, 2)))
            index = jnp.where(source >= 2, jnp.where(late, pos - 6, pos - 2), pos)
        else:
            source = jnp.zeros_like(slot)
            index = slot
        bounds = lax.dynamic_index_in_dim(spans, device, 0, keepdims=False)
        ends = jnp.clip(bounds - device + self.reach, 0, self.window - 1)
        own = key_ids[self.reach]
        low, high = own[:: self.part], own[self.part - 1 :: self.part]
        seen = (key_ids[:, -1][None] >= low[:, None]) & (key_ids[:, 0][None] <= high[:, None])
        seen = seen & (slot >= ends[0])[None] & (slot <= ends[1])[None]
        begin = jnp.min(jnp.where(seen, slot[None], self.window), axis=1)
        finish = jnp.max(jnp.where(seen, slot[None], -1), axis=1)
        return jnp.concatenate([where, source, index, ends, begin, finish]).astype(jnp.int32)

    def source_at(self, slot):
        return self.count + slot

    def index_at(self, slot):
        return self.count + self.window + slot

    def low_at(self):
        return self.count + 2 * self.window

    def range_at(self, quarter):
        at = self.count + 2 * self.window + 2 + quarter
        return at, at + self.tokens // self.part


def fetch_window(plan, table, sources, dest, sems, lo, hi, wait):
    def step(slot, carry):
        for k, source in enumerate(sources):

            @pl.when(table[plan.source_at(slot)] == k)
            def _(source=source):
                copy = pltpu.make_async_copy(
                    source.at[table[plan.index_at(slot)]], dest.at[slot], sems.at[slot]
                )
                if wait:
                    copy.wait()
                else:
                    copy.start()

        return carry

    lax.fori_loop(lo, hi + 1, step, 0)


def normalized(x):
    center = x - jnp.mean(x, axis=-1, keepdims=True)
    spread = jnp.mean(center * center, axis=-1, keepdims=True)
    r = lax.rsqrt(spread + LN_EPS)
    return center * r, r


def norm_back(grad, gain, n, r):
    g = grad * gain
    inner = jnp.mean(g, axis=-1, keepdims=True)
    outer = jnp.mean(g * n, axis=-1, keepdims=True)
    return r * (g - inner - n * outer)


def vector(ref, row, width):
    return jnp.concatenate([ref[row + j : row + j + 1, :] for j in range(width // LANES)], axis=1)


def put_vector(ref, row, value):
    for j in range(value.shape[1] // LANES):
        ref[row + j : row + j + 1, :] = value[:, LANES * j : LANES * (j + 1)]


def stacked(x):
    left = lax.broadcasted_iota(jnp.int32, x.shape, 1) < HEAD_DIM
    return jnp.concatenate([jnp.where(left, x, 0), jnp.where(left, 0, x)], axis=0)


def unstacked(x):
    half = x.shape[0] // 2
    left = lax.broadcasted_iota(jnp.int32, (half, LANES), 1) < HEAD_DIM
    return jnp.where(left, x[:half], x[half:])


def tiled(ids, width):
    ids = jnp.concatenate([ids] * (width // LANES), axis=1)
    return jnp.concatenate([ids, ids], axis=0)


def column_sum(x):
    return jnp.sum(x, axis=0, keepdims=True)


def shift_kernel(plan):
    def kernel(table, x_ref, out_ref, pad):
        s = table[0]
        x = x_ref[...]
        y = pltpu.roll(x, s, 1)
        pad[0:8, :] = jnp.zeros((8, LANES), WIDE)
        pad[8:, :] = y
        lane = lax.broadcasted_iota(jnp.int32, y.shape, 1)
        out_ref[...] = jnp.where(lane >= s, y, pad[7 : 7 + plan.rows, :]).astype(LOW)

    return kernel


def unshift_kernel(plan):
    def kernel(table, *refs):
        parts, (out_ref, sq_ref, pad) = refs[:-3], refs[-3:]
        s = table[0]
        got = [p[...].astype(WIDE) for p in parts]
        while len(got) > 1:
            got = [got[k] + got[k + 1] for k in range(0, len(got), 2)]
        y = pltpu.roll(got[0], LANES - s, 1)
        pad[0 : plan.rows, :] = y
        pad[plan.rows :, :] = jnp.zeros((8, LANES), WIDE)
        lane = lax.broadcasted_iota(jnp.int32, y.shape, 1)
        row = lax.broadcasted_iota(jnp.int32, y.shape, 0)
        out = jnp.where(lane < LANES - s, y, pad[1 : 1 + plan.rows, :])
        out = jnp.where(row * LANES + lane < plan.share, out, 0.0)
        out_ref[...] = out
        sq = jnp.sum(jnp.sum(out * out, axis=0, keepdims=True), axis=1, keepdims=True)
        sq_ref[...] = jnp.broadcast_to(sq, (8, LANES))

    return kernel


def forward_kernel(plan, sources):
    T = plan.tokens
    own = plan.reach
    half = plan.count // 2
    part = plan.part
    pairs = HEADS // 2

    def kernel(table, *refs):
        near, core = refs[:2]
        wins = refs[2 : 2 + sources]
        cot_ref, col_ref, row_ref = refs[2 + sources : 5 + sources]
        (
            out_ref,
            msg_ref,
            q_ref,
            k_ref,
            v_ref,
            triple_ref,
            normed_ref,
            mid_ref,
            act_ref,
            pre_ref,
            gbt_ref,
            n2_ref,
            att_ref,
            gbo_ref,
            vec_ref,
            stat_ref,
            gain_ref,
            kown_ref,
            vown_ref,
        ) = refs[5 + sources : 24 + sources]
        wbuf, flat, xwin, wo, wup, wdn, scores, tops, sums, accs, mix, wsem, xsem = refs[24 + sources :]
        lo = table[plan.low_at()]
        hi = table[plan.low_at() + 1]

        def weight_copy(e, wait):
            t = table[e]

            @pl.when(t < half)
            def _():
                c = pltpu.make_async_copy(near.at[t], wbuf.at[e], wsem.at[e])
                c.wait() if wait else c.start()

            @pl.when(t >= half)
            def _():
                c = pltpu.make_async_copy(core.at[t - half], wbuf.at[e], wsem.at[e])
                c.wait() if wait else c.start()

        def start_one(e, carry):
            weight_copy(e, False)
            return carry

        lax.fori_loop(0, plan.count, start_one, 0)
        fetch_window(plan, table, wins, xwin, xsem, lo, hi, False)

        def wait_one(e, carry):
            weight_copy(e, True)
            return carry

        lax.fori_loop(0, plan.count, wait_one, 0)
        for e in range(plan.count):
            r0 = plan.start[e]
            block = wbuf[e].astype(WIDE)
            if e:
                before = flat[r0 : r0 + 1, :]
                flat[r0 : r0 + plan.rows, :] = block
                flat[r0 : r0 + 1, :] = before + block[0:1, :]
            else:
                flat[r0 : r0 + plan.rows, :] = block

        def unfold(dest, name, height, width):
            wide = width // LANES
            step = min(height, 384)
            for j in range(wide):
                for i in range(0, height, step):
                    dest[i : i + step, LANES * j : LANES * (j + 1)] = flat[
                        pl.ds(AT[name] + i * wide + j, step, stride=wide), :
                    ].astype(LOW)

        unfold(triple_ref, "triple", D, 3 * D)
        gain1 = vector(flat, AT["gain1"], D)
        shift1 = vector(flat, AT["shift1"], D)
        gain_ref[...] = jnp.broadcast_to(gain1, (8, D))
        tbias = vector(flat, AT["tbias"], 2 * D)
        fetch_window(plan, table, wins, xwin, xsem, lo, hi, True)

        def project(w, carry):
            n, _ = normalized(xwin[w].astype(WIDE))
            low = (n * gain1 + shift1).astype(LOW)

            @pl.when(w == own)
            def _():
                normed_ref[...] = low

            q = dot(low, triple_ref[:, :D], NN) + tbias[:, :D]
            q_ref[w] = (q.astype(LOW).astype(WIDE) * SCALE).astype(LOW)
            k_ref[w] = dot(low, triple_ref[:, D : 2 * D], NN).astype(LOW)
            v_ref[w] = (dot(low, triple_ref[:, 2 * D :], NN) + tbias[:, D:]).astype(LOW)
            return carry

        lax.fori_loop(lo, hi + 1, project, 0)
        kown_ref[...] = k_ref[own]
        vown_ref[...] = v_ref[own]

        unfold(wo, "out", D, D)
        unfold(wup, "up", D, FF)
        unfold(wdn, "down", FF, D)

        lane = lax.broadcasted_iota(jnp.int32, (part, LANES), 1)
        for c in range(T // part):
            rows = slice(part * c, part * (c + 1))
            at, to = plan.range_at(c)
            begin, finish = table[at], table[to] + 1
            qs = [stacked(q_ref[own, rows, LANES * p : LANES * (p + 1)]) for p in range(pairs)]
            ids = tiled(col_ref[rows, :], T)
            for p in range(pairs):
                tops[p] = jnp.full((2 * part, LANES), MASKED, WIDE)
                sums[p] = jnp.zeros((2 * part, LANES), WIDE)
                accs[p] = jnp.zeros((2 * part, LANES), WIDE)

            def first(w, carry, qs=qs, ids=ids):
                seen = ids == row_ref[pl.ds(w, 1), :]
                for p in range(pairs):
                    s = dot(qs[p], k_ref[w, :, LANES * p : LANES * (p + 1)], NT)
                    s = jnp.where(seen, s, MASKED)
                    scores[p, w] = s
                    top = tops[p]
                    for j in range(0, T, LANES):
                        top = jnp.maximum(top, s[:, j : j + LANES])
                    tops[p] = top
                return carry

            lax.fori_loop(begin, finish, first, 0)
            for p in range(pairs):
                top = jnp.max(tops[p], axis=1, keepdims=True)
                tops[p] = jnp.broadcast_to(top, (2 * part, LANES))

            def second(w, carry):
                for p in range(pairs):
                    top = jnp.concatenate([tops[p]] * (T // LANES), axis=1)
                    e = jnp.exp(scores[p, w] - top)
                    total = sums[p]
                    for j in range(0, T, LANES):
                        total = total + e[:, j : j + LANES]
                    sums[p] = total
                    value = v_ref[w, :, LANES * p : LANES * (p + 1)]
                    accs[p] = accs[p] + dot(e.astype(LOW), value, NN)
                return carry

            lax.fori_loop(begin, finish, second, 0)
            stats = jnp.zeros((part, LANES), WIDE)
            for p in range(pairs):
                total = jnp.sum(sums[p], axis=1, keepdims=True)
                mixed = accs[p] / total
                mix[rows, LANES * p : LANES * (p + 1)] = unstacked(mixed)
                log = tops[p] + jnp.log(total)
                stats = jnp.where(lane == 2 * p, log[:part], stats)
                stats = jnp.where(lane == 2 * p + 1, log[part:], stats)
            stat_ref[rows, :] = stats
        att = mix[...]
        att_low = att.astype(LOW)
        att_ref[...] = att_low
        x = xwin[own].astype(WIDE)
        scale1 = vector(flat, AT["scale1"], D)
        scale2 = vector(flat, AT["scale2"], D)
        gain2 = vector(flat, AT["gain2"], D)
        branch_one = dot(att_low, wo[...], NN) + vector(flat, AT["obias"], D)
        middle = x + scale1 * branch_one
        n2, r2 = normalized(middle)
        n2_low = (n2 * gain2 + vector(flat, AT["shift2"], D)).astype(LOW)
        n2_ref[...] = n2_low
        pre = dot(n2_low, wup[...], NN) + vector(flat, AT["ubias"], FF)
        cdf = 0.5 * (1.0 + lax.erf(pre * math.sqrt(0.5)))
        act_low = (pre * cdf).astype(LOW)
        act_ref[...] = act_low
        slope = cdf + pre * (jnp.exp(-0.5 * pre * pre) * (1.0 / math.sqrt(2.0 * math.pi)))
        branch_two = dot(act_low, wdn[...], NN) + vector(flat, AT["dbias"], D)
        out_ref[...] = (middle + scale2 * branch_two).astype(LOW)

        up = cot_ref[...].astype(WIDE)
        gbt = (scale2 * up).astype(LOW)
        gbt_ref[...] = gbt
        gpre = (dot(gbt, wdn[...], NT) * slope).astype(LOW)
        pre_ref[...] = gpre
        gn2 = dot(gpre, wup[...], NT)
        gmid = up + norm_back(gn2, gain2, n2, r2)
        mid_ref[...] = gmid
        gbo = (scale1 * gmid).astype(LOW)
        gbo_ref[...] = gbo
        gatt = dot(gbo, wo[...], NT).astype(LOW)
        msg_ref[0:T, :] = gatt
        inner = gatt.astype(WIDE) * att
        stats = stat_ref[...]
        lane = lax.broadcasted_iota(jnp.int32, (T, LANES), 1)
        left = lane < HEAD_DIM
        for p in range(HEADS // 2):
            piece = inner[:, LANES * p : LANES * (p + 1)]
            one = jnp.sum(jnp.where(left, piece, 0.0), axis=1, keepdims=True)
            two = jnp.sum(jnp.where(left, 0.0, piece), axis=1, keepdims=True)
            stats = jnp.where(lane == HEADS + 2 * p, one, stats)
            stats = jnp.where(lane == HEADS + 2 * p + 1, two, stats)
        stat_ref[...] = stats
        flipped = jnp.transpose(stats)[0:16, :]
        hi16 = flipped.astype(LOW)
        rest = flipped - hi16.astype(WIDE)
        mid16 = rest.astype(LOW)
        low16 = (rest - mid16.astype(WIDE)).astype(LOW)
        packed = jnp.concatenate([hi16, mid16[:, : D - T]], axis=1)
        msg_ref[T : T + 16, :] = packed
        packed = jnp.concatenate([mid16[:, D - T :], low16], axis=1)
        msg_ref[T + 16 : T + 32, :] = packed

        vec_ref[...] = jnp.zeros(vec_ref.shape, WIDE)
        vec_ref[0:1, :D] = column_sum(up * branch_two)
        vec_ref[1:2, :D] = column_sum(gbt.astype(WIDE))
        vec_ref[2:3, :] = column_sum(gpre.astype(WIDE))
        vec_ref[3:4, :D] = column_sum(gn2 * n2)
        vec_ref[4:5, :D] = column_sum(gn2)
        vec_ref[5:6, :D] = column_sum(gmid * branch_one)
        vec_ref[6:7, :D] = column_sum(gbo.astype(WIDE))

    return kernel


def fold(dest, row, left, right, width):
    wide = width // LANES
    height = left.shape[1]
    for i in range(0, height, 384):
        part = dot(left[:, i : i + 384], right[...], TN)
        for j in range(wide):
            dest[pl.ds(row + i * wide + j, 384, stride=wide), :] = part[
                :, LANES * j : LANES * (j + 1)
            ]


def middle_kernel(plan):
    T = plan.tokens
    own = plan.reach
    base = AT["out"]
    part = plan.part
    pairs = HEADS // 2

    def kernel(
        table,
        q_ref,
        k_ref,
        v_ref,
        msg_ref,
        stat_ref,
        col_ref,
        row_ref,
        act_ref,
        pre_ref,
        gbt_ref,
        n2_ref,
        att_ref,
        gbo_ref,
        vec_ref,
        gq_ref,
        blocks_ref,
        tail_ref,
        flat,
        logs,
        dots,
        accs,
    ):
        fold(flat, AT["down"] - base, act_ref, gbt_ref, D)
        fold(flat, AT["up"] - base, n2_ref, pre_ref, FF)
        fold(flat, AT["out"] - base, att_ref, gbo_ref, D)
        put_vector(flat, AT["scale2"] - base, vec_ref[0:1, :D])
        put_vector(flat, AT["dbias"] - base, vec_ref[1:2, :D])
        put_vector(flat, AT["ubias"] - base, vec_ref[2:3, :])
        put_vector(flat, AT["gain2"] - base, vec_ref[3:4, :D])
        put_vector(flat, AT["shift2"] - base, vec_ref[4:5, :D])
        put_vector(flat, AT["scale1"] - base, vec_ref[5:6, :D])
        put_vector(flat, AT["obias"] - base, vec_ref[6:7, :D])
        end = ALL_ROWS - base
        flat[end:, :] = jnp.zeros((flat.shape[0] - end, LANES), WIDE)
        tail_ref[...] = flat[0 : plan.rows, :]
        for e in range(plan.first_late, plan.count):
            r0 = plan.start[e] - base
            blocks_ref[table[e]] = flat[r0 : r0 + plan.rows, :].astype(LOW)

        for c in range(T // part):
            rows = slice(part * c, part * (c + 1))
            at, to = plan.range_at(c)
            begin, finish = table[at], table[to] + 1
            qs = [stacked(q_ref[own, rows, LANES * p : LANES * (p + 1)]) for p in range(pairs)]
            gs = [stacked(msg_ref[rows, LANES * p : LANES * (p + 1)]) for p in range(pairs)]
            ids = tiled(col_ref[rows, :], T)
            for p in range(pairs):
                for k in range(2):
                    h = 2 * p + k
                    half = slice(part * k, part * (k + 1))
                    logs[p, half, :] = jnp.broadcast_to(stat_ref[rows, h : h + 1], (part, LANES))
                    h = h + HEADS
                    dots[p, half, :] = jnp.broadcast_to(stat_ref[rows, h : h + 1], (part, LANES))
                accs[p] = jnp.zeros((2 * part, LANES), WIDE)

            def step(w, carry, qs=qs, gs=gs, ids=ids):
                seen = ids == row_ref[pl.ds(w, 1), :]
                for p in range(pairs):
                    cols = slice(LANES * p, LANES * (p + 1))
                    key = k_ref[w, :, cols]
                    s = jnp.where(seen, dot(qs[p], key, NT), MASKED)
                    prob = jnp.exp(s - jnp.concatenate([logs[p]] * (T // LANES), axis=1))
                    inner = jnp.concatenate([dots[p]] * (T // LANES), axis=1)
                    grad = prob * (dot(gs[p], v_ref[w, :, cols], NT) - inner)
                    accs[p] = accs[p] + dot(grad.astype(LOW), key, NN)
                return carry

            lax.fori_loop(begin, finish, step, 0)
            for p in range(pairs):
                gq_ref[rows, LANES * p : LANES * (p + 1)] = (unstacked(accs[p]) * SCALE).astype(LOW)

    return kernel


def last_kernel(plan, sources):
    T = plan.tokens
    early = plan.first_late
    part = plan.part
    pairs = HEADS // 2

    def kernel(table, *refs):
        wins = refs[:sources]
        (
            q_ref,
            k_ref,
            v_ref,
            col_ref,
            row_ref,
            gq_ref,
            normed_ref,
            triple_ref,
            x_ref,
            mid_ref,
            gain_ref,
            tail_ref,
            _,
            grad_ref,
            blocks_ref,
        ) = refs[sources : sources + 15]
        mwin, flat, gt, stage, stats, acck, accv, msem, osem = refs[sources + 15 :]
        lo = table[plan.low_at()]
        hi = table[plan.low_at() + 1]
        fetch_window(plan, table, wins, mwin, msem, lo, hi, False)
        fetch_window(plan, table, wins, mwin, msem, lo, hi, True)

        def unpack(w, carry):
            one = mwin[w, T : T + 16, :].astype(WIDE)
            two = mwin[w, T + 16 : T + 32, :].astype(WIDE)
            middle = jnp.concatenate([one[:, T:], two[:, : 2 * T - D]], axis=1)
            stats[w] = (one[:, :T] + middle) + two[:, 2 * T - D :]
            return carry

        lax.fori_loop(lo, hi + 1, unpack, 0)
        for c in range(T // part):
            rows = slice(part * c, part * (c + 1))
            at, to = plan.range_at(c)
            begin, finish = table[at], table[to] + 1
            ks = [stacked(k_ref[rows, LANES * p : LANES * (p + 1)]) for p in range(pairs)]
            vs = [stacked(v_ref[rows, LANES * p : LANES * (p + 1)]) for p in range(pairs)]
            ids = tiled(col_ref[rows, :], T)
            for p in range(pairs):
                acck[p] = jnp.zeros((2 * part, LANES), WIDE)
                accv[p] = jnp.zeros((2 * part, LANES), WIDE)

            def step(w, carry, ks=ks, vs=vs, ids=ids):
                seen = ids == row_ref[pl.ds(w, 1), :]

                def pair_rows(h):
                    return jnp.concatenate(
                        [
                            jnp.broadcast_to(stats[w, h + k : h + k + 1, :], (part, T))
                            for k in range(2)
                        ],
                        axis=0,
                    )

                for p in range(pairs):
                    cols = slice(LANES * p, LANES * (p + 1))
                    q = q_ref[w, :, cols]
                    g = mwin[w, 0:T, cols]
                    s = jnp.where(seen, dot(ks[p], q, NT), MASKED)
                    prob = jnp.exp(s - pair_rows(2 * p))
                    grad = prob * (dot(vs[p], g, NT) - pair_rows(HEADS + 2 * p))
                    acck[p] = acck[p] + dot(grad.astype(LOW), q, NN)
                    accv[p] = accv[p] + dot(prob.astype(LOW), g, NN)
                return carry

            lax.fori_loop(begin, finish, step, 0)
            for p in range(pairs):
                gt[rows, D + LANES * p : D + LANES * (p + 1)] = unstacked(acck[p]).astype(LOW)
                gt[rows, 2 * D + LANES * p : 2 * D + LANES * (p + 1)] = unstacked(accv[p]).astype(
                    LOW
                )
        gt[:, :D] = gq_ref[...]
        fold(flat, AT["triple"], normed_ref, gt, 3 * D)
        put_vector(flat, AT["tbias"], column_sum(gt[:, :D].astype(WIDE)))
        put_vector(flat, AT["tbias"] + D // LANES, column_sum(gt[:, 2 * D :].astype(WIDE)))
        gn = dot(gt[...], triple_ref[...], NT)
        n, r = normalized(x_ref[...].astype(WIDE))
        put_vector(flat, AT["gain1"], column_sum(gn * n))
        put_vector(flat, AT["shift1"], column_sum(gn))
        flat[AT["out"] : AT["out"] + plan.rows, :] = tail_ref[...]
        for e in range(early):
            r0 = plan.start[e]
            stage[e] = flat[r0 : r0 + plan.rows, :].astype(LOW)
            pltpu.make_async_copy(stage.at[e], blocks_ref.at[table[e]], osem.at[e]).start()
        grad_ref[...] = mid_ref[...] + norm_back(gn, gain_ref[0:1, :], n, r)
        for e in range(early):
            pltpu.make_async_copy(stage.at[e], blocks_ref.at[table[e]], osem.at[e]).wait()

    return kernel


def shape(dims, kind):
    return jax.ShapeDtypeStruct(dims, kind)


SMEM = pl.BlockSpec(memory_space=pltpu.SMEM)
VMEM = pl.BlockSpec(memory_space=pltpu.VMEM)
ANY = pl.BlockSpec(memory_space=pl.ANY)


def build(plan):
    T = plan.tokens
    W = plan.window
    R = plan.rows
    N = plan.count
    limit = pltpu.CompilerParams(vmem_limit_bytes=60 * 1024 * 1024)

    def per_device(inputs, cotangent, master, first_moment, second_moment, image_ids, spans):
        device = lax.axis_index(BOTH).astype(jnp.int32)
        shift = ((device * plan.share) % LANES).reshape(1).astype(jnp.int32)
        padded = jnp.pad(image_ids, (plan.reach * T, plan.reach * T), constant_values=-1)
        key_ids = lax.dynamic_slice_in_dim(padded, device * T, W * T, 0).reshape(W, T)
        table = plan.table(device, spans, key_ids)
        own_ids = key_ids[plan.reach]
        columns = jnp.broadcast_to(own_ids[:, None], (T, LANES))

        shifted = pl.pallas_call(
            shift_kernel(plan),
            in_specs=[SMEM, VMEM],
            out_specs=VMEM,
            out_shape=shape((R, LANES), LOW),
            scratch_shapes=[pltpu.VMEM((R + 8, LANES), WIDE)],
            name="shift",
        )(shift, jnp.pad(master, (0, R * LANES - plan.share)).reshape(R, LANES))
        near, core = plan.spread(shifted)
        wins, (table, columns, key_ids) = plan.exchange(inputs, (table, columns, key_ids))
        sources = len(wins)

        outs = pl.pallas_call(
            forward_kernel(plan, sources),
            in_specs=[SMEM, ANY, ANY] + [ANY] * sources + [VMEM] * 3,
            out_specs=[VMEM] * 19,
            out_shape=[
                shape((T, D), LOW),
                shape((T + 32, D), LOW),
                shape((W, T, D), LOW),
                shape((W, T, D), LOW),
                shape((W, T, D), LOW),
                shape((D, 3 * D), LOW),
                shape((T, D), LOW),
                shape((T, D), WIDE),
                shape((T, FF), LOW),
                shape((T, FF), LOW),
                shape((T, D), LOW),
                shape((T, D), LOW),
                shape((T, D), LOW),
                shape((T, D), LOW),
                shape((8, FF), WIDE),
                shape((T, LANES), WIDE),
                shape((8, D), WIDE),
                shape((T, D), LOW),
                shape((T, D), LOW),
            ],
            scratch_shapes=[
                pltpu.VMEM((N, R, LANES), LOW),
                pltpu.VMEM((plan.flat_rows, LANES), WIDE),
                pltpu.VMEM((W, T, D), LOW),
                pltpu.VMEM((D, D), LOW),
                pltpu.VMEM((D, FF), LOW),
                pltpu.VMEM((FF, D), LOW),
                pltpu.VMEM((HEADS // 2, W, 2 * plan.part, T), WIDE),
                pltpu.VMEM((HEADS // 2, 2 * plan.part, LANES), WIDE),
                pltpu.VMEM((HEADS // 2, 2 * plan.part, LANES), WIDE),
                pltpu.VMEM((HEADS // 2, 2 * plan.part, LANES), WIDE),
                pltpu.VMEM((T, D), WIDE),
                pltpu.SemaphoreType.DMA((N,)),
                pltpu.SemaphoreType.DMA((W,)),
            ],
            compiler_params=limit,
            name="forward",
        )(table, near, core, *wins, cotangent, columns, key_ids)
        (
            result,
            message,
            q,
            k,
            v,
            triple,
            normed,
            gmid,
            act,
            gpre,
            gbt,
            n2,
            att,
            gbo,
            vec,
            stat,
            gain,
            k_own,
            v_own,
        ) = outs
        messages, _ = plan.exchange(message)

        middle_call = pl.pallas_call(
            middle_kernel(plan),
            in_specs=[SMEM] + [VMEM] * 14,
            out_specs=[VMEM] * 3,
            out_shape=[
                shape((T, D), LOW),
                shape((N, R, LANES), LOW),
                shape((R, LANES), WIDE),
            ],
            scratch_shapes=[
                pltpu.VMEM((plan.flat_rows - AT["out"] + 8, LANES), WIDE),
                pltpu.VMEM((HEADS // 2, 2 * plan.part, LANES), WIDE),
                pltpu.VMEM((HEADS // 2, 2 * plan.part, LANES), WIDE),
                pltpu.VMEM((HEADS // 2, 2 * plan.part, LANES), WIDE),
            ],
            compiler_params=limit,
            name="middle",
        )
        gq, blocks, tail = middle_call(
            table, q, k, v, message, stat, columns, key_ids, act, gpre, gbt, n2, att, gbo, vec
        )

        late = plan.first_late
        input_grad, blocks = pl.pallas_call(
            last_kernel(plan, sources),
            in_specs=[SMEM]
            + [ANY] * sources
            + [VMEM] * 12
            + [ANY],
            out_specs=[VMEM, ANY],
            out_shape=[shape((T, D), WIDE), shape((N, R, LANES), LOW)],
            scratch_shapes=[
                pltpu.VMEM((W, T + 32, D), LOW),
                pltpu.VMEM((AT["out"] + R + 8, LANES), WIDE),
                pltpu.VMEM((T, 3 * D), LOW),
                pltpu.VMEM((late, R, LANES), LOW),
                pltpu.VMEM((W, 16, T), WIDE),
                pltpu.VMEM((HEADS // 2, 2 * plan.part, LANES), WIDE),
                pltpu.VMEM((HEADS // 2, 2 * plan.part, LANES), WIDE),
                pltpu.SemaphoreType.DMA((W,)),
                pltpu.SemaphoreType.DMA((late,)),
            ],
            input_output_aliases={13 + sources: 1},
            compiler_params=limit,
            name="last",
        )(
            table,
            *messages,
            q,
            k_own,
            v_own,
            columns,
            key_ids,
            gq,
            normed,
            triple,
            inputs,
            gmid,
            gain,
            tail,
            blocks,
        )

        parts = plan.reduce_parts(blocks)
        grad, square = pl.pallas_call(
            unshift_kernel(plan),
            in_specs=[SMEM] + [VMEM] * len(parts),
            out_specs=[VMEM, VMEM],
            out_shape=[shape((R, LANES), WIDE), shape((8, LANES), WIDE)],
            scratch_shapes=[pltpu.VMEM((R + 8, LANES), WIDE)],
            name="unshift",
        )(shift, *parts)
        grad_shard = grad.reshape(-1)[: plan.share]
        grad_norm = jnp.sqrt(plan.total(square)[0, 0])
        ceiling = CLIP_RATIO * math.sqrt(plan.share * N)
        factor = ceiling / jnp.maximum(grad_norm, ceiling)
        clipped = grad_shard * factor
        new_first = BETA_ONE * first_moment + (1.0 - BETA_ONE) * clipped
        new_second = BETA_TWO * second_moment + (1.0 - BETA_TWO) * clipped * clipped
        new_master = master - LEARN_RATE * (
            new_first / (jnp.sqrt(new_second) + ADAM_EPS) + WEIGHT_DECAY * master
        )
        return (
            result,
            input_grad,
            grad_shard,
            grad_norm.reshape(1),
            new_first,
            new_second,
            new_master,
        )

    return per_device


def solution(mesh):
    dp = mesh.shape["dp"]
    fsdp = mesh.shape["fsdp"]
    row = P(BOTH, None)
    flat = P(BOTH)
    in_specs = (row, row, flat, flat, flat, P(), P())
    out_specs = (row, row, flat, P(), flat, flat, flat)

    def per_device(*args):
        inputs, master = args[0], args[2]
        plan = Plan(dp, fsdp, master.shape[0], inputs.shape[0])
        return build(plan)(*args)

    return jax.shard_map(
        per_device, mesh=mesh, in_specs=in_specs, out_specs=out_specs, check_vma=False
    )
```

```python
import math

import jax
import jax.numpy as jnp
from jax import lax
from jax.experimental import pallas as pl
from jax.experimental.pallas import tpu as pltpu
from jax.sharding import PartitionSpec as P


D = 384
HEADS = 6
HEAD_DIM = 64
FF = 1536
IMG = 1370
LANES = 128

LN_EPS = 1e-06
BETA_ONE = 0.5
BETA_TWO = 0.6
LEARN_RATE = 0.01
WEIGHT_DECAY = 0.05
ADAM_EPS = 1e-08
CLIP_RATIO = 0.25
MASKED = -1e30
BOTH = ("dp", "fsdp")
LOW = jnp.bfloat16
WIDE = jnp.float32
SCALE = HEAD_DIM ** (-0.5)

NT = (((1,), (1,)), ((), ()))
NN = (((1,), (0,)), ((), ()))
TN = (((0,), (0,)), ((), ()))

PIECES = [
    ("gain1", D),
    ("shift1", D),
    ("triple", 3 * D * D),
    ("tbias", 2 * D),
    ("out", D * D),
    ("obias", D),
    ("scale1", D),
    ("gain2", D),
    ("shift2", D),
    ("up", D * FF),
    ("ubias", FF),
    ("down", FF * D),
    ("dbias", D),
    ("scale2", D),
]
AT = {}
_row = 0
for _name, _count in PIECES:
    AT[_name] = _row
    _row += _count // LANES
ALL_ROWS = _row


def dot(a, b, dims):
    return lax.dot_general(a, b, dims, preferred_element_type=WIDE)


class Plan:
    def __init__(self, dp, fsdp, share, tokens):
        self.count = dp * fsdp
        self.share = share
        self.rows = -(-(2 * (LANES - 1) + share) // LANES)
        self.rows = -(-self.rows // 16) * 16
        self.start = [e * share // LANES for e in range(self.count)]
        self.tokens = tokens
        self.part = tokens
        self.reach = (IMG - 2 + tokens) // tokens
        self.window = 2 * self.reach + 1
        self.grouped = dp == 4 and fsdp == 8 and self.reach <= 6
        if self.grouped:
            self.stages = [[2, 4, 6], [16, 1, 17], [8]]
        else:
            bits = [1 << k for k in range(self.count.bit_length() - 1)]
            bits = [b for b in bits if b != fsdp] + [fsdp]
            self.stages = [[b] for b in bits]
        masks = [0]
        for stage in self.stages:
            masks = masks + [m ^ s for s in stage for m in masks]
        self.bits = [masks[1 << k] for k in range(self.count.bit_length() - 1)]
        self.first_late = next(e for e in range(self.count) if self.start[e] >= AT["out"])
        self.flat_rows = -(-(self.start[-1] + self.rows) // 8) * 8

    def send(self, x, mask):
        return lax.ppermute(x, BOTH, [(i, i ^ mask) for i in range(self.count)])

    def spread(self, own):
        buf = own[None]
        for stage in self.stages[:-1]:
            buf = jnp.concatenate([buf] + [self.send(buf, m) for m in stage], axis=0)
        return buf, self.send(buf, self.stages[-1][0])

    def reduce_parts(self, keep, away):
        parts = [keep, self.send(away, self.stages[-1][0])]
        for stage in reversed(self.stages[:-1]):
            total = parts[0].astype(WIDE)
            for part in parts[1:]:
                total = total + part.astype(WIDE)
            buf = total.astype(LOW)
            split = buf.reshape((len(stage) + 1, -1) + buf.shape[1:])
            parts = [split[0]] + [self.send(split[k + 1], m) for k, m in enumerate(stage)]
        return [part[0] for part in parts]

    def exchange(self, block, extra=()):
        own = block[None]
        if self.grouped:
            hops = []
            for m in (1, 2, 3, 4, 6):
                hops.append(self.send(own, m))
            one, two, three, four, six = hops
            pair = jnp.concatenate([four, six], axis=0)
            quad = jnp.concatenate([two, three, four, six], axis=0)
            pair, quad, extra = lax.optimization_barrier((pair, quad, extra))
            across = [(8 + j, 16 + j) for j in range(8)] + [(16 + j, 8 + j) for j in range(8)]
            skew = [(a, b ^ 1) for a, b in across]
            far = lax.ppermute(quad, BOTH, across)
            far_beside = lax.ppermute(pair, BOTH, skew)
            beside = self.send(pair, 1)
            row = jnp.concatenate([own, one, quad, beside], axis=0)
            home = self.send(row, 8)
            return [row, home, far, far_beside], extra
        slots = []
        for slot in range(self.window):
            by = self.reach - slot
            pairs = [(i, i + by) for i in range(self.count) if 0 <= i + by < self.count]
            slots.append(own if by == 0 else lax.ppermute(own, BOTH, pairs))
        return [jnp.concatenate(slots, axis=0)], extra

    def table(self, device, spans, key_ids):
        e = jnp.arange(self.count, dtype=jnp.int32)
        rel = e ^ device
        where = jnp.zeros_like(e)
        for k, bit in enumerate(self.bits):
            where = where + jnp.where((rel & bit) != 0, 1 << k, 0)
        slot = jnp.arange(self.window, dtype=jnp.int32)
        if self.grouped:
            other = device - self.reach + slot
            mask = (other ^ device) & 7
            pos = jnp.where(mask == 6, 5, jnp.where(mask == 5, 6, mask))
            cross = (other >> 3) ^ (device >> 3)
            late = pos >= 6
            source = jnp.where(cross == 0, 0, jnp.where(cross == 1, 1, jnp.where(late, 3, 2)))
            index = jnp.where(source >= 2, jnp.where(late, pos - 6, pos - 2), pos)
        else:
            source = jnp.zeros_like(slot)
            index = slot
        bounds = lax.dynamic_index_in_dim(spans, device, 0, keepdims=False)
        ends = jnp.clip(bounds - device + self.reach, 0, self.window - 1)
        own = key_ids[self.reach]
        low, high = own[:: self.part], own[self.part - 1 :: self.part]
        seen = (key_ids[:, -1][None] >= low[:, None]) & (key_ids[:, 0][None] <= high[:, None])
        seen = seen & (slot >= ends[0])[None] & (slot <= ends[1])[None]
        begin = jnp.min(jnp.where(seen, slot[None], self.window), axis=1)
        finish = jnp.max(jnp.where(seen, slot[None], -1), axis=1)
        return jnp.concatenate([where, source, index, ends, begin, finish]).astype(jnp.int32)

    def source_at(self, slot):
        return self.count + slot

    def index_at(self, slot):
        return self.count + self.window + slot

    def low_at(self):
        return self.count + 2 * self.window

    def range_at(self, quarter):
        at = self.count + 2 * self.window + 2 + quarter
        return at, at + self.tokens // self.part


def fetch_window(plan, table, sources, dest, sems, lo, hi, wait):
    def step(slot, carry):
        for k, source in enumerate(sources):

            @pl.when(table[plan.source_at(slot)] == k)
            def _(source=source):
                copy = pltpu.make_async_copy(
                    source.at[table[plan.index_at(slot)]], dest.at[slot], sems.at[slot]
                )
                if wait:
                    copy.wait()
                else:
                    copy.start()

        return carry

    lax.fori_loop(lo, hi + 1, step, 0)


def normalized(x):
    center = x - jnp.mean(x, axis=-1, keepdims=True)
    spread = jnp.mean(center * center, axis=-1, keepdims=True)
    r = lax.rsqrt(spread + LN_EPS)
    return center * r, r


def norm_back(grad, gain, n, r):
    g = grad * gain
    inner = jnp.mean(g, axis=-1, keepdims=True)
    outer = jnp.mean(g * n, axis=-1, keepdims=True)
    return r * (g - inner - n * outer)


def vector(ref, row, width):
    return jnp.concatenate([ref[row + j : row + j + 1, :] for j in range(width // LANES)], axis=1)


def put_vector(ref, row, value):
    for j in range(value.shape[1] // LANES):
        ref[row + j : row + j + 1, :] = value[:, LANES * j : LANES * (j + 1)]


def stacked(x):
    left = lax.broadcasted_iota(jnp.int32, x.shape, 1) < HEAD_DIM
    return jnp.concatenate([jnp.where(left, x, 0), jnp.where(left, 0, x)], axis=0)


def unstacked(x):
    half = x.shape[0] // 2
    left = lax.broadcasted_iota(jnp.int32, (half, LANES), 1) < HEAD_DIM
    return jnp.where(left, x[:half], x[half:])


def tiled(ids, width):
    ids = jnp.concatenate([ids] * (width // LANES), axis=1)
    return jnp.concatenate([ids, ids], axis=0)


def scaled_query(low, weight, bias):
    q = dot(low, weight, NN) + bias
    return (q.astype(LOW).astype(WIDE) * SCALE).astype(LOW)


def column_sum(x):
    return jnp.sum(x, axis=0, keepdims=True)


def shift_kernel(plan):
    def kernel(table, x_ref, out_ref, pad):
        s = table[0]
        x = x_ref[...]
        y = pltpu.roll(x, s, 1)
        pad[0:8, :] = jnp.zeros((8, LANES), WIDE)
        pad[8:, :] = y
        lane = lax.broadcasted_iota(jnp.int32, y.shape, 1)
        out_ref[...] = jnp.where(lane >= s, y, pad[7 : 7 + plan.rows, :]).astype(LOW)

    return kernel


def unshift_kernel(plan):
    def kernel(table, *refs):
        parts, (out_ref, sq_ref, pad) = refs[:-3], refs[-3:]
        s = table[0]
        got = [p[...].astype(WIDE) for p in parts]
        while len(got) > 1:
            got = [got[k] + got[k + 1] for k in range(0, len(got), 2)]
        y = pltpu.roll(got[0], LANES - s, 1)
        pad[0 : plan.rows, :] = y
        pad[plan.rows :, :] = jnp.zeros((8, LANES), WIDE)
        lane = lax.broadcasted_iota(jnp.int32, y.shape, 1)
        row = lax.broadcasted_iota(jnp.int32, y.shape, 0)
        out = jnp.where(lane < LANES - s, y, pad[1 : 1 + plan.rows, :])
        out = jnp.where(row * LANES + lane < plan.share, out, 0.0)
        out_ref[...] = out
        sq = jnp.sum(jnp.sum(out * out, axis=0, keepdims=True), axis=1, keepdims=True)
        sq_ref[...] = jnp.broadcast_to(sq, (plan.count, LANES))

    return kernel


VEC = {"gain1": 0, "shift1": 1, "tbias": 2, "obias": 3, "scale1": 4, "gain2": 5, "shift2": 6}
VEC.update({"ubias": 7, "dbias": 8, "scale2": 9})


def unpack_kernel(plan):
    half = plan.count // 2

    def kernel(table, near, core, triple_ref, wo, wup, wdn, vec_ref, wbuf, flat, wsem):
        def weight_copy(e, wait):
            t = table[e]

            @pl.when(t < half)
            def _():
                c = pltpu.make_async_copy(near.at[t], wbuf.at[e], wsem.at[e])
                c.wait() if wait else c.start()

            @pl.when(t >= half)
            def _():
                c = pltpu.make_async_copy(core.at[t - half], wbuf.at[e], wsem.at[e])
                c.wait() if wait else c.start()

        def start_one(e, carry):
            weight_copy(e, False)
            return carry

        def wait_one(e, carry):
            weight_copy(e, True)
            return carry

        lax.fori_loop(0, plan.count, start_one, 0)
        lax.fori_loop(0, plan.count, wait_one, 0)
        for e in range(plan.count):
            r0 = plan.start[e]
            block = wbuf[e].astype(WIDE)
            if e:
                before = flat[r0 : r0 + 1, :]
                flat[r0 : r0 + plan.rows, :] = block
                flat[r0 : r0 + 1, :] = before + block[0:1, :]
            else:
                flat[r0 : r0 + plan.rows, :] = block

        def unfold(dest, name, height, width):
            wide = width // LANES
            step = min(height, 384)
            for j in range(wide):
                for i in range(0, height, step):
                    dest[i : i + step, LANES * j : LANES * (j + 1)] = flat[
                        pl.ds(AT[name] + i * wide + j, step, stride=wide), :
                    ].astype(LOW)

        unfold(triple_ref, "triple", D, 3 * D)
        unfold(wo, "out", D, D)
        unfold(wup, "up", D, FF)
        unfold(wdn, "down", FF, D)
        vec_ref[...] = jnp.zeros(vec_ref.shape, WIDE)
        for name, row in VEC.items():
            width = dict(PIECES)[name]
            vec_ref[row : row + 1, :width] = vector(flat, AT[name], width)

    return kernel


def forward_kernel(plan, sources):
    T = plan.tokens
    own = plan.reach
    part = plan.part
    pairs = HEADS // 2

    def kernel(table, *refs):
        wins = refs[:sources]
        triple_ref, wo, wup, wdn, par_ref, cot_ref, col_ref, row_ref = refs[sources : 8 + sources]
        (
            out_ref,
            msg_ref,
            q_ref,
            k_ref,
            v_ref,
            norm_ref,
            normed_ref,
            mid_ref,
            act_ref,
            pre_ref,
            gbt_ref,
            n2_ref,
            att_ref,
            gbo_ref,
            vec_ref,
            stat_ref,
            kown_ref,
            vown_ref,
        ) = refs[8 + sources : 26 + sources]
        xwin, scores, tops, sums, accs, mix, xsem = refs[26 + sources :]
        lo = table[plan.low_at()]
        hi = table[plan.low_at() + 1]

        def param(name):
            row = VEC[name]
            return par_ref[row : row + 1, : dict(PIECES)[name]]

        fetch_window(plan, table, wins, xwin, xsem, lo, hi, False)
        gain1 = param("gain1")
        shift1 = param("shift1")
        tbias = param("tbias")
        fetch_window(plan, table, wins, xwin, xsem, lo, hi, True)

        def project(w, carry):
            n, _ = normalized(xwin[w].astype(WIDE))
            low = (n * gain1 + shift1).astype(LOW)
            norm_ref[w] = low
            kv = dot(low, triple_ref[:, D:], NN)
            k_ref[w] = kv[:, :D].astype(LOW)
            v_ref[w] = (kv[:, D:] + tbias[:, D:]).astype(LOW)
            return carry

        lax.fori_loop(lo, hi + 1, project, 0)
        kown_ref[...] = k_ref[own]
        vown_ref[...] = v_ref[own]
        low = norm_ref[own]
        normed_ref[...] = low
        q_ref[...] = scaled_query(low, triple_ref[:, :D], tbias[:, :D])

        lane = lax.broadcasted_iota(jnp.int32, (part, LANES), 1)
        for c in range(T // part):
            rows = slice(part * c, part * (c + 1))
            at, to = plan.range_at(c)
            begin, finish = table[at], table[to] + 1
            qs = [stacked(q_ref[rows, LANES * p : LANES * (p + 1)]) for p in range(pairs)]
            ids = tiled(col_ref[rows, :], T)
            for p in range(pairs):
                tops[p] = jnp.full((2 * part, LANES), MASKED, WIDE)
                sums[p] = jnp.zeros((2 * part, LANES), WIDE)
                accs[p] = jnp.zeros((2 * part, LANES), WIDE)

            def first(w, carry, qs=qs, ids=ids):
                seen = ids == row_ref[pl.ds(w, 1), :]
                for p in range(pairs):
                    s = dot(qs[p], k_ref[w, :, LANES * p : LANES * (p + 1)], NT)
                    s = jnp.where(seen, s, MASKED)
                    scores[p, w] = s
                    top = tops[p]
                    for j in range(0, T, LANES):
                        top = jnp.maximum(top, s[:, j : j + LANES])
                    tops[p] = top
                return carry

            lax.fori_loop(begin, finish, first, 0)
            for p in range(pairs):
                top = jnp.max(tops[p], axis=1, keepdims=True)
                tops[p] = jnp.broadcast_to(top, (2 * part, LANES))

            def second(w, carry):
                for p in range(pairs):
                    top = jnp.concatenate([tops[p]] * (T // LANES), axis=1)
                    e = jnp.exp(scores[p, w] - top)
                    total = sums[p]
                    for j in range(0, T, LANES):
                        total = total + e[:, j : j + LANES]
                    sums[p] = total
                    value = v_ref[w, :, LANES * p : LANES * (p + 1)]
                    accs[p] = accs[p] + dot(e.astype(LOW), value, NN)
                return carry

            lax.fori_loop(begin, finish, second, 0)
            stats = jnp.zeros((part, LANES), WIDE)
            for p in range(pairs):
                total = jnp.sum(sums[p], axis=1, keepdims=True)
                mixed = accs[p] / total
                mix[rows, LANES * p : LANES * (p + 1)] = unstacked(mixed)
                log = tops[p] + jnp.log(total)
                stats = jnp.where(lane == 2 * p, log[:part], stats)
                stats = jnp.where(lane == 2 * p + 1, log[part:], stats)
            stat_ref[rows, :] = stats
        att = mix[...]
        att_low = att.astype(LOW)
        att_ref[...] = att_low
        x = xwin[own].astype(WIDE)
        scale1 = param("scale1")
        scale2 = param("scale2")
        gain2 = param("gain2")
        branch_one = dot(att_low, wo[...], NN) + param("obias")
        middle = x + scale1 * branch_one
        n2, r2 = normalized(middle)
        n2_low = (n2 * gain2 + param("shift2")).astype(LOW)
        n2_ref[...] = n2_low
        pre = dot(n2_low, wup[...], NN) + param("ubias")
        cdf = 0.5 * (1.0 + lax.erf(pre * math.sqrt(0.5)))
        act_low = (pre * cdf).astype(LOW)
        act_ref[...] = act_low
        slope = cdf + pre * (jnp.exp(-0.5 * pre * pre) * (1.0 / math.sqrt(2.0 * math.pi)))
        branch_two = dot(act_low, wdn[...], NN) + param("dbias")
        out_ref[...] = (middle + scale2 * branch_two).astype(LOW)

        up = cot_ref[...].astype(WIDE)
        gbt = (scale2 * up).astype(LOW)
        gbt_ref[...] = gbt
        gpre = (dot(gbt, wdn[...], NT) * slope).astype(LOW)
        pre_ref[...] = gpre
        gn2 = dot(gpre, wup[...], NT)
        gmid = up + norm_back(gn2, gain2, n2, r2)
        mid_ref[...] = gmid
        gbo = (scale1 * gmid).astype(LOW)
        gbo_ref[...] = gbo
        gatt = dot(gbo, wo[...], NT).astype(LOW)
        msg_ref[0:T, :] = gatt
        inner = gatt.astype(WIDE) * att
        stats = stat_ref[...]
        lane = lax.broadcasted_iota(jnp.int32, (T, LANES), 1)
        left = lane < HEAD_DIM
        for p in range(HEADS // 2):
            piece = inner[:, LANES * p : LANES * (p + 1)]
            one = jnp.sum(jnp.where(left, piece, 0.0), axis=1, keepdims=True)
            two = jnp.sum(jnp.where(left, 0.0, piece), axis=1, keepdims=True)
            stats = jnp.where(lane == HEADS + 2 * p, one, stats)
            stats = jnp.where(lane == HEADS + 2 * p + 1, two, stats)
        stat_ref[...] = stats
        high = stats.astype(LOW).astype(WIDE)
        rest = pltpu.roll(stats - high, 2 * HEADS, 1)
        flipped = jnp.transpose(jnp.where(lane < 2 * HEADS, high, rest))
        tail = flipped[16:24, :]
        msg_ref[T : T + 16, 0:T] = flipped[0:16, :].astype(LOW)
        msg_ref[T : T + 16, T:] = jnp.concatenate(
            [tail[:, :LANES], tail[:, LANES:]], axis=0
        ).astype(LOW)

        vec_ref[...] = jnp.zeros(vec_ref.shape, WIDE)
        vec_ref[0:1, :D] = column_sum(up * branch_two)
        vec_ref[1:2, :D] = column_sum(gbt.astype(WIDE))
        vec_ref[2:3, :] = column_sum(gpre.astype(WIDE))
        vec_ref[3:4, :D] = column_sum(gn2 * n2)
        vec_ref[4:5, :D] = column_sum(gn2)
        vec_ref[5:6, :D] = column_sum(gmid * branch_one)
        vec_ref[6:7, :D] = column_sum(gbo.astype(WIDE))

    return kernel


def fold(dest, row, left, right, width):
    wide = width // LANES
    height = left.shape[1]
    for i in range(0, height, 384):
        part = dot(left[:, i : i + 384], right[...], TN)
        for j in range(wide):
            dest[pl.ds(row + i * wide + j, 384, stride=wide), :] = part[
                :, LANES * j : LANES * (j + 1)
            ]


def query_kernel(plan):
    T = plan.tokens
    part = plan.part
    pairs = HEADS // 2

    def kernel(
        table, q_ref, k_ref, v_ref, msg_ref, stat_ref, col_ref, row_ref, gq_ref, logs, dots, accs
    ):
        for c in range(T // part):
            rows = slice(part * c, part * (c + 1))
            at, to = plan.range_at(c)
            begin, finish = table[at], table[to] + 1
            qs = [stacked(q_ref[rows, LANES * p : LANES * (p + 1)]) for p in range(pairs)]
            gs = [stacked(msg_ref[rows, LANES * p : LANES * (p + 1)]) for p in range(pairs)]
            ids = tiled(col_ref[rows, :], T)
            for p in range(pairs):
                for k in range(2):
                    h = 2 * p + k
                    half = slice(part * k, part * (k + 1))
                    logs[p, half, :] = jnp.broadcast_to(stat_ref[rows, h : h + 1], (part, LANES))
                    h = h + HEADS
                    dots[p, half, :] = jnp.broadcast_to(stat_ref[rows, h : h + 1], (part, LANES))
                accs[p] = jnp.zeros((2 * part, LANES), WIDE)

            def step(w, carry, qs=qs, gs=gs, ids=ids):
                seen = ids == row_ref[pl.ds(w, 1), :]
                for p in range(pairs):
                    cols = slice(LANES * p, LANES * (p + 1))
                    key = k_ref[w, :, cols]
                    s = jnp.where(seen, dot(qs[p], key, NT), MASKED)
                    prob = jnp.exp(s - jnp.concatenate([logs[p]] * (T // LANES), axis=1))
                    inner = jnp.concatenate([dots[p]] * (T // LANES), axis=1)
                    grad = prob * (dot(gs[p], v_ref[w, :, cols], NT) - inner)
                    accs[p] = accs[p] + dot(grad.astype(LOW), key, NN)
                return carry

            lax.fori_loop(begin, finish, step, 0)
            for p in range(pairs):
                gq_ref[rows, LANES * p : LANES * (p + 1)] = (unstacked(accs[p]) * SCALE).astype(LOW)

    return kernel


def weight_kernel(plan):
    base = AT["out"]
    half = plan.count // 2

    def kernel(
        table,
        norm_ref,
        triple_ref,
        par_ref,
        act_ref,
        pre_ref,
        gbt_ref,
        n2_ref,
        att_ref,
        gbo_ref,
        vec_ref,
        q_ref,
        keep_ref,
        away_ref,
        tail_ref,
        flat,
    ):
        fold(flat, AT["down"] - base, act_ref, gbt_ref, D)
        fold(flat, AT["up"] - base, n2_ref, pre_ref, FF)
        fold(flat, AT["out"] - base, att_ref, gbo_ref, D)
        put_vector(flat, AT["scale2"] - base, vec_ref[0:1, :D])
        put_vector(flat, AT["dbias"] - base, vec_ref[1:2, :D])
        put_vector(flat, AT["ubias"] - base, vec_ref[2:3, :])
        put_vector(flat, AT["gain2"] - base, vec_ref[3:4, :D])
        put_vector(flat, AT["shift2"] - base, vec_ref[4:5, :D])
        put_vector(flat, AT["scale1"] - base, vec_ref[5:6, :D])
        put_vector(flat, AT["obias"] - base, vec_ref[6:7, :D])
        end = ALL_ROWS - base
        flat[end:, :] = jnp.zeros((flat.shape[0] - end, LANES), WIDE)
        tail_ref[...] = flat[0 : plan.rows, :]
        for e in range(plan.first_late, plan.count):
            r0 = plan.start[e] - base
            t = table[e]

            @pl.when(t < half)
            def _(r0=r0, t=t):
                keep_ref[t] = flat[r0 : r0 + plan.rows, :].astype(LOW)

            @pl.when(t >= half)
            def _(r0=r0, t=t):
                away_ref[t - half] = flat[r0 : r0 + plan.rows, :].astype(LOW)

        bias = par_ref[VEC["tbias"] : VEC["tbias"] + 1, :D]

        def project(w, carry):
            q_ref[w] = scaled_query(norm_ref[w], triple_ref[:, :D], bias)
            return carry

        lax.fori_loop(table[plan.low_at()], table[plan.low_at() + 1] + 1, project, 0)

    return kernel


def last_kernel(plan, sources):
    T = plan.tokens
    early = plan.first_late
    half = plan.count // 2
    part = plan.part
    pairs = HEADS // 2

    def kernel(table, *refs):
        wins = refs[:sources]
        (
            q_ref,
            k_ref,
            v_ref,
            col_ref,
            row_ref,
            gq_ref,
            normed_ref,
            triple_ref,
            x_ref,
            mid_ref,
            par_ref,
            tail_ref,
            _,
            _,
            grad_ref,
            keep_ref,
            away_ref,
        ) = refs[sources : sources + 17]
        mwin, flat, gt, stage, stats, spare, acck, accv, msem, osem = refs[sources + 17 :]
        lo = table[plan.low_at()]
        hi = table[plan.low_at() + 1]
        fetch_window(plan, table, wins, mwin, msem, lo, hi, False)
        fetch_window(plan, table, wins, mwin, msem, lo, hi, True)

        def unpack(w, carry):
            got = mwin[w, T : T + 16, :].astype(WIDE)
            spare[0:16, :] = got[:, :T]
            spare[16:24, :] = jnp.concatenate([got[:8, T:], got[8:, T:]], axis=1)
            stats[w, 0 : 2 * HEADS, :] = spare[0 : 2 * HEADS, :] + spare[2 * HEADS : 4 * HEADS, :]
            return carry

        lax.fori_loop(lo, hi + 1, unpack, 0)
        for c in range(T // part):
            rows = slice(part * c, part * (c + 1))
            at, to = plan.range_at(c)
            begin, finish = table[at], table[to] + 1
            ks = [stacked(k_ref[rows, LANES * p : LANES * (p + 1)]) for p in range(pairs)]
            vs = [stacked(v_ref[rows, LANES * p : LANES * (p + 1)]) for p in range(pairs)]
            ids = tiled(col_ref[rows, :], T)
            for p in range(pairs):
                acck[p] = jnp.zeros((2 * part, LANES), WIDE)
                accv[p] = jnp.zeros((2 * part, LANES), WIDE)

            def step(w, carry, ks=ks, vs=vs, ids=ids):
                seen = ids == row_ref[pl.ds(w, 1), :]

                def pair_rows(h):
                    return jnp.concatenate(
                        [
                            jnp.broadcast_to(stats[w, h + k : h + k + 1, :], (part, T))
                            for k in range(2)
                        ],
                        axis=0,
                    )

                for p in range(pairs):
                    cols = slice(LANES * p, LANES * (p + 1))
                    q = q_ref[w, :, cols]
                    g = mwin[w, 0:T, cols]
                    s = jnp.where(seen, dot(ks[p], q, NT), MASKED)
                    prob = jnp.exp(s - pair_rows(2 * p))
                    grad = prob * (dot(vs[p], g, NT) - pair_rows(HEADS + 2 * p))
                    acck[p] = acck[p] + dot(grad.astype(LOW), q, NN)
                    accv[p] = accv[p] + dot(prob.astype(LOW), g, NN)
                return carry

            lax.fori_loop(begin, finish, step, 0)
            for p in range(pairs):
                gt[rows, D + LANES * p : D + LANES * (p + 1)] = unstacked(acck[p]).astype(LOW)
                gt[rows, 2 * D + LANES * p : 2 * D + LANES * (p + 1)] = unstacked(accv[p]).astype(
                    LOW
                )
        gt[:, :D] = gq_ref[...]
        fold(flat, AT["triple"], normed_ref, gt, 3 * D)
        put_vector(flat, AT["tbias"], column_sum(gt[:, :D].astype(WIDE)))
        put_vector(flat, AT["tbias"] + D // LANES, column_sum(gt[:, 2 * D :].astype(WIDE)))
        gn = dot(gt[...], triple_ref[...], NT)
        n, r = normalized(x_ref[...].astype(WIDE))
        put_vector(flat, AT["gain1"], column_sum(gn * n))
        put_vector(flat, AT["shift1"], column_sum(gn))
        flat[AT["out"] : AT["out"] + plan.rows, :] = tail_ref[...]

        def put(e, wait):
            t = table[e]

            @pl.when(t < half)
            def _():
                c = pltpu.make_async_copy(stage.at[e], keep_ref.at[t], osem.at[e])
                c.wait() if wait else c.start()

            @pl.when(t >= half)
            def _():
                c = pltpu.make_async_copy(stage.at[e], away_ref.at[t - half], osem.at[e])
                c.wait() if wait else c.start()

        for e in range(early):
            r0 = plan.start[e]
            stage[e] = flat[r0 : r0 + plan.rows, :].astype(LOW)
            put(e, False)
        gain1 = par_ref[VEC["gain1"] : VEC["gain1"] + 1, :D]
        grad_ref[...] = mid_ref[...] + norm_back(gn, gain1, n, r)
        for e in range(early):
            put(e, True)

    return kernel


def shape(dims, kind):
    return jax.ShapeDtypeStruct(dims, kind)


SMEM = pl.BlockSpec(memory_space=pltpu.SMEM)
VMEM = pl.BlockSpec(memory_space=pltpu.VMEM)
ANY = pl.BlockSpec(memory_space=pl.ANY)


def build(plan):
    T = plan.tokens
    W = plan.window
    R = plan.rows
    N = plan.count
    limit = pltpu.CompilerParams(vmem_limit_bytes=60 * 1024 * 1024)

    def per_device(inputs, cotangent, master, first_moment, second_moment, image_ids, spans):
        device = lax.axis_index(BOTH).astype(jnp.int32)
        shift = ((device * plan.share) % LANES).reshape(1).astype(jnp.int32)
        padded = jnp.pad(image_ids, (plan.reach * T, plan.reach * T), constant_values=-1)
        key_ids = lax.dynamic_slice_in_dim(padded, device * T, W * T, 0).reshape(W, T)
        table = plan.table(device, spans, key_ids)
        own_ids = key_ids[plan.reach]
        columns = jnp.broadcast_to(own_ids[:, None], (T, LANES))

        shifted = pl.pallas_call(
            shift_kernel(plan),
            in_specs=[SMEM, VMEM],
            out_specs=VMEM,
            out_shape=shape((R, LANES), LOW),
            scratch_shapes=[pltpu.VMEM((R + 8, LANES), WIDE)],
            name="shift",
        )(shift, jnp.pad(master, (0, R * LANES - plan.share)).reshape(R, LANES))
        near, core = plan.spread(shifted)
        wins, (table, columns, key_ids) = plan.exchange(inputs, (table, columns, key_ids))
        sources = len(wins)

        half = pltpu.VMEM((HEADS // 2, 2 * plan.part, LANES), WIDE)
        unpack = pl.pallas_call(
            unpack_kernel(plan),
            in_specs=[SMEM, ANY, ANY],
            out_specs=[VMEM] * 5,
            out_shape=[
                shape((D, 3 * D), LOW),
                shape((D, D), LOW),
                shape((D, FF), LOW),
                shape((FF, D), LOW),
                shape((16, FF), WIDE),
            ],
            scratch_shapes=[
                pltpu.VMEM((N, R, LANES), LOW),
                pltpu.VMEM((plan.flat_rows, LANES), WIDE),
                pltpu.SemaphoreType.DMA((N,)),
            ],
            compiler_params=limit,
            name="unpack",
        )
        triple, wo, wup, wdn, params = unpack(table, near, core)

        outs = pl.pallas_call(
            forward_kernel(plan, sources),
            in_specs=[SMEM] + [ANY] * sources + [VMEM] * 8,
            out_specs=[VMEM] * 18,
            out_shape=[
                shape((T, D), LOW),
                shape((T + 16, D), LOW),
                shape((T, D), LOW),
                shape((W, T, D), LOW),
                shape((W, T, D), LOW),
                shape((W, T, D), LOW),
                shape((T, D), LOW),
                shape((T, D), WIDE),
                shape((T, FF), LOW),
                shape((T, FF), LOW),
                shape((T, D), LOW),
                shape((T, D), LOW),
                shape((T, D), LOW),
                shape((T, D), LOW),
                shape((8, FF), WIDE),
                shape((T, LANES), WIDE),
                shape((T, D), LOW),
                shape((T, D), LOW),
            ],
            scratch_shapes=[
                pltpu.VMEM((W, T, D), LOW),
                pltpu.VMEM((HEADS // 2, W, 2 * plan.part, T), WIDE),
                half,
                half,
                half,
                pltpu.VMEM((T, D), WIDE),
                pltpu.SemaphoreType.DMA((W,)),
            ],
            compiler_params=limit,
            name="forward",
        )(table, *wins, triple, wo, wup, wdn, params, cotangent, columns, key_ids)
        (
            result,
            message,
            q,
            k,
            v,
            norms,
            normed,
            gmid,
            act,
            gpre,
            gbt,
            n2,
            att,
            gbo,
            vec,
            stat,
            k_own,
            v_own,
        ) = outs
        messages, _ = plan.exchange(message)

        query_call = pl.pallas_call(
            query_kernel(plan),
            in_specs=[SMEM] + [VMEM] * 7,
            out_specs=VMEM,
            out_shape=shape((T, D), LOW),
            scratch_shapes=[half] * 3,
            compiler_params=limit,
            name="query",
        )
        gq = query_call(table, q, k, v, message, stat, columns, key_ids)
        weight_call = pl.pallas_call(
            weight_kernel(plan),
            in_specs=[SMEM] + [VMEM] * 10,
            out_specs=[VMEM] * 4,
            out_shape=[
                shape((W, T, D), LOW),
                shape((N // 2, R, LANES), LOW),
                shape((N // 2, R, LANES), LOW),
                shape((R, LANES), WIDE),
            ],
            scratch_shapes=[
                pltpu.VMEM((plan.flat_rows - AT["out"] + 8, LANES), WIDE),
            ],
            compiler_params=limit,
            name="weight",
        )
        queries, keep, away, tail = weight_call(
            table, norms, triple, params, act, gpre, gbt, n2, att, gbo, vec
        )

        late = plan.first_late
        input_grad, keep, away = pl.pallas_call(
            last_kernel(plan, sources),
            in_specs=[SMEM] + [ANY] * sources + [VMEM] * 12 + [ANY, ANY],
            out_specs=[VMEM, ANY, ANY],
            out_shape=[
                shape((T, D), WIDE),
                shape((N // 2, R, LANES), LOW),
                shape((N // 2, R, LANES), LOW),
            ],
            scratch_shapes=[
                pltpu.VMEM((W, T + 16, D), LOW),
                pltpu.VMEM((AT["out"] + R + 8, LANES), WIDE),
                pltpu.VMEM((T, 3 * D), LOW),
                pltpu.VMEM((late, R, LANES), LOW),
                pltpu.VMEM((W, 16, T), WIDE),
                pltpu.VMEM((24, T), WIDE),
                half,
                half,
                pltpu.SemaphoreType.DMA((W,)),
                pltpu.SemaphoreType.DMA((late,)),
            ],
            input_output_aliases={13 + sources: 1, 14 + sources: 2},
            compiler_params=limit,
            name="last",
        )(
            table,
            *messages,
            queries,
            k_own,
            v_own,
            columns,
            key_ids,
            gq,
            normed,
            triple,
            inputs,
            gmid,
            params,
            tail,
            keep,
            away,
        )

        parts = plan.reduce_parts(keep, away)
        grad, square = pl.pallas_call(
            unshift_kernel(plan),
            in_specs=[SMEM] + [VMEM] * len(parts),
            out_specs=[VMEM, VMEM],
            out_shape=[shape((R, LANES), WIDE), shape((N, LANES), WIDE)],
            scratch_shapes=[pltpu.VMEM((R + 8, LANES), WIDE)],
            name="unshift",
        )(shift, *parts)
        grad_shard = grad.reshape(-1)[: plan.share]
        squares = lax.all_to_all(square, BOTH, 0, 0, tiled=True)
        grad_norm = jnp.sqrt(jnp.sum(squares[:, 0]))
        ceiling = CLIP_RATIO * math.sqrt(plan.share * N)
        factor = ceiling / jnp.maximum(grad_norm, ceiling)
        clipped = grad_shard * factor
        new_first = BETA_ONE * first_moment + (1.0 - BETA_ONE) * clipped
        new_second = BETA_TWO * second_moment + (1.0 - BETA_TWO) * clipped * clipped
        new_master = master - LEARN_RATE * (
            new_first / (jnp.sqrt(new_second) + ADAM_EPS) + WEIGHT_DECAY * master
        )
        return (
            result,
            input_grad,
            grad_shard,
            grad_norm.reshape(1),
            new_first,
            new_second,
            new_master,
        )

    return per_device


def solution(mesh):
    dp = mesh.shape["dp"]
    fsdp = mesh.shape["fsdp"]
    row = P(BOTH, None)
    flat = P(BOTH)
    in_specs = (row, row, flat, flat, flat, P(), P())
    out_specs = (row, row, flat, P(), flat, flat, flat)

    def per_device(*args):
        inputs, master = args[0], args[2]
        plan = Plan(dp, fsdp, master.shape[0], inputs.shape[0])
        return build(plan)(*args)

    return jax.shard_map(
        per_device, mesh=mesh, in_specs=in_specs, out_specs=out_specs, check_vma=False
    )
```

```python
import math

import jax
import jax.numpy as jnp
from jax import lax
from jax.experimental import pallas as pl
from jax.experimental.pallas import tpu as pltpu
from jax.sharding import PartitionSpec as P


D = 384
HEADS = 6
HEAD_DIM = 64
FF = 1536
IMG = 1370
LANES = 128

LN_EPS = 1e-06
BETA_ONE = 0.5
BETA_TWO = 0.6
LEARN_RATE = 0.01
WEIGHT_DECAY = 0.05
ADAM_EPS = 1e-08
CLIP_RATIO = 0.25
MASKED = -1e30
BOTH = ("dp", "fsdp")
LOW = jnp.bfloat16
WIDE = jnp.float32
SCALE = HEAD_DIM ** (-0.5)

NT = (((1,), (1,)), ((), ()))
NN = (((1,), (0,)), ((), ()))
TN = (((0,), (0,)), ((), ()))

PIECES = [
    ("gain1", D),
    ("shift1", D),
    ("triple", 3 * D * D),
    ("tbias", 2 * D),
    ("out", D * D),
    ("obias", D),
    ("scale1", D),
    ("gain2", D),
    ("shift2", D),
    ("up", D * FF),
    ("ubias", FF),
    ("down", FF * D),
    ("dbias", D),
    ("scale2", D),
]
AT = {}
_row = 0
for _name, _count in PIECES:
    AT[_name] = _row
    _row += _count // LANES
ALL_ROWS = _row


def dot(a, b, dims):
    return lax.dot_general(a, b, dims, preferred_element_type=WIDE)


class Plan:
    def __init__(self, dp, fsdp, share, tokens):
        self.count = dp * fsdp
        self.share = share
        self.rows = -(-(2 * (LANES - 1) + share) // LANES)
        self.rows = -(-self.rows // 16) * 16
        self.start = [e * share // LANES for e in range(self.count)]
        self.tokens = tokens
        self.part = tokens // 2
        self.reach = (IMG - 2 + tokens) // tokens
        self.window = 2 * self.reach + 1
        self.grouped = dp == 4 and fsdp == 8 and self.reach <= 6
        if self.grouped:
            self.stages = [[2, 4, 6], [16, 1, 17], [8]]
        else:
            bits = [1 << k for k in range(self.count.bit_length() - 1)]
            bits = [b for b in bits if b != fsdp] + [fsdp]
            self.stages = [[b] for b in bits]
        masks = [0]
        for stage in self.stages:
            masks = masks + [m ^ s for s in stage for m in masks]
        self.bits = [masks[1 << k] for k in range(self.count.bit_length() - 1)]
        self.first_late = next(e for e in range(self.count) if self.start[e] >= AT["out"])
        self.flat_rows = -(-(self.start[-1] + self.rows) // 8) * 8

    def send(self, x, mask):
        return lax.ppermute(x, BOTH, [(i, i ^ mask) for i in range(self.count)])

    def spread(self, own, extra):
        buf = own[None]
        for level, stage in enumerate(self.stages[:-1]):
            parts = [buf]
            for m in stage:
                parts.append(self.send(buf, m))
            buf = jnp.concatenate(parts, axis=0)
            if level == 0:
                buf, extra = lax.optimization_barrier((buf, extra))
        core = self.send(buf, self.stages[-1][0])
        return buf, core, extra

    def reduce_parts(self, keep, away):
        parts = [keep, self.send(away, self.stages[-1][0])]
        for stage in reversed(self.stages[:-1]):
            total = parts[0].astype(WIDE)
            for part in parts[1:]:
                total = total + part.astype(WIDE)
            buf = total.astype(LOW)
            split = buf.reshape((len(stage) + 1, -1) + buf.shape[1:])
            parts = [split[0]] + [self.send(split[k + 1], m) for k, m in enumerate(stage)]
        return [part[0] for part in parts]

    def exchange(self, block):
        own = block[None]
        if self.grouped:
            hops = []
            for m in (1, 2, 3, 4, 6):
                hops.append(self.send(own, m))
            one, two, three, four, six = hops
            pair = jnp.concatenate([four, six], axis=0)
            quad = jnp.concatenate([two, three, four, six], axis=0)
            row = jnp.concatenate([own, one, quad], axis=0)
            pair, quad, row = lax.optimization_barrier((pair, quad, row))
            across = [(8 + j, 16 + j) for j in range(8)] + [(16 + j, 8 + j) for j in range(8)]
            skew = [(a, b ^ 1) for a, b in across]
            far = lax.ppermute(quad, BOTH, across)
            far_beside = lax.ppermute(pair, BOTH, skew)
            beside = self.send(pair, 1)
            home = self.send(row, 8)
            home_beside = self.send(beside, 8)
            return [row, beside, home, home_beside, far, far_beside]
        slots = []
        for slot in range(self.window):
            by = self.reach - slot
            pairs = [(i, i + by) for i in range(self.count) if 0 <= i + by < self.count]
            slots.append(own if by == 0 else lax.ppermute(own, BOTH, pairs))
        return [jnp.concatenate(slots, axis=0)]

    def table(self, device, spans, key_ids):
        e = jnp.arange(self.count, dtype=jnp.int32)
        rel = e ^ device
        where = jnp.zeros_like(e)
        for k, bit in enumerate(self.bits):
            where = where + jnp.where((rel & bit) != 0, 1 << k, 0)
        slot = jnp.arange(self.window, dtype=jnp.int32)
        if self.grouped:
            other = device - self.reach + slot
            mask = (other ^ device) & 7
            pos = jnp.where(mask == 6, 5, jnp.where(mask == 5, 6, mask))
            cross = (other >> 3) ^ (device >> 3)
            late = pos >= 6
            source = jnp.where(cross == 0, 0, jnp.where(cross == 1, 2, 4)) + jnp.where(late, 1, 0)
            index = jnp.where(late, pos - 6, jnp.where(source == 4, pos - 2, pos))
        else:
            source = jnp.zeros_like(slot)
            index = slot
        bounds = lax.dynamic_index_in_dim(spans, device, 0, keepdims=False)
        ends = jnp.clip(bounds - device + self.reach, 0, self.window - 1)
        own = key_ids[self.reach]
        low, high = own[:: self.part], own[self.part - 1 :: self.part]
        seen = (key_ids[:, -1][None] >= low[:, None]) & (key_ids[:, 0][None] <= high[:, None])
        seen = seen & (slot >= ends[0])[None] & (slot <= ends[1])[None]
        begin = jnp.min(jnp.where(seen, slot[None], self.window), axis=1)
        finish = jnp.max(jnp.where(seen, slot[None], -1), axis=1)
        return jnp.concatenate([where, source, index, ends, begin, finish]).astype(jnp.int32)

    def source_at(self, slot):
        return self.count + slot

    def index_at(self, slot):
        return self.count + self.window + slot

    def low_at(self):
        return self.count + 2 * self.window

    def range_at(self, quarter):
        at = self.count + 2 * self.window + 2 + quarter
        return at, at + self.tokens // self.part


def fetch_window(plan, table, sources, dest, sems, lo, hi, wait):
    def step(slot, carry):
        for k, source in enumerate(sources):

            @pl.when(table[plan.source_at(slot)] == k)
            def _(source=source):
                copy = pltpu.make_async_copy(
                    source.at[table[plan.index_at(slot)]], dest.at[slot], sems.at[slot]
                )
                if wait:
                    copy.wait()
                else:
                    copy.start()

        return carry

    lax.fori_loop(lo, hi + 1, step, 0)


def normalized(x):
    center = x - jnp.mean(x, axis=-1, keepdims=True)
    spread = jnp.mean(center * center, axis=-1, keepdims=True)
    r = lax.rsqrt(spread + LN_EPS)
    return center * r, r


def norm_back(grad, gain, n, r):
    g = grad * gain
    inner = jnp.mean(g, axis=-1, keepdims=True)
    outer = jnp.mean(g * n, axis=-1, keepdims=True)
    return r * (g - inner - n * outer)


def vector(ref, row, width):
    return jnp.concatenate([ref[row + j : row + j + 1, :] for j in range(width // LANES)], axis=1)


def put_vector(ref, row, value):
    for j in range(value.shape[1] // LANES):
        ref[row + j : row + j + 1, :] = value[:, LANES * j : LANES * (j + 1)]


def stacked(x):
    left = lax.broadcasted_iota(jnp.int32, x.shape, 1) < HEAD_DIM
    return jnp.concatenate([jnp.where(left, x, 0), jnp.where(left, 0, x)], axis=0)


def unstacked(x):
    half = x.shape[0] // 2
    left = lax.broadcasted_iota(jnp.int32, (half, LANES), 1) < HEAD_DIM
    return jnp.where(left, x[:half], x[half:])


def halves(x):
    part = x.shape[0] // 2
    return jnp.concatenate([stacked(x[:part]), stacked(x[part:])], axis=0)


def whole(x):
    part = x.shape[0] // 2
    return jnp.concatenate([unstacked(x[:part]), unstacked(x[part:])], axis=0)


def tiled(ids, width):
    part = ids.shape[0] // 2
    ids = jnp.concatenate([ids] * (width // LANES), axis=1)
    return jnp.concatenate([ids[:part], ids[:part], ids[part:], ids[part:]], axis=0)


def sweep(plan, table, body):
    (a, b), (c, d) = plan.range_at(0), plan.range_at(1)
    rows = 2 * plan.part

    def loop(begin, finish, rows):
        def step(w, carry):
            body(w, rows)
            return carry

        lax.fori_loop(begin, finish, step, 0)

    loop(table[a], table[c], slice(0, rows))
    loop(table[c], table[b] + 1, slice(0, 2 * rows))
    loop(table[b] + 1, table[d] + 1, slice(rows, 2 * rows))


def block_copies(source, dest, sems, lo, hi, wait):
    def step(slot, carry):
        copy = pltpu.make_async_copy(source.at[slot], dest.at[slot], sems.at[slot])
        copy.wait() if wait else copy.start()
        return carry

    lax.fori_loop(lo, hi + 1, step, 0)


def scaled_query(low, weight, bias):
    q = dot(low, weight, NN) + bias
    return (q.astype(LOW).astype(WIDE) * SCALE).astype(LOW)


def column_sum(x):
    return jnp.sum(x, axis=0, keepdims=True)


def shift_kernel(plan):
    def kernel(table, x_ref, out_ref, pad):
        s = table[0]
        x = x_ref[...]
        y = pltpu.roll(x, s, 1)
        pad[0:8, :] = jnp.zeros((8, LANES), WIDE)
        pad[8:, :] = y
        lane = lax.broadcasted_iota(jnp.int32, y.shape, 1)
        out_ref[...] = jnp.where(lane >= s, y, pad[7 : 7 + plan.rows, :]).astype(LOW)

    return kernel


def unshift_kernel(plan):
    def kernel(table, *refs):
        parts, (out_ref, sq_ref, pad) = refs[:-3], refs[-3:]
        s = table[0]
        got = [p[...].astype(WIDE) for p in parts]
        while len(got) > 1:
            got = [got[k] + got[k + 1] for k in range(0, len(got), 2)]
        y = pltpu.roll(got[0], LANES - s, 1)
        pad[0 : plan.rows, :] = y
        pad[plan.rows :, :] = jnp.zeros((8, LANES), WIDE)
        lane = lax.broadcasted_iota(jnp.int32, y.shape, 1)
        row = lax.broadcasted_iota(jnp.int32, y.shape, 0)
        out = jnp.where(lane < LANES - s, y, pad[1 : 1 + plan.rows, :])
        out = jnp.where(row * LANES + lane < plan.share, out, 0.0)
        out_ref[...] = out
        sq = jnp.sum(jnp.sum(out * out, axis=0, keepdims=True), axis=1, keepdims=True)
        sq_ref[...] = jnp.broadcast_to(sq, (plan.count, LANES))

    return kernel


VEC = {"gain1": 0, "shift1": 1, "tbias": 2, "obias": 3, "scale1": 4, "gain2": 5, "shift2": 6}
VEC.update({"ubias": 7, "dbias": 8, "scale2": 9})


def unpack_kernel(plan):
    half = plan.count // 2

    def kernel(table, near, core, triple_ref, wo, wup, wdn, vec_ref, wbuf, flat, wsem):
        def weight_copy(e, wait):
            t = table[e]

            @pl.when(t < half)
            def _():
                c = pltpu.make_async_copy(near.at[t], wbuf.at[e], wsem.at[e])
                c.wait() if wait else c.start()

            @pl.when(t >= half)
            def _():
                c = pltpu.make_async_copy(core.at[t - half], wbuf.at[e], wsem.at[e])
                c.wait() if wait else c.start()

        def start_one(e, carry):
            weight_copy(e, False)
            return carry

        def wait_one(e, carry):
            weight_copy(e, True)
            return carry

        lax.fori_loop(0, plan.count, start_one, 0)
        lax.fori_loop(0, plan.count, wait_one, 0)
        for e in range(plan.count):
            r0 = plan.start[e]
            block = wbuf[e].astype(WIDE)
            if e:
                before = flat[r0 : r0 + 1, :]
                flat[r0 : r0 + plan.rows, :] = block
                flat[r0 : r0 + 1, :] = before + block[0:1, :]
            else:
                flat[r0 : r0 + plan.rows, :] = block

        def unfold(dest, name, height, width):
            wide = width // LANES
            step = min(height, 384)
            for j in range(wide):
                for i in range(0, height, step):
                    dest[i : i + step, LANES * j : LANES * (j + 1)] = flat[
                        pl.ds(AT[name] + i * wide + j, step, stride=wide), :
                    ].astype(LOW)

        unfold(triple_ref, "triple", D, 3 * D)
        unfold(wo, "out", D, D)
        unfold(wup, "up", D, FF)
        unfold(wdn, "down", FF, D)
        vec_ref[...] = jnp.zeros(vec_ref.shape, WIDE)
        for name, row in VEC.items():
            width = dict(PIECES)[name]
            vec_ref[row : row + 1, :width] = vector(flat, AT[name], width)

    return kernel


def forward_kernel(plan, sources):
    T = plan.tokens
    own = plan.reach
    part = plan.part
    pairs = HEADS // 2

    def kernel(table, *refs):
        wins = refs[:sources]
        triple_ref, wo, wup, wdn, par_ref, cot_ref, col_ref, row_ref = refs[sources : 8 + sources]
        (
            out_ref,
            msg_ref,
            q_ref,
            k_ref,
            v_ref,
            norm_ref,
            normed_ref,
            mid_ref,
            act_ref,
            pre_ref,
            gbt_ref,
            n2_ref,
            att_ref,
            gbo_ref,
            vec_ref,
            stat_ref,
            kown_ref,
            vown_ref,
        ) = refs[8 + sources : 26 + sources]
        xwin, n_buf, k_buf, v_buf, scores, tops, sums, accs, mix, xsem, ksem = refs[26 + sources :]
        lo = table[plan.low_at()]
        hi = table[plan.low_at() + 1]

        def param(name):
            row = VEC[name]
            return par_ref[row : row + 1, : dict(PIECES)[name]]

        fetch_window(plan, table, wins, xwin, xsem, lo, hi, False)
        gain1 = param("gain1")
        shift1 = param("shift1")
        tbias = param("tbias")
        fetch_window(plan, table, wins, xwin, xsem, lo, hi, True)

        saved = [(n_buf, norm_ref), (k_buf, k_ref), (v_buf, v_ref)]

        def project(w, carry):
            n, _ = normalized(xwin[w].astype(WIDE))
            low = (n * gain1 + shift1).astype(LOW)
            n_buf[w] = low
            kv = dot(low, triple_ref[:, D:], NN)
            k_buf[w] = kv[:, :D].astype(LOW)
            v_buf[w] = (kv[:, D:] + tbias[:, D:]).astype(LOW)
            for i, (buf, ref) in enumerate(saved):
                pltpu.make_async_copy(buf.at[w], ref.at[w], ksem.at[i, w]).start()
            return carry

        lax.fori_loop(lo, hi + 1, project, 0)
        kown_ref[...] = k_buf[own]
        vown_ref[...] = v_buf[own]
        low = n_buf[own]
        normed_ref[...] = low
        q_ref[...] = scaled_query(low, triple_ref[:, :D], tbias[:, :D])

        lane = lax.broadcasted_iota(jnp.int32, (T, LANES), 1)
        qs = [halves(q_ref[:, LANES * p : LANES * (p + 1)]) for p in range(pairs)]
        ids = tiled(col_ref[...], T)
        for p in range(pairs):
            tops[p] = jnp.full((2 * T, LANES), MASKED, WIDE)
            sums[p] = jnp.zeros((2 * T, LANES), WIDE)
            accs[p] = jnp.zeros((2 * T, LANES), WIDE)

        def first(w, rows):
            seen = ids[rows] == row_ref[pl.ds(w, 1), :]
            for p in range(pairs):
                s = dot(qs[p][rows], k_buf[w, :, LANES * p : LANES * (p + 1)], NT)
                s = jnp.where(seen, s, MASKED)
                scores[p, w, rows, :] = s
                top = tops[p, rows, :]
                for j in range(0, T, LANES):
                    top = jnp.maximum(top, s[:, j : j + LANES])
                tops[p, rows, :] = top

        sweep(plan, table, first)
        for p in range(pairs):
            top = jnp.max(tops[p], axis=1, keepdims=True)
            tops[p] = jnp.broadcast_to(top, (2 * T, LANES))

        def second(w, rows):
            for p in range(pairs):
                top = jnp.concatenate([tops[p, rows, :]] * (T // LANES), axis=1)
                e = jnp.exp(scores[p, w, rows, :] - top)
                total = sums[p, rows, :]
                for j in range(0, T, LANES):
                    total = total + e[:, j : j + LANES]
                sums[p, rows, :] = total
                value = v_buf[w, :, LANES * p : LANES * (p + 1)]
                accs[p, rows, :] = accs[p, rows, :] + dot(e.astype(LOW), value, NN)

        sweep(plan, table, second)
        stats = jnp.zeros((T, LANES), WIDE)
        for p in range(pairs):
            total = jnp.sum(sums[p], axis=1, keepdims=True)
            mix[:, LANES * p : LANES * (p + 1)] = whole(accs[p] / total)
            log = tops[p] + jnp.log(total)
            for k in range(2):
                at = part * k
                column = jnp.concatenate(
                    [log[at : at + part], log[2 * part + at : 3 * part + at]], axis=0
                )
                stats = jnp.where(lane == 2 * p + k, column, stats)
        att = mix[...]
        att_low = att.astype(LOW)
        att_ref[...] = att_low
        x = xwin[own].astype(WIDE)
        scale1 = param("scale1")
        scale2 = param("scale2")
        gain2 = param("gain2")
        branch_one = dot(att_low, wo[...], NN) + param("obias")
        middle = x + scale1 * branch_one
        n2, r2 = normalized(middle)
        n2_low = (n2 * gain2 + param("shift2")).astype(LOW)
        n2_ref[...] = n2_low
        pre = dot(n2_low, wup[...], NN) + param("ubias")
        cdf = 0.5 * (1.0 + lax.erf(pre * math.sqrt(0.5)))
        act_low = (pre * cdf).astype(LOW)
        act_ref[...] = act_low
        slope = cdf + pre * (jnp.exp(-0.5 * pre * pre) * (1.0 / math.sqrt(2.0 * math.pi)))
        branch_two = dot(act_low, wdn[...], NN) + param("dbias")
        out_ref[...] = (middle + scale2 * branch_two).astype(LOW)

        up = cot_ref[...].astype(WIDE)
        gbt = (scale2 * up).astype(LOW)
        gbt_ref[...] = gbt
        gpre = (dot(gbt, wdn[...], NT) * slope).astype(LOW)
        pre_ref[...] = gpre
        gn2 = dot(gpre, wup[...], NT)
        gmid = up + norm_back(gn2, gain2, n2, r2)
        mid_ref[...] = gmid
        gbo = (scale1 * gmid).astype(LOW)
        gbo_ref[...] = gbo
        gatt = dot(gbo, wo[...], NT).astype(LOW)
        msg_ref[0:T, :] = gatt
        inner = gatt.astype(WIDE) * att
        left = lane < HEAD_DIM
        for p in range(HEADS // 2):
            piece = inner[:, LANES * p : LANES * (p + 1)]
            one = jnp.sum(jnp.where(left, piece, 0.0), axis=1, keepdims=True)
            two = jnp.sum(jnp.where(left, 0.0, piece), axis=1, keepdims=True)
            stats = jnp.where(lane == HEADS + 2 * p, one, stats)
            stats = jnp.where(lane == HEADS + 2 * p + 1, two, stats)
        stat_ref[...] = stats
        high = stats.astype(LOW).astype(WIDE)
        rest = pltpu.roll(stats - high, 2 * HEADS, 1)
        flipped = jnp.transpose(jnp.where(lane < 2 * HEADS, high, rest))
        tail = flipped[16:24, :]
        msg_ref[T : T + 16, 0:T] = flipped[0:16, :].astype(LOW)
        msg_ref[T : T + 16, T:] = jnp.concatenate(
            [tail[:, :LANES], tail[:, LANES:]], axis=0
        ).astype(LOW)

        vec_ref[...] = jnp.zeros(vec_ref.shape, WIDE)
        vec_ref[0:1, :D] = column_sum(up * branch_two)
        vec_ref[1:2, :D] = column_sum(gbt.astype(WIDE))
        vec_ref[2:3, :] = column_sum(gpre.astype(WIDE))
        vec_ref[3:4, :D] = column_sum(gn2 * n2)
        vec_ref[4:5, :D] = column_sum(gn2)
        vec_ref[5:6, :D] = column_sum(gmid * branch_one)
        vec_ref[6:7, :D] = column_sum(gbo.astype(WIDE))
        for i, (buf, ref) in enumerate(saved):
            block_copies(buf, ref, ksem.at[i], lo, hi, True)

    return kernel


def fold(dest, row, left, right, width):
    wide = width // LANES
    height = left.shape[1]
    for i in range(0, height, 384):
        part = dot(left[:, i : i + 384], right[...], TN)
        for j in range(wide):
            dest[pl.ds(row + i * wide + j, 384, stride=wide), :] = part[
                :, LANES * j : LANES * (j + 1)
            ]


def query_kernel(plan):
    T = plan.tokens
    part = plan.part
    pairs = HEADS // 2

    def kernel(
        table,
        q_ref,
        k_ref,
        v_ref,
        msg_ref,
        stat_ref,
        col_ref,
        row_ref,
        gq_ref,
        logs,
        dots,
        accs,
        k_buf,
        v_buf,
        ksem,
        vsem,
    ):
        lo = table[plan.low_at()]
        hi = table[plan.low_at() + 1]
        block_copies(k_ref, k_buf, ksem, lo, hi, False)
        block_copies(v_ref, v_buf, vsem, lo, hi, False)
        qs = [halves(q_ref[:, LANES * p : LANES * (p + 1)]) for p in range(pairs)]
        gs = [halves(msg_ref[0:T, LANES * p : LANES * (p + 1)]) for p in range(pairs)]
        ids = tiled(col_ref[...], T)
        for p in range(pairs):
            for k in range(2):
                for c in range(2):
                    rows = slice(part * c, part * (c + 1))
                    to = slice(part * (2 * c + k), part * (2 * c + k + 1))
                    h = 2 * p + k
                    logs[p, to, :] = jnp.broadcast_to(stat_ref[rows, h : h + 1], (part, LANES))
                    h = h + HEADS
                    dots[p, to, :] = jnp.broadcast_to(stat_ref[rows, h : h + 1], (part, LANES))
            accs[p] = jnp.zeros((2 * T, LANES), WIDE)
        block_copies(k_ref, k_buf, ksem, lo, hi, True)
        block_copies(v_ref, v_buf, vsem, lo, hi, True)

        def step(w, rows):
            seen = ids[rows] == row_ref[pl.ds(w, 1), :]
            for p in range(pairs):
                cols = slice(LANES * p, LANES * (p + 1))
                key = k_buf[w, :, cols]
                s = jnp.where(seen, dot(qs[p][rows], key, NT), MASKED)
                prob = jnp.exp(s - jnp.concatenate([logs[p, rows, :]] * (T // LANES), axis=1))
                inner = jnp.concatenate([dots[p, rows, :]] * (T // LANES), axis=1)
                grad = prob * (dot(gs[p][rows], v_buf[w, :, cols], NT) - inner)
                accs[p, rows, :] = accs[p, rows, :] + dot(grad.astype(LOW), key, NN)

        sweep(plan, table, step)
        for p in range(pairs):
            gq_ref[:, LANES * p : LANES * (p + 1)] = (whole(accs[p]) * SCALE).astype(LOW)

    return kernel


def weight_kernel(plan):
    base = AT["out"]
    half = plan.count // 2

    def kernel(
        table,
        norm_ref,
        triple_ref,
        par_ref,
        act_ref,
        pre_ref,
        gbt_ref,
        n2_ref,
        att_ref,
        gbo_ref,
        vec_ref,
        q_ref,
        keep_ref,
        away_ref,
        tail_ref,
        flat,
    ):
        fold(flat, AT["down"] - base, act_ref, gbt_ref, D)
        fold(flat, AT["up"] - base, n2_ref, pre_ref, FF)
        fold(flat, AT["out"] - base, att_ref, gbo_ref, D)
        put_vector(flat, AT["scale2"] - base, vec_ref[0:1, :D])
        put_vector(flat, AT["dbias"] - base, vec_ref[1:2, :D])
        put_vector(flat, AT["ubias"] - base, vec_ref[2:3, :])
        put_vector(flat, AT["gain2"] - base, vec_ref[3:4, :D])
        put_vector(flat, AT["shift2"] - base, vec_ref[4:5, :D])
        put_vector(flat, AT["scale1"] - base, vec_ref[5:6, :D])
        put_vector(flat, AT["obias"] - base, vec_ref[6:7, :D])
        end = ALL_ROWS - base
        flat[end:, :] = jnp.zeros((flat.shape[0] - end, LANES), WIDE)
        tail_ref[...] = flat[0 : plan.rows, :]
        for e in range(plan.first_late, plan.count):
            r0 = plan.start[e] - base
            t = table[e]

            @pl.when(t < half)
            def _(r0=r0, t=t):
                keep_ref[t] = flat[r0 : r0 + plan.rows, :].astype(LOW)

            @pl.when(t >= half)
            def _(r0=r0, t=t):
                away_ref[t - half] = flat[r0 : r0 + plan.rows, :].astype(LOW)

        bias = par_ref[VEC["tbias"] : VEC["tbias"] + 1, :D]

        def project(w, carry):
            q_ref[w] = scaled_query(norm_ref[w], triple_ref[:, :D], bias)
            return carry

        lax.fori_loop(table[plan.low_at()], table[plan.low_at() + 1] + 1, project, 0)

    return kernel


def last_kernel(plan, sources):
    T = plan.tokens
    early = plan.first_late
    half = plan.count // 2
    part = plan.part
    pairs = HEADS // 2

    def kernel(table, *refs):
        wins = refs[:sources]
        (
            q_ref,
            k_ref,
            v_ref,
            col_ref,
            row_ref,
            gq_ref,
            normed_ref,
            triple_ref,
            x_ref,
            mid_ref,
            par_ref,
            tail_ref,
            _,
            _,
            grad_ref,
            keep_ref,
            away_ref,
        ) = refs[sources : sources + 17]
        mwin, q_buf, flat, gt, stage, stats, spare, acck, accv, msem, qsem, osem = refs[
            sources + 17 :
        ]
        lo = table[plan.low_at()]
        hi = table[plan.low_at() + 1]
        fetch_window(plan, table, wins, mwin, msem, lo, hi, False)
        block_copies(q_ref, q_buf, qsem, lo, hi, False)
        ks = [halves(k_ref[:, LANES * p : LANES * (p + 1)]) for p in range(pairs)]
        vs = [halves(v_ref[:, LANES * p : LANES * (p + 1)]) for p in range(pairs)]
        ids = tiled(col_ref[...], T)
        for p in range(pairs):
            acck[p] = jnp.zeros((2 * T, LANES), WIDE)
            accv[p] = jnp.zeros((2 * T, LANES), WIDE)
        fetch_window(plan, table, wins, mwin, msem, lo, hi, True)
        block_copies(q_ref, q_buf, qsem, lo, hi, True)

        def unpack(w, carry):
            got = mwin[w, T : T + 16, :].astype(WIDE)
            spare[0:16, :] = got[:, :T]
            spare[16:24, :] = jnp.concatenate([got[:8, T:], got[8:, T:]], axis=1)
            stats[w, 0 : 2 * HEADS, :] = spare[0 : 2 * HEADS, :] + spare[2 * HEADS : 4 * HEADS, :]
            return carry

        lax.fori_loop(lo, hi + 1, unpack, 0)

        def step(w, rows):
            seen = ids[rows] == row_ref[pl.ds(w, 1), :]
            copies = (rows.stop - rows.start) // (2 * part)

            def pair_rows(h):
                two = [jnp.broadcast_to(stats[w, h + k : h + k + 1, :], (part, T)) for k in range(2)]
                return jnp.concatenate(two * copies, axis=0)

            for p in range(pairs):
                cols = slice(LANES * p, LANES * (p + 1))
                q = q_buf[w, :, cols]
                g = mwin[w, 0:T, cols]
                s = jnp.where(seen, dot(ks[p][rows], q, NT), MASKED)
                prob = jnp.exp(s - pair_rows(2 * p))
                grad = prob * (dot(vs[p][rows], g, NT) - pair_rows(HEADS + 2 * p))
                acck[p, rows, :] = acck[p, rows, :] + dot(grad.astype(LOW), q, NN)
                accv[p, rows, :] = accv[p, rows, :] + dot(prob.astype(LOW), g, NN)

        sweep(plan, table, step)
        for p in range(pairs):
            gt[:, D + LANES * p : D + LANES * (p + 1)] = whole(acck[p]).astype(LOW)
            gt[:, 2 * D + LANES * p : 2 * D + LANES * (p + 1)] = whole(accv[p]).astype(LOW)
        gt[:, :D] = gq_ref[...]
        fold(flat, AT["triple"], normed_ref, gt, 3 * D)
        put_vector(flat, AT["tbias"], column_sum(gt[:, :D].astype(WIDE)))
        put_vector(flat, AT["tbias"] + D // LANES, column_sum(gt[:, 2 * D :].astype(WIDE)))
        gn = dot(gt[...], triple_ref[...], NT)
        n, r = normalized(x_ref[...].astype(WIDE))
        put_vector(flat, AT["gain1"], column_sum(gn * n))
        put_vector(flat, AT["shift1"], column_sum(gn))
        flat[AT["out"] : AT["out"] + plan.rows, :] = tail_ref[...]

        def put(e, wait):
            t = table[e]

            @pl.when(t < half)
            def _():
                c = pltpu.make_async_copy(stage.at[e], keep_ref.at[t], osem.at[e])
                c.wait() if wait else c.start()

            @pl.when(t >= half)
            def _():
                c = pltpu.make_async_copy(stage.at[e], away_ref.at[t - half], osem.at[e])
                c.wait() if wait else c.start()

        for e in range(early):
            r0 = plan.start[e]
            stage[e] = flat[r0 : r0 + plan.rows, :].astype(LOW)
            put(e, False)
        gain1 = par_ref[VEC["gain1"] : VEC["gain1"] + 1, :D]
        grad_ref[...] = mid_ref[...] + norm_back(gn, gain1, n, r)
        for e in range(early):
            put(e, True)

    return kernel


def shape(dims, kind):
    return jax.ShapeDtypeStruct(dims, kind)


SMEM = pl.BlockSpec(memory_space=pltpu.SMEM)
VMEM = pl.BlockSpec(memory_space=pltpu.VMEM)
ANY = pl.BlockSpec(memory_space=pl.ANY)


def build(plan):
    T = plan.tokens
    W = plan.window
    R = plan.rows
    N = plan.count
    limit = pltpu.CompilerParams(vmem_limit_bytes=60 * 1024 * 1024)

    def per_device(inputs, cotangent, master, first_moment, second_moment, image_ids, spans):
        device = lax.axis_index(BOTH).astype(jnp.int32)
        shift = ((device * plan.share) % LANES).reshape(1).astype(jnp.int32)
        shifted = pl.pallas_call(
            shift_kernel(plan),
            in_specs=[SMEM, VMEM],
            out_specs=VMEM,
            out_shape=shape((R, LANES), LOW),
            scratch_shapes=[pltpu.VMEM((R + 8, LANES), WIDE)],
            name="shift",
        )(shift, jnp.pad(master, (0, R * LANES - plan.share)).reshape(R, LANES))
        near, core, (image_ids, spans) = plan.spread(shifted, (image_ids, spans))
        padded = jnp.pad(image_ids, (plan.reach * T, plan.reach * T), constant_values=-1)
        key_ids = lax.dynamic_slice_in_dim(padded, device * T, W * T, 0).reshape(W, T)
        table = plan.table(device, spans, key_ids)
        own_ids = key_ids[plan.reach]
        columns = jnp.broadcast_to(own_ids[:, None], (T, LANES))
        wins = plan.exchange(inputs)
        sources = len(wins)

        half = pltpu.VMEM((HEADS // 2, 2 * T, LANES), WIDE)
        unpack = pl.pallas_call(
            unpack_kernel(plan),
            in_specs=[SMEM, ANY, ANY],
            out_specs=[VMEM] * 5,
            out_shape=[
                shape((D, 3 * D), LOW),
                shape((D, D), LOW),
                shape((D, FF), LOW),
                shape((FF, D), LOW),
                shape((16, FF), WIDE),
            ],
            scratch_shapes=[
                pltpu.VMEM((N, R, LANES), LOW),
                pltpu.VMEM((plan.flat_rows, LANES), WIDE),
                pltpu.SemaphoreType.DMA((N,)),
            ],
            compiler_params=limit,
            name="unpack",
        )
        triple, wo, wup, wdn, params = unpack(table, near, core)

        outs = pl.pallas_call(
            forward_kernel(plan, sources),
            in_specs=[SMEM] + [ANY] * sources + [VMEM] * 8,
            out_specs=[VMEM] * 3 + [ANY] * 3 + [VMEM] * 12,
            out_shape=[
                shape((T, D), LOW),
                shape((T + 16, D), LOW),
                shape((T, D), LOW),
                shape((W, T, D), LOW),
                shape((W, T, D), LOW),
                shape((W, T, D), LOW),
                shape((T, D), LOW),
                shape((T, D), WIDE),
                shape((T, FF), LOW),
                shape((T, FF), LOW),
                shape((T, D), LOW),
                shape((T, D), LOW),
                shape((T, D), LOW),
                shape((T, D), LOW),
                shape((8, FF), WIDE),
                shape((T, LANES), WIDE),
                shape((T, D), LOW),
                shape((T, D), LOW),
            ],
            scratch_shapes=[
                pltpu.VMEM((W, T, D), LOW),
                pltpu.VMEM((W, T, D), LOW),
                pltpu.VMEM((W, T, D), LOW),
                pltpu.VMEM((W, T, D), LOW),
                pltpu.VMEM((HEADS // 2, W, 2 * T, T), WIDE),
                half,
                half,
                half,
                pltpu.VMEM((T, D), WIDE),
                pltpu.SemaphoreType.DMA((W,)),
                pltpu.SemaphoreType.DMA((3, W)),
            ],
            compiler_params=limit,
            name="forward",
        )(table, *wins, triple, wo, wup, wdn, params, cotangent, columns, key_ids)
        (
            result,
            message,
            q,
            k,
            v,
            norms,
            normed,
            gmid,
            act,
            gpre,
            gbt,
            n2,
            att,
            gbo,
            vec,
            stat,
            k_own,
            v_own,
        ) = outs
        messages = plan.exchange(message)

        query_call = pl.pallas_call(
            query_kernel(plan),
            in_specs=[SMEM, VMEM, ANY, ANY] + [VMEM] * 4,
            out_specs=VMEM,
            out_shape=shape((T, D), LOW),
            scratch_shapes=[
                half,
                half,
                half,
                pltpu.VMEM((W, T, D), LOW),
                pltpu.VMEM((W, T, D), LOW),
                pltpu.SemaphoreType.DMA((W,)),
                pltpu.SemaphoreType.DMA((W,)),
            ],
            compiler_params=limit,
            name="query",
        )
        gq = query_call(table, q, k, v, message, stat, columns, key_ids)
        weight_call = pl.pallas_call(
            weight_kernel(plan),
            in_specs=[SMEM] + [VMEM] * 10,
            out_specs=[VMEM] * 4,
            out_shape=[
                shape((W, T, D), LOW),
                shape((N // 2, R, LANES), LOW),
                shape((N // 2, R, LANES), LOW),
                shape((R, LANES), WIDE),
            ],
            scratch_shapes=[
                pltpu.VMEM((plan.flat_rows - AT["out"] + 8, LANES), WIDE),
            ],
            compiler_params=limit,
            name="weight",
        )
        queries, keep, away, tail = weight_call(
            table, norms, triple, params, act, gpre, gbt, n2, att, gbo, vec
        )

        late = plan.first_late
        input_grad, keep, away = pl.pallas_call(
            last_kernel(plan, sources),
            in_specs=[SMEM] + [ANY] * (sources + 1) + [VMEM] * 11 + [ANY, ANY],
            out_specs=[VMEM, ANY, ANY],
            out_shape=[
                shape((T, D), WIDE),
                shape((N // 2, R, LANES), LOW),
                shape((N // 2, R, LANES), LOW),
            ],
            scratch_shapes=[
                pltpu.VMEM((W, T + 16, D), LOW),
                pltpu.VMEM((W, T, D), LOW),
                pltpu.VMEM((AT["out"] + R + 8, LANES), WIDE),
                pltpu.VMEM((T, 3 * D), LOW),
                pltpu.VMEM((late, R, LANES), LOW),
                pltpu.VMEM((W, 16, T), WIDE),
                pltpu.VMEM((24, T), WIDE),
                half,
                half,
                pltpu.SemaphoreType.DMA((W,)),
                pltpu.SemaphoreType.DMA((W,)),
                pltpu.SemaphoreType.DMA((late,)),
            ],
            input_output_aliases={13 + sources: 1, 14 + sources: 2},
            compiler_params=limit,
            name="last",
        )(
            table,
            *messages,
            queries,
            k_own,
            v_own,
            columns,
            key_ids,
            gq,
            normed,
            triple,
            inputs,
            gmid,
            params,
            tail,
            keep,
            away,
        )

        parts = plan.reduce_parts(keep, away)
        grad, square = pl.pallas_call(
            unshift_kernel(plan),
            in_specs=[SMEM] + [VMEM] * len(parts),
            out_specs=[VMEM, VMEM],
            out_shape=[shape((R, LANES), WIDE), shape((N, LANES), WIDE)],
            scratch_shapes=[pltpu.VMEM((R + 8, LANES), WIDE)],
            name="unshift",
        )(shift, *parts)
        grad_shard = grad.reshape(-1)[: plan.share]
        squares = lax.all_to_all(square, BOTH, 0, 0, tiled=True)
        grad_norm = jnp.sqrt(jnp.sum(squares[:, 0]))
        ceiling = CLIP_RATIO * math.sqrt(plan.share * N)
        factor = ceiling / jnp.maximum(grad_norm, ceiling)
        clipped = grad_shard * factor
        new_first = BETA_ONE * first_moment + (1.0 - BETA_ONE) * clipped
        new_second = BETA_TWO * second_moment + (1.0 - BETA_TWO) * clipped * clipped
        new_master = master - LEARN_RATE * (
            new_first / (jnp.sqrt(new_second) + ADAM_EPS) + WEIGHT_DECAY * master
        )
        return (
            result,
            input_grad,
            grad_shard,
            grad_norm.reshape(1),
            new_first,
            new_second,
            new_master,
        )

    return per_device


def solution(mesh):
    dp = mesh.shape["dp"]
    fsdp = mesh.shape["fsdp"]
    row = P(BOTH, None)
    flat = P(BOTH)
    in_specs = (row, row, flat, flat, flat, P(), P())
    out_specs = (row, row, flat, P(), flat, flat, flat)

    def per_device(*args):
        inputs, master = args[0], args[2]
        plan = Plan(dp, fsdp, master.shape[0], inputs.shape[0])
        return build(plan)(*args)

    return jax.shard_map(
        per_device, mesh=mesh, in_specs=in_specs, out_specs=out_specs, check_vma=False
    )
```

```python
import math

import jax
import jax.numpy as jnp
from jax import lax
from jax.experimental import pallas as pl
from jax.experimental.pallas import tpu as pltpu
from jax.sharding import PartitionSpec as P


D = 384
HEADS = 6
HEAD_DIM = 64
FF = 1536
IMG = 1370
LANES = 128

LN_EPS = 1e-06
BETA_ONE = 0.5
BETA_TWO = 0.6
LEARN_RATE = 0.01
WEIGHT_DECAY = 0.05
ADAM_EPS = 1e-08
CLIP_RATIO = 0.25
MASKED = -1e30
BOTH = ("dp", "fsdp")
LOW = jnp.bfloat16
WIDE = jnp.float32
SCALE = HEAD_DIM ** (-0.5)

NT = (((1,), (1,)), ((), ()))
NN = (((1,), (0,)), ((), ()))
TN = (((0,), (0,)), ((), ()))

PIECES = [
    ("gain1", D),
    ("shift1", D),
    ("triple", 3 * D * D),
    ("tbias", 2 * D),
    ("out", D * D),
    ("obias", D),
    ("scale1", D),
    ("gain2", D),
    ("shift2", D),
    ("up", D * FF),
    ("ubias", FF),
    ("down", FF * D),
    ("dbias", D),
    ("scale2", D),
]
AT = {}
_row = 0
for _name, _count in PIECES:
    AT[_name] = _row
    _row += _count // LANES
ALL_ROWS = _row


def dot(a, b, dims):
    return lax.dot_general(a, b, dims, preferred_element_type=WIDE)


class Plan:
    def __init__(self, dp, fsdp, share, tokens):
        self.count = dp * fsdp
        self.share = share
        self.rows = -(-(2 * (LANES - 1) + share) // LANES)
        self.rows = -(-self.rows // 16) * 16
        self.cut = self.rows * 3 // 64 * 16
        self.start = [e * share // LANES for e in range(self.count)]
        self.tokens = tokens
        self.part = tokens // 2
        self.reach = (IMG - 2 + tokens) // tokens
        self.window = 2 * self.reach + 1
        self.grouped = dp == 4 and fsdp == 8 and self.reach <= 6
        if self.grouped:
            self.stages = [[2, 4, 6], [16, 1, 17], [8]]
        else:
            bits = [1 << k for k in range(self.count.bit_length() - 1)]
            bits = [b for b in bits if b != fsdp] + [fsdp]
            self.stages = [[b] for b in bits]
        masks = [0]
        for stage in self.stages:
            masks = masks + [m ^ s for s in stage for m in masks]
        self.bits = [masks[1 << k] for k in range(self.count.bit_length() - 1)]
        self.first_late = next(e for e in range(self.count) if self.start[e] >= AT["out"])
        self.flat_rows = -(-(self.start[-1] + self.rows) // 8) * 8

    def send(self, x, mask):
        return lax.ppermute(x, BOTH, [(i, i ^ mask) for i in range(self.count)])

    def spread(self, own, extra):
        buf = own[None]
        for level, stage in enumerate(self.stages[:-1]):
            parts = [buf]
            for m in stage:
                parts.append(self.send(buf, m))
            buf = jnp.concatenate(parts, axis=0)
            if level == 0:
                buf, extra = lax.optimization_barrier((buf, extra))
        core = self.send(buf, self.stages[-1][0])
        return buf, core, extra

    def reduce_parts(self, keep, away):
        def added(parts):
            total = parts[0].astype(WIDE)
            for part in parts[1:]:
                total = total + part.astype(WIDE)
            return total.astype(LOW)

        def one(buf, axis, level):
            parts = [lax.index_in_dim(buf, 0, axis, keepdims=False)]
            for k, m in enumerate(self.stages[level]):
                parts.append(self.send(lax.index_in_dim(buf, k + 1, axis, keepdims=False), m))
            return parts

        buf = added([keep, self.send(away, self.stages[-1][0])])
        if self.grouped:
            buf = buf.reshape((len(self.stages[1]) + 1, len(self.stages[0]) + 1) + buf.shape[1:])
            lead, rest = buf[:, :, : self.cut], buf[:, :, self.cut :]
            lead = one(lead, 0, 1)
            rest = one(rest, 1, 0)
            return one(added(lead), 0, 0) + one(added(rest), 0, 1)
        for level in reversed(range(len(self.stages) - 1)):
            buf = buf.reshape((len(self.stages[level]) + 1, -1) + buf.shape[1:])
            parts = one(buf, 0, level)
            buf = added(parts)
        return [part[0] for part in parts]

    def exchange(self, block):
        own = block[None]
        if self.grouped:
            hops = []
            for m in (1, 2, 3, 4, 6):
                hops.append(self.send(own, m))
            one, two, three, four, six = hops
            pair = jnp.concatenate([four, six], axis=0)
            quad = jnp.concatenate([two, three, four, six], axis=0)
            row = jnp.concatenate([own, one, quad], axis=0)
            pair, quad, row = lax.optimization_barrier((pair, quad, row))
            across = [(8 + j, 16 + j) for j in range(8)] + [(16 + j, 8 + j) for j in range(8)]
            skew = [(a, b ^ 1) for a, b in across]
            far = lax.ppermute(quad, BOTH, across)
            far_beside = lax.ppermute(pair, BOTH, skew)
            beside = self.send(pair, 1)
            home = self.send(row, 8)
            home_beside = self.send(beside, 8)
            return [row, beside, home, home_beside, far, far_beside]
        slots = []
        for slot in range(self.window):
            by = self.reach - slot
            pairs = [(i, i + by) for i in range(self.count) if 0 <= i + by < self.count]
            slots.append(own if by == 0 else lax.ppermute(own, BOTH, pairs))
        return [jnp.concatenate(slots, axis=0)]

    def table(self, device, spans, key_ids):
        e = jnp.arange(self.count, dtype=jnp.int32)
        rel = e ^ device
        where = jnp.zeros_like(e)
        for k, bit in enumerate(self.bits):
            where = where + jnp.where((rel & bit) != 0, 1 << k, 0)
        slot = jnp.arange(self.window, dtype=jnp.int32)
        if self.grouped:
            other = device - self.reach + slot
            mask = (other ^ device) & 7
            pos = jnp.where(mask == 6, 5, jnp.where(mask == 5, 6, mask))
            cross = (other >> 3) ^ (device >> 3)
            late = pos >= 6
            source = jnp.where(cross == 0, 0, jnp.where(cross == 1, 2, 4)) + jnp.where(late, 1, 0)
            index = jnp.where(late, pos - 6, jnp.where(source == 4, pos - 2, pos))
        else:
            source = jnp.zeros_like(slot)
            index = slot
        bounds = lax.dynamic_index_in_dim(spans, device, 0, keepdims=False)
        ends = jnp.clip(bounds - device + self.reach, 0, self.window - 1)
        own = key_ids[self.reach]
        low, high = own[:: self.part], own[self.part - 1 :: self.part]
        seen = (key_ids[:, -1][None] >= low[:, None]) & (key_ids[:, 0][None] <= high[:, None])
        seen = seen & (slot >= ends[0])[None] & (slot <= ends[1])[None]
        begin = jnp.min(jnp.where(seen, slot[None], self.window), axis=1)
        finish = jnp.max(jnp.where(seen, slot[None], -1), axis=1)
        return jnp.concatenate([where, source, index, ends, begin, finish]).astype(jnp.int32)

    def source_at(self, slot):
        return self.count + slot

    def index_at(self, slot):
        return self.count + self.window + slot

    def low_at(self):
        return self.count + 2 * self.window

    def range_at(self, quarter):
        at = self.count + 2 * self.window + 2 + quarter
        return at, at + self.tokens // self.part


def fetch_window(plan, table, sources, dest, sems, lo, hi, wait):
    def step(slot, carry):
        for k, source in enumerate(sources):

            @pl.when(table[plan.source_at(slot)] == k)
            def _(source=source):
                copy = pltpu.make_async_copy(
                    source.at[table[plan.index_at(slot)]], dest.at[slot], sems.at[slot]
                )
                if wait:
                    copy.wait()
                else:
                    copy.start()

        return carry

    lax.fori_loop(lo, hi + 1, step, 0)


def normalized(x):
    center = x - jnp.mean(x, axis=-1, keepdims=True)
    spread = jnp.mean(center * center, axis=-1, keepdims=True)
    r = lax.rsqrt(spread + LN_EPS)
    return center * r, r


def norm_back(grad, gain, n, r):
    g = grad * gain
    inner = jnp.mean(g, axis=-1, keepdims=True)
    outer = jnp.mean(g * n, axis=-1, keepdims=True)
    return r * (g - inner - n * outer)


def vector(ref, row, width):
    return jnp.concatenate([ref[row + j : row + j + 1, :] for j in range(width // LANES)], axis=1)


def put_vector(ref, row, value):
    for j in range(value.shape[1] // LANES):
        ref[row + j : row + j + 1, :] = value[:, LANES * j : LANES * (j + 1)]


def stacked(x):
    left = lax.broadcasted_iota(jnp.int32, x.shape, 1) < HEAD_DIM
    return jnp.concatenate([jnp.where(left, x, 0), jnp.where(left, 0, x)], axis=0)


def unstacked(x):
    half = x.shape[0] // 2
    left = lax.broadcasted_iota(jnp.int32, (half, LANES), 1) < HEAD_DIM
    return jnp.where(left, x[:half], x[half:])


def halves(x):
    part = x.shape[0] // 2
    return jnp.concatenate([stacked(x[:part]), stacked(x[part:])], axis=0)


def whole(x):
    part = x.shape[0] // 2
    return jnp.concatenate([unstacked(x[:part]), unstacked(x[part:])], axis=0)


def tiled(ids, width):
    part = ids.shape[0] // 2
    ids = jnp.concatenate([ids] * (width // LANES), axis=1)
    return jnp.concatenate([ids[:part], ids[:part], ids[part:], ids[part:]], axis=0)


def sweep(plan, table, body):
    (a, b), (c, d) = plan.range_at(0), plan.range_at(1)
    rows = 2 * plan.part

    def loop(begin, finish, rows):
        def step(w, carry):
            body(w, rows)
            return carry

        lax.fori_loop(begin, finish, step, 0)

    loop(table[a], table[c], slice(0, rows))
    loop(table[c], table[b] + 1, slice(0, 2 * rows))
    loop(table[b] + 1, table[d] + 1, slice(rows, 2 * rows))


def launch(source, dest, sem):
    copy = pltpu.make_async_copy(source, dest, sem)
    copy.start()
    return copy


def block_copies(source, dest, sems, lo, hi, wait):
    def step(slot, carry):
        copy = pltpu.make_async_copy(source.at[slot], dest.at[slot], sems.at[slot])
        copy.wait() if wait else copy.start()
        return carry

    lax.fori_loop(lo, hi + 1, step, 0)


def scaled_query(low, weight, bias):
    q = dot(low, weight, NN) + bias
    return (q.astype(LOW).astype(WIDE) * SCALE).astype(LOW)


def column_sum(x):
    return jnp.sum(x, axis=0, keepdims=True)


def shift_kernel(plan):
    def kernel(table, x_ref, out_ref, pad):
        s = table[0]
        x = x_ref[...]
        y = pltpu.roll(x, s, 1)
        pad[0:8, :] = jnp.zeros((8, LANES), WIDE)
        pad[8:, :] = y
        lane = lax.broadcasted_iota(jnp.int32, y.shape, 1)
        out_ref[...] = jnp.where(lane >= s, y, pad[7 : 7 + plan.rows, :]).astype(LOW)

    return kernel


def unshift_kernel(plan):
    def kernel(table, *refs):
        parts, (out_ref, sq_ref, pad) = refs[:-3], refs[-3:]
        s = table[0]

        def total(parts):
            got = [p[...].astype(WIDE) for p in parts]
            while len(got) > 1:
                got = [got[k] + got[k + 1] for k in range(0, len(got), 2)]
            return got[0]

        if plan.grouped:
            lead = len(plan.stages[0]) + 1
            y = jnp.concatenate([total(parts[:lead]), total(parts[lead:])], axis=0)
        else:
            y = total(parts)
        y = pltpu.roll(y, LANES - s, 1)
        pad[0 : plan.rows, :] = y
        pad[plan.rows :, :] = jnp.zeros((8, LANES), WIDE)
        lane = lax.broadcasted_iota(jnp.int32, y.shape, 1)
        row = lax.broadcasted_iota(jnp.int32, y.shape, 0)
        out = jnp.where(lane < LANES - s, y, pad[1 : 1 + plan.rows, :])
        out = jnp.where(row * LANES + lane < plan.share, out, 0.0)
        out_ref[...] = out
        sq = jnp.sum(jnp.sum(out * out, axis=0, keepdims=True), axis=1, keepdims=True)
        sq_ref[...] = jnp.broadcast_to(sq, (plan.count, LANES))

    return kernel


VEC = {"gain1": 0, "shift1": 1, "tbias": 2, "obias": 3, "scale1": 4, "gain2": 5, "shift2": 6}
VEC.update({"ubias": 7, "dbias": 8, "scale2": 9})


def unpack_kernel(plan):
    half = plan.count // 2

    def kernel(table, near, core, triple_ref, wo, wup, wdn, vec_ref, wbuf, flat, wsem):
        def weight_copy(e, wait):
            t = table[e]

            @pl.when(t < half)
            def _():
                c = pltpu.make_async_copy(near.at[t], wbuf.at[e], wsem.at[e])
                c.wait() if wait else c.start()

            @pl.when(t >= half)
            def _():
                c = pltpu.make_async_copy(core.at[t - half], wbuf.at[e], wsem.at[e])
                c.wait() if wait else c.start()

        def start_one(e, carry):
            weight_copy(e, False)
            return carry

        def wait_one(e, carry):
            weight_copy(e, True)
            return carry

        lax.fori_loop(0, plan.count, start_one, 0)
        lax.fori_loop(0, plan.count, wait_one, 0)
        for e in range(plan.count):
            r0 = plan.start[e]
            block = wbuf[e].astype(WIDE)
            if e:
                before = flat[r0 : r0 + 1, :]
                flat[r0 : r0 + plan.rows, :] = block
                flat[r0 : r0 + 1, :] = before + block[0:1, :]
            else:
                flat[r0 : r0 + plan.rows, :] = block

        def unfold(dest, name, height, width):
            wide = width // LANES
            step = min(height, 384)
            for j in range(wide):
                for i in range(0, height, step):
                    dest[i : i + step, LANES * j : LANES * (j + 1)] = flat[
                        pl.ds(AT[name] + i * wide + j, step, stride=wide), :
                    ].astype(LOW)

        unfold(triple_ref, "triple", D, 3 * D)
        unfold(wo, "out", D, D)
        unfold(wup, "up", D, FF)
        unfold(wdn, "down", FF, D)
        vec_ref[...] = jnp.zeros(vec_ref.shape, WIDE)
        for name, row in VEC.items():
            width = dict(PIECES)[name]
            vec_ref[row : row + 1, :width] = vector(flat, AT[name], width)

    return kernel


def forward_kernel(plan, sources):
    T = plan.tokens
    own = plan.reach
    part = plan.part
    pairs = HEADS // 2

    def kernel(table, *refs):
        wins = refs[:sources]
        triple_ref, wo_ref, wup_ref, wdn_ref, par_ref, cot_ref, col_ref, row_ref = refs[
            sources : 8 + sources
        ]
        (
            out_ref,
            msg_ref,
            q_ref,
            k_ref,
            v_ref,
            norm_ref,
            normed_ref,
            mid_ref,
            act_ref,
            pre_ref,
            gbt_ref,
            n2_ref,
            att_ref,
            gbo_ref,
            vec_ref,
            stat_ref,
            kown_ref,
            vown_ref,
        ) = refs[8 + sources : 26 + sources]
        xwin, n_buf, k_buf, v_buf, scores, tops, sums, accs, mix = refs[26 + sources : 35 + sources]
        wo, wup, wdn, act_buf, pre_buf, xsem, ksem, osem = refs[35 + sources :]
        lo = table[plan.low_at()]
        hi = table[plan.low_at() + 1]

        def param(name):
            row = VEC[name]
            return par_ref[row : row + 1, : dict(PIECES)[name]]

        fetch_window(plan, table, wins, xwin, xsem, lo, hi, False)
        pairs_in = [(wo_ref, wo), (wup_ref, wup), (wdn_ref, wdn)]
        loads = [launch(a, b, osem.at[i]) for i, (a, b) in enumerate(pairs_in)]
        gain1 = param("gain1")
        shift1 = param("shift1")
        tbias = param("tbias")
        fetch_window(plan, table, wins, xwin, xsem, lo, hi, True)

        saved = [(n_buf, norm_ref), (k_buf, k_ref), (v_buf, v_ref)]

        def project(w, carry):
            n, _ = normalized(xwin[w].astype(WIDE))
            low = (n * gain1 + shift1).astype(LOW)
            n_buf[w] = low
            kv = dot(low, triple_ref[:, D:], NN)
            k_buf[w] = kv[:, :D].astype(LOW)
            v_buf[w] = (kv[:, D:] + tbias[:, D:]).astype(LOW)
            for i, (buf, ref) in enumerate(saved):
                pltpu.make_async_copy(buf.at[w], ref.at[w], ksem.at[i, w]).start()
            return carry

        lax.fori_loop(lo, hi + 1, project, 0)
        kown_ref[...] = k_buf[own]
        vown_ref[...] = v_buf[own]
        low = n_buf[own]
        normed_ref[...] = low
        q_ref[...] = scaled_query(low, triple_ref[:, :D], tbias[:, :D])

        lane = lax.broadcasted_iota(jnp.int32, (T, LANES), 1)
        qs = [halves(q_ref[:, LANES * p : LANES * (p + 1)]) for p in range(pairs)]
        ids = tiled(col_ref[...], T)
        for p in range(pairs):
            tops[p] = jnp.full((2 * T, LANES), MASKED, WIDE)
            sums[p] = jnp.zeros((2 * T, LANES), WIDE)
            accs[p] = jnp.zeros((2 * T, LANES), WIDE)

        def first(w, rows):
            seen = ids[rows] == row_ref[pl.ds(w, 1), :]
            for p in range(pairs):
                s = dot(qs[p][rows], k_buf[w, :, LANES * p : LANES * (p + 1)], NT)
                s = jnp.where(seen, s, MASKED)
                scores[p, w, rows, :] = s
                top = tops[p, rows, :]
                for j in range(0, T, LANES):
                    top = jnp.maximum(top, s[:, j : j + LANES])
                tops[p, rows, :] = top

        sweep(plan, table, first)
        for p in range(pairs):
            top = jnp.max(tops[p], axis=1, keepdims=True)
            tops[p] = jnp.broadcast_to(top, (2 * T, LANES))

        def second(w, rows):
            for p in range(pairs):
                top = jnp.concatenate([tops[p, rows, :]] * (T // LANES), axis=1)
                e = jnp.exp(scores[p, w, rows, :] - top)
                total = sums[p, rows, :]
                for j in range(0, T, LANES):
                    total = total + e[:, j : j + LANES]
                sums[p, rows, :] = total
                value = v_buf[w, :, LANES * p : LANES * (p + 1)]
                accs[p, rows, :] = accs[p, rows, :] + dot(e.astype(LOW), value, NN)

        sweep(plan, table, second)
        stats = jnp.zeros((T, LANES), WIDE)
        for p in range(pairs):
            total = jnp.sum(sums[p], axis=1, keepdims=True)
            mix[:, LANES * p : LANES * (p + 1)] = whole(accs[p] / total)
            log = tops[p] + jnp.log(total)
            for k in range(2):
                at = part * k
                column = jnp.concatenate(
                    [log[at : at + part], log[2 * part + at : 3 * part + at]], axis=0
                )
                stats = jnp.where(lane == 2 * p + k, column, stats)
        att = mix[...]
        for load in loads:
            load.wait()
        att_low = att.astype(LOW)
        att_ref[...] = att_low
        x = xwin[own].astype(WIDE)
        scale1 = param("scale1")
        scale2 = param("scale2")
        gain2 = param("gain2")
        branch_one = dot(att_low, wo[...], NN) + param("obias")
        middle = x + scale1 * branch_one
        n2, r2 = normalized(middle)
        n2_low = (n2 * gain2 + param("shift2")).astype(LOW)
        n2_ref[...] = n2_low
        pre = dot(n2_low, wup[...], NN) + param("ubias")
        cdf = 0.5 * (1.0 + lax.erf(pre * math.sqrt(0.5)))
        act_low = (pre * cdf).astype(LOW)
        act_buf[...] = act_low
        saves = [launch(act_buf, act_ref, osem.at[3])]
        slope = cdf + pre * (jnp.exp(-0.5 * pre * pre) * (1.0 / math.sqrt(2.0 * math.pi)))
        branch_two = dot(act_low, wdn[...], NN) + param("dbias")
        out_ref[...] = (middle + scale2 * branch_two).astype(LOW)

        up = cot_ref[...].astype(WIDE)
        gbt = (scale2 * up).astype(LOW)
        gbt_ref[...] = gbt
        gpre = (dot(gbt, wdn[...], NT) * slope).astype(LOW)
        pre_buf[...] = gpre
        saves.append(launch(pre_buf, pre_ref, osem.at[4]))
        gn2 = dot(gpre, wup[...], NT)
        gmid = up + norm_back(gn2, gain2, n2, r2)
        mid_ref[...] = gmid
        gbo = (scale1 * gmid).astype(LOW)
        gbo_ref[...] = gbo
        gatt = dot(gbo, wo[...], NT).astype(LOW)
        msg_ref[0:T, :] = gatt
        inner = gatt.astype(WIDE) * att
        left = lane < HEAD_DIM
        for p in range(HEADS // 2):
            piece = inner[:, LANES * p : LANES * (p + 1)]
            one = jnp.sum(jnp.where(left, piece, 0.0), axis=1, keepdims=True)
            two = jnp.sum(jnp.where(left, 0.0, piece), axis=1, keepdims=True)
            stats = jnp.where(lane == HEADS + 2 * p, one, stats)
            stats = jnp.where(lane == HEADS + 2 * p + 1, two, stats)
        stat_ref[...] = stats
        high = stats.astype(LOW).astype(WIDE)
        rest = pltpu.roll(stats - high, 2 * HEADS, 1)
        flipped = jnp.transpose(jnp.where(lane < 2 * HEADS, high, rest))
        tail = flipped[16:24, :]
        msg_ref[T : T + 16, 0:T] = flipped[0:16, :].astype(LOW)
        msg_ref[T : T + 16, T:] = jnp.concatenate(
            [tail[:, :LANES], tail[:, LANES:]], axis=0
        ).astype(LOW)

        vec_ref[...] = jnp.zeros(vec_ref.shape, WIDE)
        vec_ref[0:1, :D] = column_sum(up * branch_two)
        vec_ref[1:2, :D] = column_sum(gbt.astype(WIDE))
        vec_ref[2:3, :] = column_sum(gpre.astype(WIDE))
        vec_ref[3:4, :D] = column_sum(gn2 * n2)
        vec_ref[4:5, :D] = column_sum(gn2)
        vec_ref[5:6, :D] = column_sum(gmid * branch_one)
        vec_ref[6:7, :D] = column_sum(gbo.astype(WIDE))
        for i, (buf, ref) in enumerate(saved):
            block_copies(buf, ref, ksem.at[i], lo, hi, True)
        for save in saves:
            save.wait()

    return kernel


def fold(dest, row, left, right, width):
    wide = width // LANES
    height = left.shape[1]
    for i in range(0, height, 384):
        part = dot(left[:, i : i + 384], right[...], TN)
        for j in range(wide):
            dest[pl.ds(row + i * wide + j, 384, stride=wide), :] = part[
                :, LANES * j : LANES * (j + 1)
            ]


def query_kernel(plan):
    T = plan.tokens
    part = plan.part
    pairs = HEADS // 2

    def kernel(
        table,
        q_ref,
        k_ref,
        v_ref,
        msg_ref,
        stat_ref,
        col_ref,
        row_ref,
        gq_ref,
        logs,
        dots,
        accs,
        k_buf,
        v_buf,
        ksem,
        vsem,
    ):
        lo = table[plan.low_at()]
        hi = table[plan.low_at() + 1]
        block_copies(k_ref, k_buf, ksem, lo, hi, False)
        block_copies(v_ref, v_buf, vsem, lo, hi, False)
        qs = [halves(q_ref[:, LANES * p : LANES * (p + 1)]) for p in range(pairs)]
        gs = [halves(msg_ref[0:T, LANES * p : LANES * (p + 1)]) for p in range(pairs)]
        ids = tiled(col_ref[...], T)
        for p in range(pairs):
            for k in range(2):
                for c in range(2):
                    rows = slice(part * c, part * (c + 1))
                    to = slice(part * (2 * c + k), part * (2 * c + k + 1))
                    h = 2 * p + k
                    logs[p, to, :] = jnp.broadcast_to(stat_ref[rows, h : h + 1], (part, LANES))
                    h = h + HEADS
                    dots[p, to, :] = jnp.broadcast_to(stat_ref[rows, h : h + 1], (part, LANES))
            accs[p] = jnp.zeros((2 * T, LANES), WIDE)
        block_copies(k_ref, k_buf, ksem, lo, hi, True)
        block_copies(v_ref, v_buf, vsem, lo, hi, True)

        def step(w, rows):
            seen = ids[rows] == row_ref[pl.ds(w, 1), :]
            for p in range(pairs):
                cols = slice(LANES * p, LANES * (p + 1))
                key = k_buf[w, :, cols]
                s = jnp.where(seen, dot(qs[p][rows], key, NT), MASKED)
                prob = jnp.exp(s - jnp.concatenate([logs[p, rows, :]] * (T // LANES), axis=1))
                inner = jnp.concatenate([dots[p, rows, :]] * (T // LANES), axis=1)
                grad = prob * (dot(gs[p][rows], v_buf[w, :, cols], NT) - inner)
                accs[p, rows, :] = accs[p, rows, :] + dot(grad.astype(LOW), key, NN)

        sweep(plan, table, step)
        for p in range(pairs):
            gq_ref[:, LANES * p : LANES * (p + 1)] = (whole(accs[p]) * SCALE).astype(LOW)

    return kernel


def weight_kernel(plan):
    base = AT["out"]
    half = plan.count // 2

    def kernel(
        table,
        norm_ref,
        triple_ref,
        par_ref,
        act_ref,
        pre_ref,
        gbt_ref,
        n2_ref,
        att_ref,
        gbo_ref,
        vec_ref,
        q_ref,
        keep_ref,
        away_ref,
        tail_ref,
        flat,
        stage,
        n_buf,
        q_buf,
        nsem,
        qsem,
        ssem,
    ):
        lo = table[plan.low_at()]
        hi = table[plan.low_at() + 1]
        block_copies(norm_ref, n_buf, nsem, lo, hi, False)
        fold(flat, AT["down"] - base, act_ref, gbt_ref, D)
        fold(flat, AT["up"] - base, n2_ref, pre_ref, FF)
        fold(flat, AT["out"] - base, att_ref, gbo_ref, D)
        put_vector(flat, AT["scale2"] - base, vec_ref[0:1, :D])
        put_vector(flat, AT["dbias"] - base, vec_ref[1:2, :D])
        put_vector(flat, AT["ubias"] - base, vec_ref[2:3, :])
        put_vector(flat, AT["gain2"] - base, vec_ref[3:4, :D])
        put_vector(flat, AT["shift2"] - base, vec_ref[4:5, :D])
        put_vector(flat, AT["scale1"] - base, vec_ref[5:6, :D])
        put_vector(flat, AT["obias"] - base, vec_ref[6:7, :D])
        end = ALL_ROWS - base
        flat[end:, :] = jnp.zeros((flat.shape[0] - end, LANES), WIDE)
        tail_ref[...] = flat[0 : plan.rows, :]

        def put(e, wait):
            t = table[e]
            i = e - plan.first_late

            @pl.when(t < half)
            def _():
                c = pltpu.make_async_copy(stage.at[i], keep_ref.at[t], ssem.at[i])
                c.wait() if wait else c.start()

            @pl.when(t >= half)
            def _():
                c = pltpu.make_async_copy(stage.at[i], away_ref.at[t - half], ssem.at[i])
                c.wait() if wait else c.start()

        for e in range(plan.first_late, plan.count):
            r0 = plan.start[e] - base
            stage[e - plan.first_late] = flat[r0 : r0 + plan.rows, :].astype(LOW)
            put(e, False)

        bias = par_ref[VEC["tbias"] : VEC["tbias"] + 1, :D]
        block_copies(norm_ref, n_buf, nsem, lo, hi, True)

        def project(w, carry):
            q_buf[w] = scaled_query(n_buf[w], triple_ref[:, :D], bias)
            pltpu.make_async_copy(q_buf.at[w], q_ref.at[w], qsem.at[w]).start()
            return carry

        lax.fori_loop(lo, hi + 1, project, 0)
        block_copies(q_buf, q_ref, qsem, lo, hi, True)

        def finish(e, carry):
            put(e, True)
            return carry

        lax.fori_loop(plan.first_late, plan.count, finish, 0)

    return kernel


def last_kernel(plan, sources):
    T = plan.tokens
    early = plan.first_late
    half = plan.count // 2
    part = plan.part
    pairs = HEADS // 2

    def kernel(table, *refs):
        wins = refs[:sources]
        (
            q_ref,
            k_ref,
            v_ref,
            col_ref,
            row_ref,
            gq_ref,
            normed_ref,
            triple_any,
            x_ref,
            mid_ref,
            par_ref,
            tail_ref,
            _,
            _,
            grad_ref,
            keep_ref,
            away_ref,
        ) = refs[sources : sources + 17]
        mwin, q_buf, triple_ref, flat, gt, stage, stats, spare, acck, accv, msem, qsem, tsem, osem = refs[
            sources + 17 :
        ]
        lo = table[plan.low_at()]
        hi = table[plan.low_at() + 1]
        fetch_window(plan, table, wins, mwin, msem, lo, hi, False)
        block_copies(q_ref, q_buf, qsem, lo, hi, False)
        load = launch(triple_any, triple_ref, tsem.at[0])
        ks = [halves(k_ref[:, LANES * p : LANES * (p + 1)]) for p in range(pairs)]
        vs = [halves(v_ref[:, LANES * p : LANES * (p + 1)]) for p in range(pairs)]
        ids = tiled(col_ref[...], T)
        for p in range(pairs):
            acck[p] = jnp.zeros((2 * T, LANES), WIDE)
            accv[p] = jnp.zeros((2 * T, LANES), WIDE)
        fetch_window(plan, table, wins, mwin, msem, lo, hi, True)
        block_copies(q_ref, q_buf, qsem, lo, hi, True)

        def unpack(w, carry):
            got = mwin[w, T : T + 16, :].astype(WIDE)
            spare[0:16, :] = got[:, :T]
            spare[16:24, :] = jnp.concatenate([got[:8, T:], got[8:, T:]], axis=1)
            stats[w, 0 : 2 * HEADS, :] = spare[0 : 2 * HEADS, :] + spare[2 * HEADS : 4 * HEADS, :]
            return carry

        lax.fori_loop(lo, hi + 1, unpack, 0)

        def step(w, rows):
            seen = ids[rows] == row_ref[pl.ds(w, 1), :]
            copies = (rows.stop - rows.start) // (2 * part)

            def pair_rows(h):
                two = [jnp.broadcast_to(stats[w, h + k : h + k + 1, :], (part, T)) for k in range(2)]
                return jnp.concatenate(two * copies, axis=0)

            for p in range(pairs):
                cols = slice(LANES * p, LANES * (p + 1))
                q = q_buf[w, :, cols]
                g = mwin[w, 0:T, cols]
                s = jnp.where(seen, dot(ks[p][rows], q, NT), MASKED)
                prob = jnp.exp(s - pair_rows(2 * p))
                grad = prob * (dot(vs[p][rows], g, NT) - pair_rows(HEADS + 2 * p))
                acck[p, rows, :] = acck[p, rows, :] + dot(grad.astype(LOW), q, NN)
                accv[p, rows, :] = accv[p, rows, :] + dot(prob.astype(LOW), g, NN)

        sweep(plan, table, step)
        for p in range(pairs):
            gt[:, D + LANES * p : D + LANES * (p + 1)] = whole(acck[p]).astype(LOW)
            gt[:, 2 * D + LANES * p : 2 * D + LANES * (p + 1)] = whole(accv[p]).astype(LOW)
        gt[:, :D] = gq_ref[...]
        fold(flat, AT["triple"], normed_ref, gt, 3 * D)
        put_vector(flat, AT["tbias"], column_sum(gt[:, :D].astype(WIDE)))
        put_vector(flat, AT["tbias"] + D // LANES, column_sum(gt[:, 2 * D :].astype(WIDE)))
        load.wait()
        gn = dot(gt[...], triple_ref[...], NT)
        n, r = normalized(x_ref[...].astype(WIDE))
        put_vector(flat, AT["gain1"], column_sum(gn * n))
        put_vector(flat, AT["shift1"], column_sum(gn))
        flat[AT["out"] : AT["out"] + plan.rows, :] = tail_ref[...]

        def put(e, wait):
            t = table[e]

            @pl.when(t < half)
            def _():
                c = pltpu.make_async_copy(stage.at[e], keep_ref.at[t], osem.at[e])
                c.wait() if wait else c.start()

            @pl.when(t >= half)
            def _():
                c = pltpu.make_async_copy(stage.at[e], away_ref.at[t - half], osem.at[e])
                c.wait() if wait else c.start()

        for e in range(early):
            r0 = plan.start[e]
            stage[e] = flat[r0 : r0 + plan.rows, :].astype(LOW)
            put(e, False)
        gain1 = par_ref[VEC["gain1"] : VEC["gain1"] + 1, :D]
        grad_ref[...] = mid_ref[...] + norm_back(gn, gain1, n, r)
        for e in range(early):
            put(e, True)

    return kernel


def shape(dims, kind):
    return jax.ShapeDtypeStruct(dims, kind)


SMEM = pl.BlockSpec(memory_space=pltpu.SMEM)
VMEM = pl.BlockSpec(memory_space=pltpu.VMEM)
ANY = pl.BlockSpec(memory_space=pl.ANY)


def build(plan):
    T = plan.tokens
    W = plan.window
    R = plan.rows
    N = plan.count
    limit = pltpu.CompilerParams(vmem_limit_bytes=60 * 1024 * 1024)

    def per_device(inputs, cotangent, master, first_moment, second_moment, image_ids, spans):
        device = lax.axis_index(BOTH).astype(jnp.int32)
        shift = ((device * plan.share) % LANES).reshape(1).astype(jnp.int32)
        shifted = pl.pallas_call(
            shift_kernel(plan),
            in_specs=[SMEM, VMEM],
            out_specs=VMEM,
            out_shape=shape((R, LANES), LOW),
            scratch_shapes=[pltpu.VMEM((R + 8, LANES), WIDE)],
            name="shift",
        )(shift, jnp.pad(master, (0, R * LANES - plan.share)).reshape(R, LANES))
        near, core, (image_ids, spans) = plan.spread(shifted, (image_ids, spans))
        padded = jnp.pad(image_ids, (plan.reach * T, plan.reach * T), constant_values=-1)
        key_ids = lax.dynamic_slice_in_dim(padded, device * T, W * T, 0).reshape(W, T)
        table = plan.table(device, spans, key_ids)
        own_ids = key_ids[plan.reach]
        columns = jnp.broadcast_to(own_ids[:, None], (T, LANES))
        wins = plan.exchange(inputs)
        sources = len(wins)

        half = pltpu.VMEM((HEADS // 2, 2 * T, LANES), WIDE)
        unpack = pl.pallas_call(
            unpack_kernel(plan),
            in_specs=[SMEM, ANY, ANY],
            out_specs=[VMEM] * 5,
            out_shape=[
                shape((D, 3 * D), LOW),
                shape((D, D), LOW),
                shape((D, FF), LOW),
                shape((FF, D), LOW),
                shape((16, FF), WIDE),
            ],
            scratch_shapes=[
                pltpu.VMEM((N, R, LANES), LOW),
                pltpu.VMEM((plan.flat_rows, LANES), WIDE),
                pltpu.SemaphoreType.DMA((N,)),
            ],
            compiler_params=limit,
            name="unpack",
        )
        triple, wo, wup, wdn, params = unpack(table, near, core)

        outs = pl.pallas_call(
            forward_kernel(plan, sources),
            in_specs=[SMEM] + [ANY] * sources + [VMEM] + [ANY] * 3 + [VMEM] * 4,
            out_specs=[VMEM] * 3 + [ANY] * 3 + [VMEM] * 2 + [ANY] * 2 + [VMEM] * 8,
            out_shape=[
                shape((T, D), LOW),
                shape((T + 16, D), LOW),
                shape((T, D), LOW),
                shape((W, T, D), LOW),
                shape((W, T, D), LOW),
                shape((W, T, D), LOW),
                shape((T, D), LOW),
                shape((T, D), WIDE),
                shape((T, FF), LOW),
                shape((T, FF), LOW),
                shape((T, D), LOW),
                shape((T, D), LOW),
                shape((T, D), LOW),
                shape((T, D), LOW),
                shape((8, FF), WIDE),
                shape((T, LANES), WIDE),
                shape((T, D), LOW),
                shape((T, D), LOW),
            ],
            scratch_shapes=[
                pltpu.VMEM((W, T, D), LOW),
                pltpu.VMEM((W, T, D), LOW),
                pltpu.VMEM((W, T, D), LOW),
                pltpu.VMEM((W, T, D), LOW),
                pltpu.VMEM((HEADS // 2, W, 2 * T, T), WIDE),
                half,
                half,
                half,
                pltpu.VMEM((T, D), WIDE),
                pltpu.VMEM((D, D), LOW),
                pltpu.VMEM((D, FF), LOW),
                pltpu.VMEM((FF, D), LOW),
                pltpu.VMEM((T, FF), LOW),
                pltpu.VMEM((T, FF), LOW),
                pltpu.SemaphoreType.DMA((W,)),
                pltpu.SemaphoreType.DMA((3, W)),
                pltpu.SemaphoreType.DMA((5,)),
            ],
            compiler_params=limit,
            name="forward",
        )(table, *wins, triple, wo, wup, wdn, params, cotangent, columns, key_ids)
        (
            result,
            message,
            q,
            k,
            v,
            norms,
            normed,
            gmid,
            act,
            gpre,
            gbt,
            n2,
            att,
            gbo,
            vec,
            stat,
            k_own,
            v_own,
        ) = outs
        messages = plan.exchange(message)

        query_call = pl.pallas_call(
            query_kernel(plan),
            in_specs=[SMEM, VMEM, ANY, ANY] + [VMEM] * 4,
            out_specs=VMEM,
            out_shape=shape((T, D), LOW),
            scratch_shapes=[
                half,
                half,
                half,
                pltpu.VMEM((W, T, D), LOW),
                pltpu.VMEM((W, T, D), LOW),
                pltpu.SemaphoreType.DMA((W,)),
                pltpu.SemaphoreType.DMA((W,)),
            ],
            compiler_params=limit,
            name="query",
        )
        gq = query_call(table, q, k, v, message, stat, columns, key_ids)
        weight_call = pl.pallas_call(
            weight_kernel(plan),
            in_specs=[SMEM, ANY] + [VMEM] * 9,
            out_specs=[ANY] * 3 + [VMEM],
            out_shape=[
                shape((W, T, D), LOW),
                shape((N // 2, R, LANES), LOW),
                shape((N // 2, R, LANES), LOW),
                shape((R, LANES), WIDE),
            ],
            scratch_shapes=[
                pltpu.VMEM((plan.flat_rows - AT["out"] + 8, LANES), WIDE),
                pltpu.VMEM((N - plan.first_late, R, LANES), LOW),
                pltpu.VMEM((W, T, D), LOW),
                pltpu.VMEM((W, T, D), LOW),
                pltpu.SemaphoreType.DMA((W,)),
                pltpu.SemaphoreType.DMA((W,)),
                pltpu.SemaphoreType.DMA((N - plan.first_late,)),
            ],
            compiler_params=limit,
            name="weight",
        )
        queries, keep, away, tail = weight_call(
            table, norms, triple, params, act, gpre, gbt, n2, att, gbo, vec
        )

        late = plan.first_late
        input_grad, keep, away = pl.pallas_call(
            last_kernel(plan, sources),
            in_specs=[SMEM] + [ANY] * (sources + 1) + [VMEM] * 6 + [ANY] + [VMEM] * 4 + [ANY, ANY],
            out_specs=[VMEM, ANY, ANY],
            out_shape=[
                shape((T, D), WIDE),
                shape((N // 2, R, LANES), LOW),
                shape((N // 2, R, LANES), LOW),
            ],
            scratch_shapes=[
                pltpu.VMEM((W, T + 16, D), LOW),
                pltpu.VMEM((W, T, D), LOW),
                pltpu.VMEM((D, 3 * D), LOW),
                pltpu.VMEM((AT["out"] + R + 8, LANES), WIDE),
                pltpu.VMEM((T, 3 * D), LOW),
                pltpu.VMEM((late, R, LANES), LOW),
                pltpu.VMEM((W, 16, T), WIDE),
                pltpu.VMEM((24, T), WIDE),
                half,
                half,
                pltpu.SemaphoreType.DMA((W,)),
                pltpu.SemaphoreType.DMA((W,)),
                pltpu.SemaphoreType.DMA((1,)),
                pltpu.SemaphoreType.DMA((late,)),
            ],
            input_output_aliases={13 + sources: 1, 14 + sources: 2},
            compiler_params=limit,
            name="last",
        )(
            table,
            *messages,
            queries,
            k_own,
            v_own,
            columns,
            key_ids,
            gq,
            normed,
            triple,
            inputs,
            gmid,
            params,
            tail,
            keep,
            away,
        )

        parts = plan.reduce_parts(keep, away)
        grad, square = pl.pallas_call(
            unshift_kernel(plan),
            in_specs=[SMEM] + [VMEM] * len(parts),
            out_specs=[VMEM, VMEM],
            out_shape=[shape((R, LANES), WIDE), shape((N, LANES), WIDE)],
            scratch_shapes=[pltpu.VMEM((R + 8, LANES), WIDE)],
            name="unshift",
        )(shift, *parts)
        grad_shard = grad.reshape(-1)[: plan.share]
        squares = lax.all_to_all(square, BOTH, 0, 0, tiled=True)
        grad_norm = jnp.sqrt(jnp.sum(squares[:, 0]))
        ceiling = CLIP_RATIO * math.sqrt(plan.share * N)
        factor = ceiling / jnp.maximum(grad_norm, ceiling)
        clipped = grad_shard * factor
        new_first = BETA_ONE * first_moment + (1.0 - BETA_ONE) * clipped
        new_second = BETA_TWO * second_moment + (1.0 - BETA_TWO) * clipped * clipped
        new_master = master - LEARN_RATE * (
            new_first / (jnp.sqrt(new_second) + ADAM_EPS) + WEIGHT_DECAY * master
        )
        return (
            result,
            input_grad,
            grad_shard,
            grad_norm.reshape(1),
            new_first,
            new_second,
            new_master,
        )

    return per_device


def solution(mesh):
    dp = mesh.shape["dp"]
    fsdp = mesh.shape["fsdp"]
    row = P(BOTH, None)
    flat = P(BOTH)
    in_specs = (row, row, flat, flat, flat, P(), P())
    out_specs = (row, row, flat, P(), flat, flat, flat)

    def per_device(*args):
        inputs, master = args[0], args[2]
        plan = Plan(dp, fsdp, master.shape[0], inputs.shape[0])
        return build(plan)(*args)

    return jax.shard_map(
        per_device, mesh=mesh, in_specs=in_specs, out_specs=out_specs, check_vma=False
    )
```

```python
import math

import jax
import jax.numpy as jnp
from jax import lax
from jax.experimental import pallas as pl
from jax.experimental.pallas import tpu as pltpu
from jax.sharding import PartitionSpec as P


D = 384
HEADS = 6
HEAD_DIM = 64
FF = 1536
IMG = 1370
LANES = 128

LN_EPS = 1e-06
BETA_ONE = 0.5
BETA_TWO = 0.6
LEARN_RATE = 0.01
WEIGHT_DECAY = 0.05
ADAM_EPS = 1e-08
CLIP_RATIO = 0.25
MASKED = -1e30
BOTH = ("dp", "fsdp")
LOW = jnp.bfloat16
WIDE = jnp.float32
SCALE = HEAD_DIM ** (-0.5)

NT = (((1,), (1,)), ((), ()))
NN = (((1,), (0,)), ((), ()))
TN = (((0,), (0,)), ((), ()))

PIECES = [
    ("gain1", D),
    ("shift1", D),
    ("triple", 3 * D * D),
    ("tbias", 2 * D),
    ("out", D * D),
    ("obias", D),
    ("scale1", D),
    ("gain2", D),
    ("shift2", D),
    ("up", D * FF),
    ("ubias", FF),
    ("down", FF * D),
    ("dbias", D),
    ("scale2", D),
]
AT = {}
_row = 0
for _name, _count in PIECES:
    AT[_name] = _row
    _row += _count // LANES
ALL_ROWS = _row


def dot(a, b, dims):
    return lax.dot_general(a, b, dims, preferred_element_type=WIDE)


class Plan:
    def __init__(self, dp, fsdp, share, tokens):
        self.count = dp * fsdp
        self.share = share
        self.rows = -(-(2 * (LANES - 1) + share) // LANES)
        self.rows = -(-self.rows // 16) * 16
        self.cut = self.rows * 3 // 64 * 16
        self.start = [e * share // LANES for e in range(self.count)]
        self.tokens = tokens
        self.part = tokens // 2
        self.reach = (IMG - 2 + tokens) // tokens
        self.window = 2 * self.reach + 1
        self.grouped = dp == 4 and fsdp == 8 and self.reach <= 6
        if self.grouped:
            self.stages = [[2, 4, 6], [16, 1, 17], [8]]
        else:
            bits = [1 << k for k in range(self.count.bit_length() - 1)]
            bits = [b for b in bits if b != fsdp] + [fsdp]
            self.stages = [[b] for b in bits]
        masks = [0]
        for stage in self.stages:
            masks = masks + [m ^ s for s in stage for m in masks]
        self.bits = [masks[1 << k] for k in range(self.count.bit_length() - 1)]
        self.first_late = next(e for e in range(self.count) if self.start[e] >= AT["out"])
        self.flat_rows = -(-(self.start[-1] + self.rows) // 8) * 8

    def send(self, x, mask):
        return lax.ppermute(x, BOTH, [(i, i ^ mask) for i in range(self.count)])

    def spread(self, own, extra):
        buf = own[None]
        for level, stage in enumerate(self.stages[:-1]):
            parts = [buf]
            for m in stage:
                parts.append(self.send(buf, m))
            buf = jnp.concatenate(parts, axis=0)
            if level == 0:
                buf, extra = lax.optimization_barrier((buf, extra))
        core = self.send(buf, self.stages[-1][0])
        return buf, core, extra

    def reduce_parts(self, keep, away):
        def added(parts):
            total = parts[0].astype(WIDE)
            for part in parts[1:]:
                total = total + part.astype(WIDE)
            return total.astype(LOW)

        def one(pieces, level):
            parts = [pieces[0]]
            for k, m in enumerate(self.stages[level]):
                parts.append(self.send(pieces[k + 1], m))
            return parts

        got = [keep, self.send(away, self.stages[-1][0])]
        if self.grouped:
            wide, deep = len(self.stages[1]) + 1, len(self.stages[0]) + 1
            got = [x.reshape((wide, deep) + x.shape[1:]) for x in got]
            lead = [added([x[k, :, : self.cut] for x in got]) for k in range(wide)]
            rest = [added([x[:, k, self.cut :] for x in got]) for k in range(deep)]
            lead = one(lead, 1)
            rest = one(rest, 0)
            lead = [added([x[k] for x in lead]) for k in range(deep)]
            rest = [added([x[k] for x in rest]) for k in range(wide)]
            return one(lead, 0) + one(rest, 1)
        for level in reversed(range(len(self.stages) - 1)):
            count = len(self.stages[level]) + 1
            got = [x.reshape((count, -1) + x.shape[1:]) for x in got]
            got = one([added([x[k] for x in got]) for k in range(count)], level)
        return [part[0] for part in got]

    def exchange(self, block):
        own = block[None]
        if self.grouped:
            hops = []
            for m in (1, 2, 3, 4, 6):
                hops.append(self.send(own, m))
            one, two, three, four, six = hops
            pair = jnp.concatenate([four, six], axis=0)
            quad = jnp.concatenate([two, three, four, six], axis=0)
            pair, quad = lax.optimization_barrier((pair, quad))
            across = [(8 + j, 16 + j) for j in range(6)] + [(16 + j, 8 + j) for j in range(2, 8)]
            skew = [(8 + j, 16 + (j ^ 1)) for j in range(4)]
            skew += [(16 + j, 8 + (j ^ 1)) for j in range(4, 8)]
            far = lax.ppermute(quad, BOTH, across)
            far_beside = lax.ppermute(pair, BOTH, skew)
            beside = self.send(pair, 1)
            home = self.send(quad, 8)
            home_beside = self.send(beside, 8)
            return [own, one, quad, beside, home, home_beside, far, far_beside]
        slots = []
        for slot in range(self.window):
            by = self.reach - slot
            pairs = [(i, i + by) for i in range(self.count) if 0 <= i + by < self.count]
            slots.append(own if by == 0 else lax.ppermute(own, BOTH, pairs))
        return [jnp.concatenate(slots, axis=0)]

    def table(self, device, spans, key_ids):
        e = jnp.arange(self.count, dtype=jnp.int32)
        rel = e ^ device
        where = jnp.zeros_like(e)
        for k, bit in enumerate(self.bits):
            where = where + jnp.where((rel & bit) != 0, 1 << k, 0)
        slot = jnp.arange(self.window, dtype=jnp.int32)
        if self.grouped:
            other = device - self.reach + slot
            mask = (other ^ device) & 7
            late = (mask == 5) | (mask == 7)
            index = jnp.where(late, mask >> 2 & mask >> 1, jnp.where(mask == 6, 3, mask - 2))
            index = jnp.where(mask < 2, 0, index)
            group = jnp.where(mask < 2, mask, jnp.where(late, 3, 2))
            cross = (other >> 3) ^ (device >> 3)
            source = group + jnp.where(cross == 0, 0, jnp.where(cross == 1, 2, 4))
        else:
            source = jnp.zeros_like(slot)
            index = slot
        bounds = lax.dynamic_index_in_dim(spans, device, 0, keepdims=False)
        ends = jnp.clip(bounds - device + self.reach, 0, self.window - 1)
        own = key_ids[self.reach]
        low, high = own[:: self.part], own[self.part - 1 :: self.part]
        seen = (key_ids[:, -1][None] >= low[:, None]) & (key_ids[:, 0][None] <= high[:, None])
        seen = seen & (slot >= ends[0])[None] & (slot <= ends[1])[None]
        begin = jnp.min(jnp.where(seen, slot[None], self.window), axis=1)
        finish = jnp.max(jnp.where(seen, slot[None], -1), axis=1)
        return jnp.concatenate([where, source, index, ends, begin, finish]).astype(jnp.int32)

    def source_at(self, slot):
        return self.count + slot

    def index_at(self, slot):
        return self.count + self.window + slot

    def low_at(self):
        return self.count + 2 * self.window

    def range_at(self, quarter):
        at = self.count + 2 * self.window + 2 + quarter
        return at, at + self.tokens // self.part


def fetch_window(plan, table, sources, dest, sems, lo, hi, wait):
    def step(slot, carry):
        if wait:
            pltpu.make_async_copy(sources[0].at[0], dest.at[slot], sems.at[slot]).wait()
            return carry
        for k, source in enumerate(sources):

            @pl.when(table[plan.source_at(slot)] == k)
            def _(source=source):
                copy = pltpu.make_async_copy(
                    source.at[table[plan.index_at(slot)]], dest.at[slot], sems.at[slot]
                )
                copy.start()

        return carry

    lax.fori_loop(lo, hi + 1, step, 0)


def normalized(x):
    center = x - jnp.mean(x, axis=-1, keepdims=True)
    spread = jnp.mean(center * center, axis=-1, keepdims=True)
    r = lax.rsqrt(spread + LN_EPS)
    return center * r, r


def norm_back(grad, gain, n, r):
    g = grad * gain
    inner = jnp.mean(g, axis=-1, keepdims=True)
    outer = jnp.mean(g * n, axis=-1, keepdims=True)
    return r * (g - inner - n * outer)


def vector(ref, row, width):
    return jnp.concatenate([ref[row + j : row + j + 1, :] for j in range(width // LANES)], axis=1)


def put_vector(ref, row, value):
    for j in range(value.shape[1] // LANES):
        ref[row + j : row + j + 1, :] = value[:, LANES * j : LANES * (j + 1)]


def stacked(x):
    left = lax.broadcasted_iota(jnp.int32, x.shape, 1) < HEAD_DIM
    return jnp.concatenate([jnp.where(left, x, 0), jnp.where(left, 0, x)], axis=0)


def unstacked(x):
    half = x.shape[0] // 2
    left = lax.broadcasted_iota(jnp.int32, (half, LANES), 1) < HEAD_DIM
    return jnp.where(left, x[:half], x[half:])


def halves(x):
    part = x.shape[0] // 2
    return jnp.concatenate([stacked(x[:part]), stacked(x[part:])], axis=0)


def whole(x):
    part = x.shape[0] // 2
    return jnp.concatenate([unstacked(x[:part]), unstacked(x[part:])], axis=0)


def tiled(ids, width):
    part = ids.shape[0] // 2
    ids = jnp.concatenate([ids] * (width // LANES), axis=1)
    return jnp.concatenate([ids[:part], ids[:part], ids[part:], ids[part:]], axis=0)


def sweep(plan, table, body):
    (a, b), (c, d) = plan.range_at(0), plan.range_at(1)
    rows = 2 * plan.part

    def loop(begin, finish, rows):
        def step(w, carry):
            body(w, rows)
            return carry

        lax.fori_loop(begin, finish, step, 0)

    loop(table[a], table[c], slice(0, rows))
    loop(table[c], table[b] + 1, slice(0, 2 * rows))
    loop(table[b] + 1, table[d] + 1, slice(rows, 2 * rows))


def launch(source, dest, sem):
    copy = pltpu.make_async_copy(source, dest, sem)
    copy.start()
    return copy


def block_copies(source, dest, sems, lo, hi, wait):
    def step(slot, carry):
        copy = pltpu.make_async_copy(source.at[slot], dest.at[slot], sems.at[slot])
        copy.wait() if wait else copy.start()
        return carry

    lax.fori_loop(lo, hi + 1, step, 0)


def scaled_query(low, weight, bias):
    q = dot(low, weight, NN) + bias
    return (q.astype(LOW).astype(WIDE) * SCALE).astype(LOW)


def column_sum(x):
    return jnp.sum(x, axis=0, keepdims=True)


def shift_kernel(plan):
    def kernel(table, x_ref, out_ref, pad):
        s = table[0]
        x = x_ref[...]
        y = pltpu.roll(x, s, 1)
        pad[0:8, :] = jnp.zeros((8, LANES), WIDE)
        pad[8:, :] = y
        lane = lax.broadcasted_iota(jnp.int32, y.shape, 1)
        out_ref[...] = jnp.where(lane >= s, y, pad[7 : 7 + plan.rows, :]).astype(LOW)

    return kernel


def unshift_kernel(plan):
    def kernel(table, *refs):
        parts, (out_ref, sq_ref, pad) = refs[:-3], refs[-3:]
        s = table[0]

        def total(parts):
            got = [p[...].astype(WIDE) for p in parts]
            while len(got) > 1:
                got = [got[k] + got[k + 1] for k in range(0, len(got), 2)]
            return got[0]

        if plan.grouped:
            lead = len(plan.stages[0]) + 1
            y = jnp.concatenate([total(parts[:lead]), total(parts[lead:])], axis=0)
        else:
            y = total(parts)
        y = pltpu.roll(y, LANES - s, 1)
        pad[0 : plan.rows, :] = y
        pad[plan.rows :, :] = jnp.zeros((8, LANES), WIDE)
        lane = lax.broadcasted_iota(jnp.int32, y.shape, 1)
        row = lax.broadcasted_iota(jnp.int32, y.shape, 0)
        out = jnp.where(lane < LANES - s, y, pad[1 : 1 + plan.rows, :])
        out = jnp.where(row * LANES + lane < plan.share, out, 0.0)
        out_ref[...] = out
        sq = jnp.sum(jnp.sum(out * out, axis=0, keepdims=True), axis=1, keepdims=True)
        sq_ref[...] = jnp.broadcast_to(sq, (plan.count, LANES))

    return kernel


VEC = {"gain1": 0, "shift1": 1, "tbias": 2, "obias": 3, "scale1": 4, "gain2": 5, "shift2": 6}
VEC.update({"ubias": 7, "dbias": 8, "scale2": 9})


def unpack_kernel(plan):
    half = plan.count // 2

    def kernel(
        table,
        near,
        core,
        triple_ref,
        wo_ref,
        wup_ref,
        wdn_ref,
        vec_ref,
        wbuf,
        flat,
        triple,
        wo,
        wup,
        wdn,
        wsem,
        osem,
    ):
        def weight_copy(e, wait):
            t = table[e]

            @pl.when(t < half)
            def _():
                c = pltpu.make_async_copy(near.at[t], wbuf.at[e], wsem.at[e])
                c.wait() if wait else c.start()

            @pl.when(t >= half)
            def _():
                c = pltpu.make_async_copy(core.at[t - half], wbuf.at[e], wsem.at[e])
                c.wait() if wait else c.start()

        def start_one(e, carry):
            weight_copy(e, False)
            return carry

        lax.fori_loop(0, plan.count, start_one, 0)
        for e in range(plan.count):
            weight_copy(e, True)
            r0 = plan.start[e]
            block = wbuf[e].astype(WIDE)
            if e:
                before = flat[r0 : r0 + 1, :]
                flat[r0 : r0 + plan.rows, :] = block
                flat[r0 : r0 + 1, :] = before + block[0:1, :]
            else:
                flat[r0 : r0 + plan.rows, :] = block

        def unfold(dest, name, height, width):
            wide = width // LANES
            step = min(height, 384)
            for j in range(wide):
                for i in range(0, height, step):
                    dest[i : i + step, LANES * j : LANES * (j + 1)] = flat[
                        pl.ds(AT[name] + i * wide + j, step, stride=wide), :
                    ].astype(LOW)

        unfold(wup, "up", D, FF)
        saves = [launch(wup, wup_ref, osem.at[0])]
        unfold(wdn, "down", FF, D)
        saves.append(launch(wdn, wdn_ref, osem.at[1]))
        unfold(triple, "triple", D, 3 * D)
        saves.append(launch(triple, triple_ref, osem.at[2]))
        unfold(wo, "out", D, D)
        saves.append(launch(wo, wo_ref, osem.at[3]))
        vec_ref[...] = jnp.zeros(vec_ref.shape, WIDE)
        for name, row in VEC.items():
            width = dict(PIECES)[name]
            vec_ref[row : row + 1, :width] = vector(flat, AT[name], width)
        for save in saves:
            save.wait()

    return kernel


def forward_kernel(plan, sources):
    T = plan.tokens
    own = plan.reach
    part = plan.part
    pairs = HEADS // 2

    def kernel(table, *refs):
        wins = refs[:sources]
        triple_ref, wo_ref, wup_ref, wdn_ref, par_ref, cot_ref, col_ref, row_ref = refs[
            sources : 8 + sources
        ]
        (
            out_ref,
            msg_ref,
            q_ref,
            k_ref,
            v_ref,
            norm_ref,
            normed_ref,
            mid_ref,
            act_ref,
            pre_ref,
            gbt_ref,
            n2_ref,
            att_ref,
            gbo_ref,
            vec_ref,
            stat_ref,
            kown_ref,
            vown_ref,
        ) = refs[8 + sources : 26 + sources]
        xwin, n_buf, k_buf, v_buf, scores, tops, sums, accs, mix = refs[26 + sources : 35 + sources]
        wo, wup, wdn, act_buf, pre_buf, xsem, ksem, osem = refs[35 + sources :]
        lo = table[plan.low_at()]
        hi = table[plan.low_at() + 1]

        def param(name):
            row = VEC[name]
            return par_ref[row : row + 1, : dict(PIECES)[name]]

        fetch_window(plan, table, wins, xwin, xsem, lo, hi, False)
        pairs_in = [(wo_ref, wo), (wup_ref, wup), (wdn_ref, wdn)]
        loads = [launch(a, b, osem.at[i]) for i, (a, b) in enumerate(pairs_in)]
        gain1 = param("gain1")
        shift1 = param("shift1")
        tbias = param("tbias")
        fetch_window(plan, table, wins, xwin, xsem, lo, hi, True)

        saved = [(n_buf, norm_ref), (k_buf, k_ref), (v_buf, v_ref)]

        def project(w, carry):
            n, _ = normalized(xwin[w].astype(WIDE))
            low = (n * gain1 + shift1).astype(LOW)
            n_buf[w] = low
            kv = dot(low, triple_ref[:, D:], NN)
            k_buf[w] = kv[:, :D].astype(LOW)
            v_buf[w] = (kv[:, D:] + tbias[:, D:]).astype(LOW)
            for i, (buf, ref) in enumerate(saved):
                pltpu.make_async_copy(buf.at[w], ref.at[w], ksem.at[i, w]).start()
            return carry

        lax.fori_loop(lo, hi + 1, project, 0)
        kown_ref[...] = k_buf[own]
        vown_ref[...] = v_buf[own]
        low = n_buf[own]
        normed_ref[...] = low
        q_ref[...] = scaled_query(low, triple_ref[:, :D], tbias[:, :D])

        lane = lax.broadcasted_iota(jnp.int32, (T, LANES), 1)
        qs = [halves(q_ref[:, LANES * p : LANES * (p + 1)]) for p in range(pairs)]
        ids = tiled(col_ref[...], T)
        for p in range(pairs):
            tops[p] = jnp.full((2 * T, LANES), MASKED, WIDE)
            sums[p] = jnp.zeros((2 * T, LANES), WIDE)
            accs[p] = jnp.zeros((2 * T, LANES), WIDE)

        def first(w, rows):
            seen = ids[rows] == row_ref[pl.ds(w, 1), :]
            for p in range(pairs):
                s = dot(qs[p][rows], k_buf[w, :, LANES * p : LANES * (p + 1)], NT)
                s = jnp.where(seen, s, MASKED)
                scores[p, w, rows, :] = s
                top = tops[p, rows, :]
                for j in range(0, T, LANES):
                    top = jnp.maximum(top, s[:, j : j + LANES])
                tops[p, rows, :] = top

        sweep(plan, table, first)
        for p in range(pairs):
            top = jnp.max(tops[p], axis=1, keepdims=True)
            tops[p] = jnp.broadcast_to(top, (2 * T, LANES))

        def second(w, rows):
            for p in range(pairs):
                top = jnp.concatenate([tops[p, rows, :]] * (T // LANES), axis=1)
                e = jnp.exp(scores[p, w, rows, :] - top)
                total = sums[p, rows, :]
                for j in range(0, T, LANES):
                    total = total + e[:, j : j + LANES]
                sums[p, rows, :] = total
                value = v_buf[w, :, LANES * p : LANES * (p + 1)]
                accs[p, rows, :] = accs[p, rows, :] + dot(e.astype(LOW), value, NN)

        sweep(plan, table, second)
        stats = jnp.zeros((T, LANES), WIDE)
        for p in range(pairs):
            total = jnp.sum(sums[p], axis=1, keepdims=True)
            mix[:, LANES * p : LANES * (p + 1)] = whole(accs[p] / total)
            log = tops[p] + jnp.log(total)
            for k in range(2):
                at = part * k
                column = jnp.concatenate(
                    [log[at : at + part], log[2 * part + at : 3 * part + at]], axis=0
                )
                stats = jnp.where(lane == 2 * p + k, column, stats)
        att = mix[...]
        for load in loads:
            load.wait()
        att_low = att.astype(LOW)
        att_ref[...] = att_low
        x = xwin[own].astype(WIDE)
        scale1 = param("scale1")
        scale2 = param("scale2")
        gain2 = param("gain2")
        branch_one = dot(att_low, wo[...], NN) + param("obias")
        middle = x + scale1 * branch_one
        n2, r2 = normalized(middle)
        n2_low = (n2 * gain2 + param("shift2")).astype(LOW)
        n2_ref[...] = n2_low
        pre = dot(n2_low, wup[...], NN) + param("ubias")
        cdf = 0.5 * (1.0 + lax.erf(pre * math.sqrt(0.5)))
        act_low = (pre * cdf).astype(LOW)
        act_buf[...] = act_low
        saves = [launch(act_buf, act_ref, osem.at[3])]
        slope = cdf + pre * (jnp.exp(-0.5 * pre * pre) * (1.0 / math.sqrt(2.0 * math.pi)))
        branch_two = dot(act_low, wdn[...], NN) + param("dbias")
        out_ref[...] = (middle + scale2 * branch_two).astype(LOW)

        up = cot_ref[...].astype(WIDE)
        gbt = (scale2 * up).astype(LOW)
        gbt_ref[...] = gbt
        gpre = (dot(gbt, wdn[...], NT) * slope).astype(LOW)
        pre_buf[...] = gpre
        saves.append(launch(pre_buf, pre_ref, osem.at[4]))
        gn2 = dot(gpre, wup[...], NT)
        gmid = up + norm_back(gn2, gain2, n2, r2)
        mid_ref[...] = gmid
        gbo = (scale1 * gmid).astype(LOW)
        gbo_ref[...] = gbo
        gatt = dot(gbo, wo[...], NT).astype(LOW)
        msg_ref[0:T, :] = gatt
        inner = gatt.astype(WIDE) * att
        left = lane < HEAD_DIM
        for p in range(HEADS // 2):
            piece = inner[:, LANES * p : LANES * (p + 1)]
            one = jnp.sum(jnp.where(left, piece, 0.0), axis=1, keepdims=True)
            two = jnp.sum(jnp.where(left, 0.0, piece), axis=1, keepdims=True)
            stats = jnp.where(lane == HEADS + 2 * p, one, stats)
            stats = jnp.where(lane == HEADS + 2 * p + 1, two, stats)
        stat_ref[...] = stats
        high = stats.astype(LOW).astype(WIDE)
        rest = pltpu.roll(stats - high, 2 * HEADS, 1)
        flipped = jnp.transpose(jnp.where(lane < 2 * HEADS, high, rest))
        tail = flipped[16:24, :]
        msg_ref[T : T + 16, 0:T] = flipped[0:16, :].astype(LOW)
        msg_ref[T : T + 16, T:] = jnp.concatenate(
            [tail[:, :LANES], tail[:, LANES:]], axis=0
        ).astype(LOW)

        vec_ref[...] = jnp.zeros(vec_ref.shape, WIDE)
        vec_ref[0:1, :D] = column_sum(up * branch_two)
        vec_ref[1:2, :D] = column_sum(gbt.astype(WIDE))
        vec_ref[2:3, :] = column_sum(gpre.astype(WIDE))
        vec_ref[3:4, :D] = column_sum(gn2 * n2)
        vec_ref[4:5, :D] = column_sum(gn2)
        vec_ref[5:6, :D] = column_sum(gmid * branch_one)
        vec_ref[6:7, :D] = column_sum(gbo.astype(WIDE))
        for i, (buf, ref) in enumerate(saved):
            block_copies(buf, ref, ksem.at[i], lo, hi, True)
        for save in saves:
            save.wait()

    return kernel


def fold(dest, row, left, right, width):
    wide = width // LANES
    height = left.shape[1]
    for i in range(0, height, 384):
        part = dot(left[:, i : i + 384], right[...], TN)
        for j in range(wide):
            dest[pl.ds(row + i * wide + j, 384, stride=wide), :] = part[
                :, LANES * j : LANES * (j + 1)
            ]


def query_kernel(plan):
    T = plan.tokens
    part = plan.part
    pairs = HEADS // 2

    def kernel(
        table,
        q_ref,
        k_ref,
        v_ref,
        msg_ref,
        stat_ref,
        col_ref,
        row_ref,
        gq_ref,
        logs,
        dots,
        accs,
        k_buf,
        v_buf,
        ksem,
        vsem,
    ):
        lo = table[plan.low_at()]
        hi = table[plan.low_at() + 1]
        block_copies(k_ref, k_buf, ksem, lo, hi, False)
        block_copies(v_ref, v_buf, vsem, lo, hi, False)
        qs = [halves(q_ref[:, LANES * p : LANES * (p + 1)]) for p in range(pairs)]
        gs = [halves(msg_ref[0:T, LANES * p : LANES * (p + 1)]) for p in range(pairs)]
        ids = tiled(col_ref[...], T)
        for p in range(pairs):
            for k in range(2):
                for c in range(2):
                    rows = slice(part * c, part * (c + 1))
                    to = slice(part * (2 * c + k), part * (2 * c + k + 1))
                    h = 2 * p + k
                    logs[p, to, :] = jnp.broadcast_to(stat_ref[rows, h : h + 1], (part, LANES))
                    h = h + HEADS
                    dots[p, to, :] = jnp.broadcast_to(stat_ref[rows, h : h + 1], (part, LANES))
            accs[p] = jnp.zeros((2 * T, LANES), WIDE)
        block_copies(k_ref, k_buf, ksem, lo, hi, True)
        block_copies(v_ref, v_buf, vsem, lo, hi, True)

        def step(w, rows):
            seen = ids[rows] == row_ref[pl.ds(w, 1), :]
            for p in range(pairs):
                cols = slice(LANES * p, LANES * (p + 1))
                key = k_buf[w, :, cols]
                s = jnp.where(seen, dot(qs[p][rows], key, NT), MASKED)
                prob = jnp.exp(s - jnp.concatenate([logs[p, rows, :]] * (T // LANES), axis=1))
                inner = jnp.concatenate([dots[p, rows, :]] * (T // LANES), axis=1)
                grad = prob * (dot(gs[p][rows], v_buf[w, :, cols], NT) - inner)
                accs[p, rows, :] = accs[p, rows, :] + dot(grad.astype(LOW), key, NN)

        sweep(plan, table, step)
        for p in range(pairs):
            gq_ref[:, LANES * p : LANES * (p + 1)] = (whole(accs[p]) * SCALE).astype(LOW)

    return kernel


def weight_kernel(plan):
    base = AT["out"]
    half = plan.count // 2

    def kernel(
        table,
        norm_ref,
        triple_ref,
        par_ref,
        act_ref,
        pre_ref,
        gbt_ref,
        n2_ref,
        att_ref,
        gbo_ref,
        vec_ref,
        q_ref,
        keep_ref,
        away_ref,
        tail_ref,
        flat,
        stage,
        n_buf,
        q_buf,
        nsem,
        qsem,
        ssem,
    ):
        lo = table[plan.low_at()]
        hi = table[plan.low_at() + 1]
        block_copies(norm_ref, n_buf, nsem, lo, hi, False)
        fold(flat, AT["down"] - base, act_ref, gbt_ref, D)
        fold(flat, AT["up"] - base, n2_ref, pre_ref, FF)
        fold(flat, AT["out"] - base, att_ref, gbo_ref, D)
        put_vector(flat, AT["scale2"] - base, vec_ref[0:1, :D])
        put_vector(flat, AT["dbias"] - base, vec_ref[1:2, :D])
        put_vector(flat, AT["ubias"] - base, vec_ref[2:3, :])
        put_vector(flat, AT["gain2"] - base, vec_ref[3:4, :D])
        put_vector(flat, AT["shift2"] - base, vec_ref[4:5, :D])
        put_vector(flat, AT["scale1"] - base, vec_ref[5:6, :D])
        put_vector(flat, AT["obias"] - base, vec_ref[6:7, :D])
        end = ALL_ROWS - base
        flat[end:, :] = jnp.zeros((flat.shape[0] - end, LANES), WIDE)
        tail_ref[...] = flat[0 : plan.rows, :]

        def put(e, wait):
            t = table[e]
            i = e - plan.first_late

            @pl.when(t < half)
            def _():
                c = pltpu.make_async_copy(stage.at[i], keep_ref.at[t], ssem.at[i])
                c.wait() if wait else c.start()

            @pl.when(t >= half)
            def _():
                c = pltpu.make_async_copy(stage.at[i], away_ref.at[t - half], ssem.at[i])
                c.wait() if wait else c.start()

        for e in range(plan.first_late, plan.count):
            r0 = plan.start[e] - base
            stage[e - plan.first_late] = flat[r0 : r0 + plan.rows, :].astype(LOW)
            put(e, False)

        bias = par_ref[VEC["tbias"] : VEC["tbias"] + 1, :D]
        block_copies(norm_ref, n_buf, nsem, lo, hi, True)

        def project(w, carry):
            q_buf[w] = scaled_query(n_buf[w], triple_ref[:, :D], bias)
            pltpu.make_async_copy(q_buf.at[w], q_ref.at[w], qsem.at[w]).start()
            return carry

        lax.fori_loop(lo, hi + 1, project, 0)
        block_copies(q_buf, q_ref, qsem, lo, hi, True)

        def finish(e, carry):
            put(e, True)
            return carry

        lax.fori_loop(plan.first_late, plan.count, finish, 0)

    return kernel


def last_kernel(plan, sources):
    T = plan.tokens
    early = plan.first_late
    half = plan.count // 2
    part = plan.part
    pairs = HEADS // 2

    def kernel(table, *refs):
        wins = refs[:sources]
        (
            q_ref,
            k_ref,
            v_ref,
            col_ref,
            row_ref,
            gq_ref,
            normed_ref,
            triple_any,
            x_ref,
            mid_ref,
            par_ref,
            tail_ref,
            _,
            _,
            grad_ref,
            keep_ref,
            away_ref,
        ) = refs[sources : sources + 17]
        mwin, q_buf, triple_ref, flat, gt, stage, stats, spare, acck, accv, msem, qsem, tsem, osem = refs[
            sources + 17 :
        ]
        lo = table[plan.low_at()]
        hi = table[plan.low_at() + 1]
        fetch_window(plan, table, wins, mwin, msem, lo, hi, False)
        block_copies(q_ref, q_buf, qsem, lo, hi, False)
        load = launch(triple_any, triple_ref, tsem.at[0])
        ks = [halves(k_ref[:, LANES * p : LANES * (p + 1)]) for p in range(pairs)]
        vs = [halves(v_ref[:, LANES * p : LANES * (p + 1)]) for p in range(pairs)]
        ids = tiled(col_ref[...], T)
        for p in range(pairs):
            acck[p] = jnp.zeros((2 * T, LANES), WIDE)
            accv[p] = jnp.zeros((2 * T, LANES), WIDE)
        fetch_window(plan, table, wins, mwin, msem, lo, hi, True)
        block_copies(q_ref, q_buf, qsem, lo, hi, True)

        def unpack(w, carry):
            got = mwin[w, T : T + 16, :].astype(WIDE)
            spare[0:16, :] = got[:, :T]
            spare[16:24, :] = jnp.concatenate([got[:8, T:], got[8:, T:]], axis=1)
            stats[w, 0 : 2 * HEADS, :] = spare[0 : 2 * HEADS, :] + spare[2 * HEADS : 4 * HEADS, :]
            return carry

        lax.fori_loop(lo, hi + 1, unpack, 0)

        def step(w, rows):
            seen = ids[rows] == row_ref[pl.ds(w, 1), :]
            copies = (rows.stop - rows.start) // (2 * part)

            def pair_rows(h):
                two = [jnp.broadcast_to(stats[w, h + k : h + k + 1, :], (part, T)) for k in range(2)]
                return jnp.concatenate(two * copies, axis=0)

            for p in range(pairs):
                cols = slice(LANES * p, LANES * (p + 1))
                q = q_buf[w, :, cols]
                g = mwin[w, 0:T, cols]
                s = jnp.where(seen, dot(ks[p][rows], q, NT), MASKED)
                prob = jnp.exp(s - pair_rows(2 * p))
                grad = prob * (dot(vs[p][rows], g, NT) - pair_rows(HEADS + 2 * p))
                acck[p, rows, :] = acck[p, rows, :] + dot(grad.astype(LOW), q, NN)
                accv[p, rows, :] = accv[p, rows, :] + dot(prob.astype(LOW), g, NN)

        sweep(plan, table, step)
        for p in range(pairs):
            gt[:, D + LANES * p : D + LANES * (p + 1)] = whole(acck[p]).astype(LOW)
            gt[:, 2 * D + LANES * p : 2 * D + LANES * (p + 1)] = whole(accv[p]).astype(LOW)
        gt[:, :D] = gq_ref[...]
        fold(flat, AT["triple"], normed_ref, gt, 3 * D)
        put_vector(flat, AT["tbias"], column_sum(gt[:, :D].astype(WIDE)))
        put_vector(flat, AT["tbias"] + D // LANES, column_sum(gt[:, 2 * D :].astype(WIDE)))
        load.wait()
        gn = dot(gt[...], triple_ref[...], NT)
        n, r = normalized(x_ref[...].astype(WIDE))
        put_vector(flat, AT["gain1"], column_sum(gn * n))
        put_vector(flat, AT["shift1"], column_sum(gn))
        flat[AT["out"] : AT["out"] + plan.rows, :] = tail_ref[...]

        def put(e, wait):
            t = table[e]

            @pl.when(t < half)
            def _():
                c = pltpu.make_async_copy(stage.at[e], keep_ref.at[t], osem.at[e])
                c.wait() if wait else c.start()

            @pl.when(t >= half)
            def _():
                c = pltpu.make_async_copy(stage.at[e], away_ref.at[t - half], osem.at[e])
                c.wait() if wait else c.start()

        for e in range(early):
            r0 = plan.start[e]
            stage[e] = flat[r0 : r0 + plan.rows, :].astype(LOW)
            put(e, False)
        gain1 = par_ref[VEC["gain1"] : VEC["gain1"] + 1, :D]
        grad_ref[...] = mid_ref[...] + norm_back(gn, gain1, n, r)
        for e in range(early):
            put(e, True)

    return kernel


def shape(dims, kind):
    return jax.ShapeDtypeStruct(dims, kind)


SMEM = pl.BlockSpec(memory_space=pltpu.SMEM)
VMEM = pl.BlockSpec(memory_space=pltpu.VMEM)
ANY = pl.BlockSpec(memory_space=pl.ANY)


def build(plan):
    T = plan.tokens
    W = plan.window
    R = plan.rows
    N = plan.count
    limit = pltpu.CompilerParams(vmem_limit_bytes=60 * 1024 * 1024)

    def per_device(inputs, cotangent, master, first_moment, second_moment, image_ids, spans):
        device = lax.axis_index(BOTH).astype(jnp.int32)
        shift = ((device * plan.share) % LANES).reshape(1).astype(jnp.int32)
        shifted = pl.pallas_call(
            shift_kernel(plan),
            in_specs=[SMEM, VMEM],
            out_specs=VMEM,
            out_shape=shape((R, LANES), LOW),
            scratch_shapes=[pltpu.VMEM((R + 8, LANES), WIDE)],
            name="shift",
        )(shift, jnp.pad(master, (0, R * LANES - plan.share)).reshape(R, LANES))
        near, core, (image_ids, spans) = plan.spread(shifted, (image_ids, spans))
        padded = jnp.pad(image_ids, (plan.reach * T, plan.reach * T), constant_values=-1)
        key_ids = lax.dynamic_slice_in_dim(padded, device * T, W * T, 0).reshape(W, T)
        table = plan.table(device, spans, key_ids)
        own_ids = key_ids[plan.reach]
        columns = jnp.broadcast_to(own_ids[:, None], (T, LANES))
        wins = plan.exchange(inputs)
        sources = len(wins)

        half = pltpu.VMEM((HEADS // 2, 2 * T, LANES), WIDE)
        unpack = pl.pallas_call(
            unpack_kernel(plan),
            in_specs=[SMEM, ANY, ANY],
            out_specs=[ANY] * 4 + [VMEM],
            out_shape=[
                shape((D, 3 * D), LOW),
                shape((D, D), LOW),
                shape((D, FF), LOW),
                shape((FF, D), LOW),
                shape((16, FF), WIDE),
            ],
            scratch_shapes=[
                pltpu.VMEM((N, R, LANES), LOW),
                pltpu.VMEM((plan.flat_rows, LANES), WIDE),
                pltpu.VMEM((D, 3 * D), LOW),
                pltpu.VMEM((D, D), LOW),
                pltpu.VMEM((D, FF), LOW),
                pltpu.VMEM((FF, D), LOW),
                pltpu.SemaphoreType.DMA((N,)),
                pltpu.SemaphoreType.DMA((4,)),
            ],
            compiler_params=limit,
            name="unpack",
        )
        triple, wo, wup, wdn, params = unpack(table, near, core)

        outs = pl.pallas_call(
            forward_kernel(plan, sources),
            in_specs=[SMEM] + [ANY] * sources + [VMEM] + [ANY] * 3 + [VMEM] * 4,
            out_specs=[VMEM] * 3 + [ANY] * 3 + [VMEM] * 2 + [ANY] * 2 + [VMEM] * 8,
            out_shape=[
                shape((T, D), LOW),
                shape((T + 16, D), LOW),
                shape((T, D), LOW),
                shape((W, T, D), LOW),
                shape((W, T, D), LOW),
                shape((W, T, D), LOW),
                shape((T, D), LOW),
                shape((T, D), WIDE),
                shape((T, FF), LOW),
                shape((T, FF), LOW),
                shape((T, D), LOW),
                shape((T, D), LOW),
                shape((T, D), LOW),
                shape((T, D), LOW),
                shape((8, FF), WIDE),
                shape((T, LANES), WIDE),
                shape((T, D), LOW),
                shape((T, D), LOW),
            ],
            scratch_shapes=[
                pltpu.VMEM((W, T, D), LOW),
                pltpu.VMEM((W, T, D), LOW),
                pltpu.VMEM((W, T, D), LOW),
                pltpu.VMEM((W, T, D), LOW),
                pltpu.VMEM((HEADS // 2, W, 2 * T, T), WIDE),
                half,
                half,
                half,
                pltpu.VMEM((T, D), WIDE),
                pltpu.VMEM((D, D), LOW),
                pltpu.VMEM((D, FF), LOW),
                pltpu.VMEM((FF, D), LOW),
                pltpu.VMEM((T, FF), LOW),
                pltpu.VMEM((T, FF), LOW),
                pltpu.SemaphoreType.DMA((W,)),
                pltpu.SemaphoreType.DMA((3, W)),
                pltpu.SemaphoreType.DMA((5,)),
            ],
            compiler_params=limit,
            name="forward",
        )(table, *wins, triple, wo, wup, wdn, params, cotangent, columns, key_ids)
        (
            result,
            message,
            q,
            k,
            v,
            norms,
            normed,
            gmid,
            act,
            gpre,
            gbt,
            n2,
            att,
            gbo,
            vec,
            stat,
            k_own,
            v_own,
        ) = outs
        messages = plan.exchange(message)

        query_call = pl.pallas_call(
            query_kernel(plan),
            in_specs=[SMEM, VMEM, ANY, ANY] + [VMEM] * 4,
            out_specs=VMEM,
            out_shape=shape((T, D), LOW),
            scratch_shapes=[
                half,
                half,
                half,
                pltpu.VMEM((W, T, D), LOW),
                pltpu.VMEM((W, T, D), LOW),
                pltpu.SemaphoreType.DMA((W,)),
                pltpu.SemaphoreType.DMA((W,)),
            ],
            compiler_params=limit,
            name="query",
        )
        gq = query_call(table, q, k, v, message, stat, columns, key_ids)
        weight_call = pl.pallas_call(
            weight_kernel(plan),
            in_specs=[SMEM, ANY] + [VMEM] * 9,
            out_specs=[ANY] * 3 + [VMEM],
            out_shape=[
                shape((W, T, D), LOW),
                shape((N // 2, R, LANES), LOW),
                shape((N // 2, R, LANES), LOW),
                shape((R, LANES), WIDE),
            ],
            scratch_shapes=[
                pltpu.VMEM((plan.flat_rows - AT["out"] + 8, LANES), WIDE),
                pltpu.VMEM((N - plan.first_late, R, LANES), LOW),
                pltpu.VMEM((W, T, D), LOW),
                pltpu.VMEM((W, T, D), LOW),
                pltpu.SemaphoreType.DMA((W,)),
                pltpu.SemaphoreType.DMA((W,)),
                pltpu.SemaphoreType.DMA((N - plan.first_late,)),
            ],
            compiler_params=limit,
            name="weight",
        )
        queries, keep, away, tail = weight_call(
            table, norms, triple, params, act, gpre, gbt, n2, att, gbo, vec
        )

        late = plan.first_late
        input_grad, keep, away = pl.pallas_call(
            last_kernel(plan, sources),
            in_specs=[SMEM] + [ANY] * (sources + 1) + [VMEM] * 6 + [ANY] + [VMEM] * 4 + [ANY, ANY],
            out_specs=[VMEM, ANY, ANY],
            out_shape=[
                shape((T, D), WIDE),
                shape((N // 2, R, LANES), LOW),
                shape((N // 2, R, LANES), LOW),
            ],
            scratch_shapes=[
                pltpu.VMEM((W, T + 16, D), LOW),
                pltpu.VMEM((W, T, D), LOW),
                pltpu.VMEM((D, 3 * D), LOW),
                pltpu.VMEM((AT["out"] + R + 8, LANES), WIDE),
                pltpu.VMEM((T, 3 * D), LOW),
                pltpu.VMEM((late, R, LANES), LOW),
                pltpu.VMEM((W, 16, T), WIDE),
                pltpu.VMEM((24, T), WIDE),
                half,
                half,
                pltpu.SemaphoreType.DMA((W,)),
                pltpu.SemaphoreType.DMA((W,)),
                pltpu.SemaphoreType.DMA((1,)),
                pltpu.SemaphoreType.DMA((late,)),
            ],
            input_output_aliases={13 + sources: 1, 14 + sources: 2},
            compiler_params=limit,
            name="last",
        )(
            table,
            *messages,
            queries,
            k_own,
            v_own,
            columns,
            key_ids,
            gq,
            normed,
            triple,
            inputs,
            gmid,
            params,
            tail,
            keep,
            away,
        )

        parts = plan.reduce_parts(keep, away)
        grad, square = pl.pallas_call(
            unshift_kernel(plan),
            in_specs=[SMEM] + [VMEM] * len(parts),
            out_specs=[VMEM, VMEM],
            out_shape=[shape((R, LANES), WIDE), shape((N, LANES), WIDE)],
            scratch_shapes=[pltpu.VMEM((R + 8, LANES), WIDE)],
            name="unshift",
        )(shift, *parts)
        grad_shard = grad.reshape(-1)[: plan.share]
        squares = lax.all_to_all(square, BOTH, 0, 0, tiled=True)
        grad_norm = jnp.sqrt(jnp.sum(squares[:, 0]))
        ceiling = CLIP_RATIO * math.sqrt(plan.share * N)
        factor = ceiling / jnp.maximum(grad_norm, ceiling)
        clipped = grad_shard * factor
        new_first = BETA_ONE * first_moment + (1.0 - BETA_ONE) * clipped
        new_second = BETA_TWO * second_moment + (1.0 - BETA_TWO) * clipped * clipped
        new_master = master - LEARN_RATE * (
            new_first / (jnp.sqrt(new_second) + ADAM_EPS) + WEIGHT_DECAY * master
        )
        return (
            result,
            input_grad,
            grad_shard,
            grad_norm.reshape(1),
            new_first,
            new_second,
            new_master,
        )

    return per_device


def solution(mesh):
    dp = mesh.shape["dp"]
    fsdp = mesh.shape["fsdp"]
    row = P(BOTH, None)
    flat = P(BOTH)
    in_specs = (row, row, flat, flat, flat, P(), P())
    out_specs = (row, row, flat, P(), flat, flat, flat)

    def per_device(*args):
        inputs, master = args[0], args[2]
        plan = Plan(dp, fsdp, master.shape[0], inputs.shape[0])
        return build(plan)(*args)

    return jax.shard_map(
        per_device, mesh=mesh, in_specs=in_specs, out_specs=out_specs, check_vma=False
    )
```

```python
import math

import jax
import jax.numpy as jnp
from jax import lax
from jax.experimental import pallas as pl
from jax.experimental.pallas import tpu as pltpu
from jax.sharding import PartitionSpec as P


D = 384
HEADS = 6
HEAD_DIM = 64
FF = 1536
IMG = 1370
LANES = 128

LN_EPS = 1e-06
BETA_ONE = 0.5
BETA_TWO = 0.6
LEARN_RATE = 0.01
WEIGHT_DECAY = 0.05
ADAM_EPS = 1e-08
CLIP_RATIO = 0.25
MASKED = -1e30
BOTH = ("dp", "fsdp")
LOW = jnp.bfloat16
WIDE = jnp.float32
SCALE = HEAD_DIM ** (-0.5)

NT = (((1,), (1,)), ((), ()))
NN = (((1,), (0,)), ((), ()))
TN = (((0,), (0,)), ((), ()))

PIECES = [
    ("gain1", D),
    ("shift1", D),
    ("triple", 3 * D * D),
    ("tbias", 2 * D),
    ("out", D * D),
    ("obias", D),
    ("scale1", D),
    ("gain2", D),
    ("shift2", D),
    ("up", D * FF),
    ("ubias", FF),
    ("down", FF * D),
    ("dbias", D),
    ("scale2", D),
]
AT = {}
_row = 0
for _name, _count in PIECES:
    AT[_name] = _row
    _row += _count // LANES
ALL_ROWS = _row


def dot(a, b, dims):
    return lax.dot_general(a, b, dims, preferred_element_type=WIDE)


class Plan:
    def __init__(self, dp, fsdp, share, tokens):
        self.count = dp * fsdp
        self.share = share
        self.rows = -(-(2 * (LANES - 1) + share) // LANES)
        self.rows = -(-self.rows // 16) * 16
        self.cut = self.rows * 11 // 16 // 16 * 16
        self.start = [e * share // LANES for e in range(self.count)]
        self.tokens = tokens
        self.part = tokens // 2
        self.reach = (IMG - 2 + tokens) // tokens
        self.window = 2 * self.reach + 1
        self.grouped = dp == 4 and fsdp == 8 and self.reach <= 6
        if self.grouped:
            self.stages = [[2, 4, 6], [16, 1, 17], [8]]
        else:
            bits = [1 << k for k in range(self.count.bit_length() - 1)]
            bits = [b for b in bits if b != fsdp] + [fsdp]
            self.stages = [[b] for b in bits]
        masks = [0]
        for stage in self.stages:
            masks = masks + [m ^ s for s in stage for m in masks]
        self.bits = [masks[1 << k] for k in range(self.count.bit_length() - 1)]
        self.first_late = next(e for e in range(self.count) if self.start[e] >= AT["out"])
        self.flat_rows = -(-(self.start[-1] + self.rows) // 8) * 8

    def send(self, x, mask):
        return lax.ppermute(x, BOTH, [(i, i ^ mask) for i in range(self.count)])

    def spread(self, own, extra):
        buf = own[None]
        for level, stage in enumerate(self.stages[:-1]):
            parts = [buf]
            for m in stage:
                parts.append(self.send(buf, m))
            buf = jnp.concatenate(parts, axis=0)
            if level == 0:
                buf, extra = lax.optimization_barrier((buf, extra))
        core = self.send(buf, self.stages[-1][0])
        return buf, core, extra

    def reduce_parts(self, keep, away):
        def added(parts):
            total = parts[0].astype(WIDE)
            for part in parts[1:]:
                total = total + part.astype(WIDE)
            return total.astype(LOW)

        def one(pieces, level):
            parts = [pieces[0]]
            for k, m in enumerate(self.stages[level]):
                parts.append(self.send(pieces[k + 1], m))
            return parts

        got = [keep, self.send(away, self.stages[-1][0])]
        if self.grouped:
            wide, deep = len(self.stages[1]) + 1, len(self.stages[0]) + 1
            got = [x.reshape((wide, deep) + x.shape[1:]) for x in got]
            lead = [added([x[k, :, : self.cut] for x in got]) for k in range(wide)]
            rest = [added([x[:, k, self.cut :] for x in got]) for k in range(deep)]
            lead = one(lead, 1)
            rest = one(rest, 0)
            lead = [added([x[k] for x in lead]) for k in range(deep)]
            rest = [added([x[k] for x in rest]) for k in range(wide)]
            return one(lead, 0) + one(rest, 1)
        for level in reversed(range(len(self.stages) - 1)):
            count = len(self.stages[level]) + 1
            got = [x.reshape((count, -1) + x.shape[1:]) for x in got]
            got = one([added([x[k] for x in got]) for k in range(count)], level)
        return [part[0] for part in got]

    def exchange(self, block):
        own = block[None]
        if self.grouped:
            hops = []
            for m in (1, 2, 3, 4, 6):
                hops.append(self.send(own, m))
            one, two, three, four, six = hops
            pair = jnp.concatenate([four, six], axis=0)
            quad = jnp.concatenate([two, three, four, six], axis=0)
            pair, quad = lax.optimization_barrier((pair, quad))
            across = [(8 + j, 16 + j) for j in range(6)] + [(16 + j, 8 + j) for j in range(2, 8)]
            skew = [(8 + j, 16 + (j ^ 1)) for j in range(4)]
            skew += [(16 + j, 8 + (j ^ 1)) for j in range(4, 8)]
            far = lax.ppermute(quad, BOTH, across)
            far_beside = lax.ppermute(pair, BOTH, skew)
            beside = self.send(pair, 1)
            home = self.send(quad, 8)
            home_beside = self.send(beside, 8)
            return [own, one, quad, beside, home, home_beside, far, far_beside]
        slots = []
        for slot in range(self.window):
            by = self.reach - slot
            pairs = [(i, i + by) for i in range(self.count) if 0 <= i + by < self.count]
            slots.append(own if by == 0 else lax.ppermute(own, BOTH, pairs))
        return [jnp.concatenate(slots, axis=0)]

    def table(self, device, spans, key_ids):
        e = jnp.arange(self.count, dtype=jnp.int32)
        rel = e ^ device
        where = jnp.zeros_like(e)
        for k, bit in enumerate(self.bits):
            where = where + jnp.where((rel & bit) != 0, 1 << k, 0)
        slot = jnp.arange(self.window, dtype=jnp.int32)
        if self.grouped:
            other = device - self.reach + slot
            mask = (other ^ device) & 7
            late = (mask == 5) | (mask == 7)
            index = jnp.where(late, mask >> 2 & mask >> 1, jnp.where(mask == 6, 3, mask - 2))
            index = jnp.where(mask < 2, 0, index)
            group = jnp.where(mask < 2, mask, jnp.where(late, 3, 2))
            cross = (other >> 3) ^ (device >> 3)
            source = group + jnp.where(cross == 0, 0, jnp.where(cross == 1, 2, 4))
        else:
            source = jnp.zeros_like(slot)
            index = slot
        bounds = lax.dynamic_index_in_dim(spans, device, 0, keepdims=False)
        ends = jnp.clip(bounds - device + self.reach, 0, self.window - 1)
        own = key_ids[self.reach]
        low, high = own[:: self.part], own[self.part - 1 :: self.part]
        seen = (key_ids[:, -1][None] >= low[:, None]) & (key_ids[:, 0][None] <= high[:, None])
        seen = seen & (slot >= ends[0])[None] & (slot <= ends[1])[None]
        begin = jnp.min(jnp.where(seen, slot[None], self.window), axis=1)
        finish = jnp.max(jnp.where(seen, slot[None], -1), axis=1)
        return jnp.concatenate([where, source, index, ends, begin, finish]).astype(jnp.int32)

    def source_at(self, slot):
        return self.count + slot

    def index_at(self, slot):
        return self.count + self.window + slot

    def low_at(self):
        return self.count + 2 * self.window

    def range_at(self, quarter):
        at = self.count + 2 * self.window + 2 + quarter
        return at, at + self.tokens // self.part


def fetch_window(plan, table, sources, dest, sems, lo, hi, wait):
    def step(slot, carry):
        if wait:
            pltpu.make_async_copy(sources[0].at[0], dest.at[slot], sems.at[slot]).wait()
            return carry
        for k, source in enumerate(sources):

            @pl.when(table[plan.source_at(slot)] == k)
            def _(source=source):
                copy = pltpu.make_async_copy(
                    source.at[table[plan.index_at(slot)]], dest.at[slot], sems.at[slot]
                )
                copy.start()

        return carry

    lax.fori_loop(lo, hi + 1, step, 0)


def normalized(x):
    center = x - jnp.mean(x, axis=-1, keepdims=True)
    spread = jnp.mean(center * center, axis=-1, keepdims=True)
    r = lax.rsqrt(spread + LN_EPS)
    return center * r, r


def norm_back(grad, gain, n, r):
    g = grad * gain
    inner = jnp.mean(g, axis=-1, keepdims=True)
    outer = jnp.mean(g * n, axis=-1, keepdims=True)
    return r * (g - inner - n * outer)


def vector(ref, row, width):
    return jnp.concatenate([ref[row + j : row + j + 1, :] for j in range(width // LANES)], axis=1)


def put_vector(ref, row, value):
    for j in range(value.shape[1] // LANES):
        ref[row + j : row + j + 1, :] = value[:, LANES * j : LANES * (j + 1)]


def stacked(x):
    left = lax.broadcasted_iota(jnp.int32, x.shape, 1) < HEAD_DIM
    return jnp.concatenate([jnp.where(left, x, 0), jnp.where(left, 0, x)], axis=0)


def unstacked(x):
    half = x.shape[0] // 2
    left = lax.broadcasted_iota(jnp.int32, (half, LANES), 1) < HEAD_DIM
    return jnp.where(left, x[:half], x[half:])


def halves(x):
    part = x.shape[0] // 2
    return jnp.concatenate([stacked(x[:part]), stacked(x[part:])], axis=0)


def whole(x):
    part = x.shape[0] // 2
    return jnp.concatenate([unstacked(x[:part]), unstacked(x[part:])], axis=0)


def tiled(ids, width):
    part = ids.shape[0] // 2
    ids = jnp.concatenate([ids] * (width // LANES), axis=1)
    return jnp.concatenate([ids[:part], ids[:part], ids[part:], ids[part:]], axis=0)


def sweep(plan, table, body):
    (a, b), (c, d) = plan.range_at(0), plan.range_at(1)
    rows = 2 * plan.part

    def loop(begin, finish, rows):
        def step(w, carry):
            body(w, rows)
            return carry

        lax.fori_loop(begin, finish, step, 0)

    loop(table[a], table[c], slice(0, rows))
    loop(table[c], table[b] + 1, slice(0, 2 * rows))
    loop(table[b] + 1, table[d] + 1, slice(rows, 2 * rows))


def launch(source, dest, sem):
    copy = pltpu.make_async_copy(source, dest, sem)
    copy.start()
    return copy


def block_copies(source, dest, sems, lo, hi, wait):
    def step(slot, carry):
        copy = pltpu.make_async_copy(source.at[slot], dest.at[slot], sems.at[slot])
        copy.wait() if wait else copy.start()
        return carry

    lax.fori_loop(lo, hi + 1, step, 0)


def scaled_query(low, weight, bias):
    q = dot(low, weight, NN) + bias
    return (q.astype(LOW).astype(WIDE) * SCALE).astype(LOW)


def column_sum(x):
    return jnp.sum(x, axis=0, keepdims=True)


def shift_kernel(plan):
    def kernel(table, x_ref, out_ref, pad):
        s = table[0]
        x = x_ref[...]
        y = pltpu.roll(x, s, 1)
        pad[0:8, :] = jnp.zeros((8, LANES), WIDE)
        pad[8:, :] = y
        lane = lax.broadcasted_iota(jnp.int32, y.shape, 1)
        out_ref[...] = jnp.where(lane >= s, y, pad[7 : 7 + plan.rows, :]).astype(LOW)

    return kernel


def unshift_kernel(plan):
    def kernel(table, *refs):
        parts, (out_ref, sq_ref, pad) = refs[:-3], refs[-3:]
        s = table[0]

        def total(parts):
            got = [p[...].astype(WIDE) for p in parts]
            while len(got) > 1:
                got = [got[k] + got[k + 1] for k in range(0, len(got), 2)]
            return got[0]

        if plan.grouped:
            lead = len(plan.stages[0]) + 1
            y = jnp.concatenate([total(parts[:lead]), total(parts[lead:])], axis=0)
        else:
            y = total(parts)
        y = pltpu.roll(y, LANES - s, 1)
        pad[0 : plan.rows, :] = y
        pad[plan.rows :, :] = jnp.zeros((8, LANES), WIDE)
        lane = lax.broadcasted_iota(jnp.int32, y.shape, 1)
        row = lax.broadcasted_iota(jnp.int32, y.shape, 0)
        out = jnp.where(lane < LANES - s, y, pad[1 : 1 + plan.rows, :])
        out = jnp.where(row * LANES + lane < plan.share, out, 0.0)
        out_ref[...] = out
        sq = jnp.sum(jnp.sum(out * out, axis=0, keepdims=True), axis=1, keepdims=True)
        sq_ref[...] = jnp.broadcast_to(sq, (plan.count, LANES))

    return kernel


VEC = {"gain1": 0, "shift1": 1, "tbias": 2, "obias": 3, "scale1": 4, "gain2": 5, "shift2": 6}
VEC.update({"ubias": 7, "dbias": 8, "scale2": 9})


def unpack_kernel(plan):
    half = plan.count // 2

    def kernel(
        table,
        near,
        core,
        triple_ref,
        wo_ref,
        wup_ref,
        wdn_ref,
        vec_ref,
        wbuf,
        flat,
        triple,
        wo,
        wup,
        wdn,
        wsem,
        osem,
    ):
        def weight_copy(e, wait):
            t = table[e]

            @pl.when(t < half)
            def _():
                c = pltpu.make_async_copy(near.at[t], wbuf.at[e], wsem.at[e])
                c.wait() if wait else c.start()

            @pl.when(t >= half)
            def _():
                c = pltpu.make_async_copy(core.at[t - half], wbuf.at[e], wsem.at[e])
                c.wait() if wait else c.start()

        def start_one(e, carry):
            weight_copy(e, False)
            return carry

        lax.fori_loop(0, plan.count, start_one, 0)
        for e in range(plan.count):
            weight_copy(e, True)
            r0 = plan.start[e]
            block = wbuf[e].astype(WIDE)
            if e:
                before = flat[r0 : r0 + 1, :]
                flat[r0 : r0 + plan.rows, :] = block
                flat[r0 : r0 + 1, :] = before + block[0:1, :]
            else:
                flat[r0 : r0 + plan.rows, :] = block

        def unfold(dest, name, height, width):
            wide = width // LANES
            step = min(height, 384)
            for j in range(wide):
                for i in range(0, height, step):
                    dest[i : i + step, LANES * j : LANES * (j + 1)] = flat[
                        pl.ds(AT[name] + i * wide + j, step, stride=wide), :
                    ].astype(LOW)

        unfold(wup, "up", D, FF)
        saves = [launch(wup, wup_ref, osem.at[0])]
        unfold(wdn, "down", FF, D)
        saves.append(launch(wdn, wdn_ref, osem.at[1]))
        unfold(triple, "triple", D, 3 * D)
        saves.append(launch(triple, triple_ref, osem.at[2]))
        unfold(wo, "out", D, D)
        saves.append(launch(wo, wo_ref, osem.at[3]))
        vec_ref[...] = jnp.zeros(vec_ref.shape, WIDE)
        for name, row in VEC.items():
            width = dict(PIECES)[name]
            vec_ref[row : row + 1, :width] = vector(flat, AT[name], width)
        for save in saves:
            save.wait()

    return kernel


def forward_kernel(plan, sources):
    T = plan.tokens
    own = plan.reach
    part = plan.part
    pairs = HEADS // 2

    def kernel(table, *refs):
        wins = refs[:sources]
        triple_ref, wo_ref, wup_ref, wdn_ref, par_ref, cot_ref, col_ref, row_ref = refs[
            sources : 8 + sources
        ]
        (
            out_ref,
            msg_ref,
            q_ref,
            k_ref,
            v_ref,
            norm_ref,
            normed_ref,
            mid_ref,
            act_ref,
            pre_ref,
            gbt_ref,
            n2_ref,
            att_ref,
            gbo_ref,
            vec_ref,
            stat_ref,
            kown_ref,
            vown_ref,
        ) = refs[8 + sources : 26 + sources]
        xwin, n_buf, k_buf, v_buf, scores, tops, sums, accs, mix = refs[26 + sources : 35 + sources]
        wo, wup, wdn, act_buf, pre_buf, xsem, ksem, osem = refs[35 + sources :]
        lo = table[plan.low_at()]
        hi = table[plan.low_at() + 1]

        def param(name):
            row = VEC[name]
            return par_ref[row : row + 1, : dict(PIECES)[name]]

        fetch_window(plan, table, wins, xwin, xsem, lo, hi, False)
        pairs_in = [(wo_ref, wo), (wup_ref, wup), (wdn_ref, wdn)]
        loads = [launch(a, b, osem.at[i]) for i, (a, b) in enumerate(pairs_in)]
        gain1 = param("gain1")
        shift1 = param("shift1")
        tbias = param("tbias")
        fetch_window(plan, table, wins, xwin, xsem, lo, hi, True)

        saved = [(n_buf, norm_ref), (k_buf, k_ref), (v_buf, v_ref)]

        def project(w, carry):
            n, _ = normalized(xwin[w].astype(WIDE))
            low = (n * gain1 + shift1).astype(LOW)
            n_buf[w] = low
            kv = dot(low, triple_ref[:, D:], NN)
            k_buf[w] = kv[:, :D].astype(LOW)
            v_buf[w] = (kv[:, D:] + tbias[:, D:]).astype(LOW)
            for i, (buf, ref) in enumerate(saved):
                pltpu.make_async_copy(buf.at[w], ref.at[w], ksem.at[i, w]).start()
            return carry

        lax.fori_loop(lo, hi + 1, project, 0)
        kown_ref[...] = k_buf[own]
        vown_ref[...] = v_buf[own]
        low = n_buf[own]
        normed_ref[...] = low
        q_ref[...] = scaled_query(low, triple_ref[:, :D], tbias[:, :D])

        lane = lax.broadcasted_iota(jnp.int32, (T, LANES), 1)
        qs = [halves(q_ref[:, LANES * p : LANES * (p + 1)]) for p in range(pairs)]
        ids = tiled(col_ref[...], T)
        for p in range(pairs):
            tops[p] = jnp.full((2 * T, LANES), MASKED, WIDE)
            sums[p] = jnp.zeros((2 * T, LANES), WIDE)
            accs[p] = jnp.zeros((2 * T, LANES), WIDE)

        def first(w, rows):
            seen = ids[rows] == row_ref[pl.ds(w, 1), :]
            for p in range(pairs):
                s = dot(qs[p][rows], k_buf[w, :, LANES * p : LANES * (p + 1)], NT)
                s = jnp.where(seen, s, MASKED)
                scores[p, w, rows, :] = s
                top = tops[p, rows, :]
                for j in range(0, T, LANES):
                    top = jnp.maximum(top, s[:, j : j + LANES])
                tops[p, rows, :] = top

        sweep(plan, table, first)
        for p in range(pairs):
            top = jnp.max(tops[p], axis=1, keepdims=True)
            tops[p] = jnp.broadcast_to(top, (2 * T, LANES))

        def second(w, rows):
            for p in range(pairs):
                top = jnp.concatenate([tops[p, rows, :]] * (T // LANES), axis=1)
                e = jnp.exp(scores[p, w, rows, :] - top)
                total = sums[p, rows, :]
                for j in range(0, T, LANES):
                    total = total + e[:, j : j + LANES]
                sums[p, rows, :] = total
                value = v_buf[w, :, LANES * p : LANES * (p + 1)]
                accs[p, rows, :] = accs[p, rows, :] + dot(e.astype(LOW), value, NN)

        sweep(plan, table, second)
        stats = jnp.zeros((T, LANES), WIDE)
        for p in range(pairs):
            total = jnp.sum(sums[p], axis=1, keepdims=True)
            mix[:, LANES * p : LANES * (p + 1)] = whole(accs[p] / total)
            log = tops[p] + jnp.log(total)
            for k in range(2):
                at = part * k
                column = jnp.concatenate(
                    [log[at : at + part], log[2 * part + at : 3 * part + at]], axis=0
                )
                stats = jnp.where(lane == 2 * p + k, column, stats)
        att = mix[...]
        for load in loads:
            load.wait()
        att_low = att.astype(LOW)
        att_ref[...] = att_low
        x = xwin[own].astype(WIDE)
        scale1 = param("scale1")
        scale2 = param("scale2")
        gain2 = param("gain2")
        branch_one = dot(att_low, wo[...], NN) + param("obias")
        middle = x + scale1 * branch_one
        n2, r2 = normalized(middle)
        n2_low = (n2 * gain2 + param("shift2")).astype(LOW)
        n2_ref[...] = n2_low
        pre = dot(n2_low, wup[...], NN) + param("ubias")
        cdf = 0.5 * (1.0 + lax.erf(pre * math.sqrt(0.5)))
        act_low = (pre * cdf).astype(LOW)
        act_buf[...] = act_low
        saves = [launch(act_buf, act_ref, osem.at[3])]
        slope = cdf + pre * (jnp.exp(-0.5 * pre * pre) * (1.0 / math.sqrt(2.0 * math.pi)))
        branch_two = dot(act_low, wdn[...], NN) + param("dbias")
        out_ref[...] = (middle + scale2 * branch_two).astype(LOW)

        up = cot_ref[...].astype(WIDE)
        gbt = (scale2 * up).astype(LOW)
        gbt_ref[...] = gbt
        gpre = (dot(gbt, wdn[...], NT) * slope).astype(LOW)
        pre_buf[...] = gpre
        saves.append(launch(pre_buf, pre_ref, osem.at[4]))
        gn2 = dot(gpre, wup[...], NT)
        gmid = up + norm_back(gn2, gain2, n2, r2)
        mid_ref[...] = gmid
        gbo = (scale1 * gmid).astype(LOW)
        gbo_ref[...] = gbo
        gatt = dot(gbo, wo[...], NT).astype(LOW)
        msg_ref[0:T, :] = gatt
        inner = gatt.astype(WIDE) * att
        left = lane < HEAD_DIM
        for p in range(HEADS // 2):
            piece = inner[:, LANES * p : LANES * (p + 1)]
            one = jnp.sum(jnp.where(left, piece, 0.0), axis=1, keepdims=True)
            two = jnp.sum(jnp.where(left, 0.0, piece), axis=1, keepdims=True)
            stats = jnp.where(lane == HEADS + 2 * p, one, stats)
            stats = jnp.where(lane == HEADS + 2 * p + 1, two, stats)
        stat_ref[...] = stats
        high = stats.astype(LOW).astype(WIDE)
        rest = pltpu.roll(stats - high, 2 * HEADS, 1)
        flipped = jnp.transpose(jnp.where(lane < 2 * HEADS, high, rest))
        tail = flipped[16:24, :]
        msg_ref[T : T + 16, 0:T] = flipped[0:16, :].astype(LOW)
        msg_ref[T : T + 16, T:] = jnp.concatenate(
            [tail[:, :LANES], tail[:, LANES:]], axis=0
        ).astype(LOW)

        vec_ref[...] = jnp.zeros(vec_ref.shape, WIDE)
        vec_ref[0:1, :D] = column_sum(up * branch_two)
        vec_ref[1:2, :D] = column_sum(gbt.astype(WIDE))
        vec_ref[2:3, :] = column_sum(gpre.astype(WIDE))
        vec_ref[3:4, :D] = column_sum(gn2 * n2)
        vec_ref[4:5, :D] = column_sum(gn2)
        vec_ref[5:6, :D] = column_sum(gmid * branch_one)
        vec_ref[6:7, :D] = column_sum(gbo.astype(WIDE))
        for i, (buf, ref) in enumerate(saved):
            block_copies(buf, ref, ksem.at[i], lo, hi, True)
        for save in saves:
            save.wait()

    return kernel


def fold(dest, row, left, right, width):
    wide = width // LANES
    height = left.shape[1]
    for i in range(0, height, 384):
        part = dot(left[:, i : i + 384], right[...], TN)
        for j in range(wide):
            dest[pl.ds(row + i * wide + j, 384, stride=wide), :] = part[
                :, LANES * j : LANES * (j + 1)
            ]


def query_kernel(plan):
    T = plan.tokens
    part = plan.part
    pairs = HEADS // 2

    def kernel(
        table,
        q_ref,
        k_ref,
        v_ref,
        msg_ref,
        stat_ref,
        col_ref,
        row_ref,
        gq_ref,
        logs,
        dots,
        accs,
        k_buf,
        v_buf,
        ksem,
        vsem,
    ):
        lo = table[plan.low_at()]
        hi = table[plan.low_at() + 1]
        block_copies(k_ref, k_buf, ksem, lo, hi, False)
        block_copies(v_ref, v_buf, vsem, lo, hi, False)
        qs = [halves(q_ref[:, LANES * p : LANES * (p + 1)]) for p in range(pairs)]
        gs = [halves(msg_ref[0:T, LANES * p : LANES * (p + 1)]) for p in range(pairs)]
        ids = tiled(col_ref[...], T)
        for p in range(pairs):
            for k in range(2):
                for c in range(2):
                    rows = slice(part * c, part * (c + 1))
                    to = slice(part * (2 * c + k), part * (2 * c + k + 1))
                    h = 2 * p + k
                    logs[p, to, :] = jnp.broadcast_to(stat_ref[rows, h : h + 1], (part, LANES))
                    h = h + HEADS
                    dots[p, to, :] = jnp.broadcast_to(stat_ref[rows, h : h + 1], (part, LANES))
            accs[p] = jnp.zeros((2 * T, LANES), WIDE)
        block_copies(k_ref, k_buf, ksem, lo, hi, True)
        block_copies(v_ref, v_buf, vsem, lo, hi, True)

        def step(w, rows):
            seen = ids[rows] == row_ref[pl.ds(w, 1), :]
            for p in range(pairs):
                cols = slice(LANES * p, LANES * (p + 1))
                key = k_buf[w, :, cols]
                s = jnp.where(seen, dot(qs[p][rows], key, NT), MASKED)
                prob = jnp.exp(s - jnp.concatenate([logs[p, rows, :]] * (T // LANES), axis=1))
                inner = jnp.concatenate([dots[p, rows, :]] * (T // LANES), axis=1)
                grad = prob * (dot(gs[p][rows], v_buf[w, :, cols], NT) - inner)
                accs[p, rows, :] = accs[p, rows, :] + dot(grad.astype(LOW), key, NN)

        sweep(plan, table, step)
        for p in range(pairs):
            gq_ref[:, LANES * p : LANES * (p + 1)] = (whole(accs[p]) * SCALE).astype(LOW)

    return kernel


def weight_kernel(plan):
    base = AT["out"]
    half = plan.count // 2

    def kernel(
        table,
        norm_ref,
        triple_ref,
        par_ref,
        act_ref,
        pre_ref,
        gbt_ref,
        n2_ref,
        att_ref,
        gbo_ref,
        vec_ref,
        q_ref,
        keep_ref,
        away_ref,
        tail_ref,
        flat,
        stage,
        n_buf,
        q_buf,
        nsem,
        qsem,
        ssem,
    ):
        lo = table[plan.low_at()]
        hi = table[plan.low_at() + 1]
        block_copies(norm_ref, n_buf, nsem, lo, hi, False)
        fold(flat, AT["down"] - base, act_ref, gbt_ref, D)
        fold(flat, AT["up"] - base, n2_ref, pre_ref, FF)
        fold(flat, AT["out"] - base, att_ref, gbo_ref, D)
        put_vector(flat, AT["scale2"] - base, vec_ref[0:1, :D])
        put_vector(flat, AT["dbias"] - base, vec_ref[1:2, :D])
        put_vector(flat, AT["ubias"] - base, vec_ref[2:3, :])
        put_vector(flat, AT["gain2"] - base, vec_ref[3:4, :D])
        put_vector(flat, AT["shift2"] - base, vec_ref[4:5, :D])
        put_vector(flat, AT["scale1"] - base, vec_ref[5:6, :D])
        put_vector(flat, AT["obias"] - base, vec_ref[6:7, :D])
        end = ALL_ROWS - base
        flat[end:, :] = jnp.zeros((flat.shape[0] - end, LANES), WIDE)
        tail_ref[...] = flat[0 : plan.rows, :]

        def put(e, wait):
            t = table[e]
            i = e - plan.first_late

            @pl.when(t < half)
            def _():
                c = pltpu.make_async_copy(stage.at[i], keep_ref.at[t], ssem.at[i])
                c.wait() if wait else c.start()

            @pl.when(t >= half)
            def _():
                c = pltpu.make_async_copy(stage.at[i], away_ref.at[t - half], ssem.at[i])
                c.wait() if wait else c.start()

        for e in range(plan.first_late, plan.count):
            r0 = plan.start[e] - base
            stage[e - plan.first_late] = flat[r0 : r0 + plan.rows, :].astype(LOW)
            put(e, False)

        bias = par_ref[VEC["tbias"] : VEC["tbias"] + 1, :D]
        block_copies(norm_ref, n_buf, nsem, lo, hi, True)

        def project(w, carry):
            q_buf[w] = scaled_query(n_buf[w], triple_ref[:, :D], bias)
            pltpu.make_async_copy(q_buf.at[w], q_ref.at[w], qsem.at[w]).start()
            return carry

        lax.fori_loop(lo, hi + 1, project, 0)
        block_copies(q_buf, q_ref, qsem, lo, hi, True)

        def finish(e, carry):
            put(e, True)
            return carry

        lax.fori_loop(plan.first_late, plan.count, finish, 0)

    return kernel


def last_kernel(plan, sources):
    T = plan.tokens
    early = plan.first_late
    half = plan.count // 2
    part = plan.part
    pairs = HEADS // 2

    def kernel(table, *refs):
        wins = refs[:sources]
        (
            q_ref,
            k_ref,
            v_ref,
            col_ref,
            row_ref,
            gq_ref,
            normed_ref,
            triple_any,
            x_ref,
            mid_ref,
            par_ref,
            tail_ref,
            _,
            _,
            grad_ref,
            keep_ref,
            away_ref,
        ) = refs[sources : sources + 17]
        mwin, q_buf, triple_ref, flat, gt, stage, stats, spare, acck, accv, msem, qsem, tsem, osem = refs[
            sources + 17 :
        ]
        lo = table[plan.low_at()]
        hi = table[plan.low_at() + 1]
        fetch_window(plan, table, wins, mwin, msem, lo, hi, False)
        block_copies(q_ref, q_buf, qsem, lo, hi, False)
        load = launch(triple_any, triple_ref, tsem.at[0])
        ks = [halves(k_ref[:, LANES * p : LANES * (p + 1)]) for p in range(pairs)]
        vs = [halves(v_ref[:, LANES * p : LANES * (p + 1)]) for p in range(pairs)]
        ids = tiled(col_ref[...], T)
        for p in range(pairs):
            acck[p] = jnp.zeros((2 * T, LANES), WIDE)
            accv[p] = jnp.zeros((2 * T, LANES), WIDE)
        fetch_window(plan, table, wins, mwin, msem, lo, hi, True)
        block_copies(q_ref, q_buf, qsem, lo, hi, True)

        def unpack(w, carry):
            got = mwin[w, T : T + 16, :].astype(WIDE)
            spare[0:16, :] = got[:, :T]
            spare[16:24, :] = jnp.concatenate([got[:8, T:], got[8:, T:]], axis=1)
            stats[w, 0 : 2 * HEADS, :] = spare[0 : 2 * HEADS, :] + spare[2 * HEADS : 4 * HEADS, :]
            return carry

        lax.fori_loop(lo, hi + 1, unpack, 0)

        def step(w, rows):
            seen = ids[rows] == row_ref[pl.ds(w, 1), :]
            copies = (rows.stop - rows.start) // (2 * part)

            def pair_rows(h):
                two = [jnp.broadcast_to(stats[w, h + k : h + k + 1, :], (part, T)) for k in range(2)]
                return jnp.concatenate(two * copies, axis=0)

            for p in range(pairs):
                cols = slice(LANES * p, LANES * (p + 1))
                q = q_buf[w, :, cols]
                g = mwin[w, 0:T, cols]
                s = jnp.where(seen, dot(ks[p][rows], q, NT), MASKED)
                prob = jnp.exp(s - pair_rows(2 * p))
                grad = prob * (dot(vs[p][rows], g, NT) - pair_rows(HEADS + 2 * p))
                acck[p, rows, :] = acck[p, rows, :] + dot(grad.astype(LOW), q, NN)
                accv[p, rows, :] = accv[p, rows, :] + dot(prob.astype(LOW), g, NN)

        sweep(plan, table, step)
        for p in range(pairs):
            gt[:, D + LANES * p : D + LANES * (p + 1)] = whole(acck[p]).astype(LOW)
            gt[:, 2 * D + LANES * p : 2 * D + LANES * (p + 1)] = whole(accv[p]).astype(LOW)
        gt[:, :D] = gq_ref[...]
        fold(flat, AT["triple"], normed_ref, gt, 3 * D)
        put_vector(flat, AT["tbias"], column_sum(gt[:, :D].astype(WIDE)))
        put_vector(flat, AT["tbias"] + D // LANES, column_sum(gt[:, 2 * D :].astype(WIDE)))
        load.wait()
        gn = dot(gt[...], triple_ref[...], NT)
        n, r = normalized(x_ref[...].astype(WIDE))
        put_vector(flat, AT["gain1"], column_sum(gn * n))
        put_vector(flat, AT["shift1"], column_sum(gn))
        flat[AT["out"] : AT["out"] + plan.rows, :] = tail_ref[...]

        def put(e, wait):
            t = table[e]

            @pl.when(t < half)
            def _():
                c = pltpu.make_async_copy(stage.at[e], keep_ref.at[t], osem.at[e])
                c.wait() if wait else c.start()

            @pl.when(t >= half)
            def _():
                c = pltpu.make_async_copy(stage.at[e], away_ref.at[t - half], osem.at[e])
                c.wait() if wait else c.start()

        for e in range(early):
            r0 = plan.start[e]
            stage[e] = flat[r0 : r0 + plan.rows, :].astype(LOW)
            put(e, False)
        gain1 = par_ref[VEC["gain1"] : VEC["gain1"] + 1, :D]
        grad_ref[...] = mid_ref[...] + norm_back(gn, gain1, n, r)
        for e in range(early):
            put(e, True)

    return kernel


def shape(dims, kind):
    return jax.ShapeDtypeStruct(dims, kind)


SMEM = pl.BlockSpec(memory_space=pltpu.SMEM)
VMEM = pl.BlockSpec(memory_space=pltpu.VMEM)
ANY = pl.BlockSpec(memory_space=pl.ANY)


def build(plan):
    T = plan.tokens
    W = plan.window
    R = plan.rows
    N = plan.count
    limit = pltpu.CompilerParams(vmem_limit_bytes=60 * 1024 * 1024)

    def per_device(inputs, cotangent, master, first_moment, second_moment, image_ids, spans):
        device = lax.axis_index(BOTH).astype(jnp.int32)
        shift = ((device * plan.share) % LANES).reshape(1).astype(jnp.int32)
        shifted = pl.pallas_call(
            shift_kernel(plan),
            in_specs=[SMEM, VMEM],
            out_specs=VMEM,
            out_shape=shape((R, LANES), LOW),
            scratch_shapes=[pltpu.VMEM((R + 8, LANES), WIDE)],
            name="shift",
        )(shift, jnp.pad(master, (0, R * LANES - plan.share)).reshape(R, LANES))
        near, core, (image_ids, spans) = plan.spread(shifted, (image_ids, spans))
        padded = jnp.pad(image_ids, (plan.reach * T, plan.reach * T), constant_values=-1)
        key_ids = lax.dynamic_slice_in_dim(padded, device * T, W * T, 0).reshape(W, T)
        table = plan.table(device, spans, key_ids)
        own_ids = key_ids[plan.reach]
        columns = jnp.broadcast_to(own_ids[:, None], (T, LANES))
        wins = plan.exchange(inputs)
        sources = len(wins)

        half = pltpu.VMEM((HEADS // 2, 2 * T, LANES), WIDE)
        unpack = pl.pallas_call(
            unpack_kernel(plan),
            in_specs=[SMEM, ANY, ANY],
            out_specs=[ANY] * 4 + [VMEM],
            out_shape=[
                shape((D, 3 * D), LOW),
                shape((D, D), LOW),
                shape((D, FF), LOW),
                shape((FF, D), LOW),
                shape((16, FF), WIDE),
            ],
            scratch_shapes=[
                pltpu.VMEM((N, R, LANES), LOW),
                pltpu.VMEM((plan.flat_rows, LANES), WIDE),
                pltpu.VMEM((D, 3 * D), LOW),
                pltpu.VMEM((D, D), LOW),
                pltpu.VMEM((D, FF), LOW),
                pltpu.VMEM((FF, D), LOW),
                pltpu.SemaphoreType.DMA((N,)),
                pltpu.SemaphoreType.DMA((4,)),
            ],
            compiler_params=limit,
            name="unpack",
        )
        triple, wo, wup, wdn, params = unpack(table, near, core)

        outs = pl.pallas_call(
            forward_kernel(plan, sources),
            in_specs=[SMEM] + [ANY] * sources + [VMEM] + [ANY] * 3 + [VMEM] * 4,
            out_specs=[VMEM] * 3 + [ANY] * 3 + [VMEM] * 2 + [ANY] * 2 + [VMEM] * 8,
            out_shape=[
                shape((T, D), LOW),
                shape((T + 16, D), LOW),
                shape((T, D), LOW),
                shape((W, T, D), LOW),
                shape((W, T, D), LOW),
                shape((W, T, D), LOW),
                shape((T, D), LOW),
                shape((T, D), WIDE),
                shape((T, FF), LOW),
                shape((T, FF), LOW),
                shape((T, D), LOW),
                shape((T, D), LOW),
                shape((T, D), LOW),
                shape((T, D), LOW),
                shape((8, FF), WIDE),
                shape((T, LANES), WIDE),
                shape((T, D), LOW),
                shape((T, D), LOW),
            ],
            scratch_shapes=[
                pltpu.VMEM((W, T, D), LOW),
                pltpu.VMEM((W, T, D), LOW),
                pltpu.VMEM((W, T, D), LOW),
                pltpu.VMEM((W, T, D), LOW),
                pltpu.VMEM((HEADS // 2, W, 2 * T, T), WIDE),
                half,
                half,
                half,
                pltpu.VMEM((T, D), WIDE),
                pltpu.VMEM((D, D), LOW),
                pltpu.VMEM((D, FF), LOW),
                pltpu.VMEM((FF, D), LOW),
                pltpu.VMEM((T, FF), LOW),
                pltpu.VMEM((T, FF), LOW),
                pltpu.SemaphoreType.DMA((W,)),
                pltpu.SemaphoreType.DMA((3, W)),
                pltpu.SemaphoreType.DMA((5,)),
            ],
            compiler_params=limit,
            name="forward",
        )(table, *wins, triple, wo, wup, wdn, params, cotangent, columns, key_ids)
        (
            result,
            message,
            q,
            k,
            v,
            norms,
            normed,
            gmid,
            act,
            gpre,
            gbt,
            n2,
            att,
            gbo,
            vec,
            stat,
            k_own,
            v_own,
        ) = outs
        messages = plan.exchange(message)

        query_call = pl.pallas_call(
            query_kernel(plan),
            in_specs=[SMEM, VMEM, ANY, ANY] + [VMEM] * 4,
            out_specs=VMEM,
            out_shape=shape((T, D), LOW),
            scratch_shapes=[
                half,
                half,
                half,
                pltpu.VMEM((W, T, D), LOW),
                pltpu.VMEM((W, T, D), LOW),
                pltpu.SemaphoreType.DMA((W,)),
                pltpu.SemaphoreType.DMA((W,)),
            ],
            compiler_params=limit,
            name="query",
        )
        gq = query_call(table, q, k, v, message, stat, columns, key_ids)
        weight_call = pl.pallas_call(
            weight_kernel(plan),
            in_specs=[SMEM, ANY] + [VMEM] * 9,
            out_specs=[ANY] * 3 + [VMEM],
            out_shape=[
                shape((W, T, D), LOW),
                shape((N // 2, R, LANES), LOW),
                shape((N // 2, R, LANES), LOW),
                shape((R, LANES), WIDE),
            ],
            scratch_shapes=[
                pltpu.VMEM((-(-(plan.flat_rows - AT["out"]) // 8) * 8 + 8, LANES), WIDE),
                pltpu.VMEM((N - plan.first_late, R, LANES), LOW),
                pltpu.VMEM((W, T, D), LOW),
                pltpu.VMEM((W, T, D), LOW),
                pltpu.SemaphoreType.DMA((W,)),
                pltpu.SemaphoreType.DMA((W,)),
                pltpu.SemaphoreType.DMA((N - plan.first_late,)),
            ],
            compiler_params=limit,
            name="weight",
        )
        queries, keep, away, tail = weight_call(
            table, norms, triple, params, act, gpre, gbt, n2, att, gbo, vec
        )

        late = plan.first_late
        input_grad, keep, away = pl.pallas_call(
            last_kernel(plan, sources),
            in_specs=[SMEM] + [ANY] * (sources + 1) + [VMEM] * 6 + [ANY] + [VMEM] * 4 + [ANY, ANY],
            out_specs=[VMEM, ANY, ANY],
            out_shape=[
                shape((T, D), WIDE),
                shape((N // 2, R, LANES), LOW),
                shape((N // 2, R, LANES), LOW),
            ],
            scratch_shapes=[
                pltpu.VMEM((W, T + 16, D), LOW),
                pltpu.VMEM((W, T, D), LOW),
                pltpu.VMEM((D, 3 * D), LOW),
                pltpu.VMEM((-(-(AT["out"] + R) // 8) * 8 + 8, LANES), WIDE),
                pltpu.VMEM((T, 3 * D), LOW),
                pltpu.VMEM((late, R, LANES), LOW),
                pltpu.VMEM((W, 16, T), WIDE),
                pltpu.VMEM((24, T), WIDE),
                half,
                half,
                pltpu.SemaphoreType.DMA((W,)),
                pltpu.SemaphoreType.DMA((W,)),
                pltpu.SemaphoreType.DMA((1,)),
                pltpu.SemaphoreType.DMA((late,)),
            ],
            input_output_aliases={13 + sources: 1, 14 + sources: 2},
            compiler_params=limit,
            name="last",
        )(
            table,
            *messages,
            queries,
            k_own,
            v_own,
            columns,
            key_ids,
            gq,
            normed,
            triple,
            inputs,
            gmid,
            params,
            tail,
            keep,
            away,
        )

        parts = plan.reduce_parts(keep, away)
        grad, square = pl.pallas_call(
            unshift_kernel(plan),
            in_specs=[SMEM] + [VMEM] * len(parts),
            out_specs=[VMEM, VMEM],
            out_shape=[shape((R, LANES), WIDE), shape((N, LANES), WIDE)],
            scratch_shapes=[pltpu.VMEM((R + 8, LANES), WIDE)],
            name="unshift",
        )(shift, *parts)
        grad_shard = grad.reshape(-1)[: plan.share]
        squares = lax.all_to_all(square, BOTH, 0, 0, tiled=True)
        grad_norm = jnp.sqrt(jnp.sum(squares[:, 0]))
        ceiling = CLIP_RATIO * math.sqrt(plan.share * N)
        factor = ceiling / jnp.maximum(grad_norm, ceiling)
        clipped = grad_shard * factor
        new_first = BETA_ONE * first_moment + (1.0 - BETA_ONE) * clipped
        new_second = BETA_TWO * second_moment + (1.0 - BETA_TWO) * clipped * clipped
        new_master = master - LEARN_RATE * (
            new_first / (jnp.sqrt(new_second) + ADAM_EPS) + WEIGHT_DECAY * master
        )
        return (
            result,
            input_grad,
            grad_shard,
            grad_norm.reshape(1),
            new_first,
            new_second,
            new_master,
        )

    return per_device


def solution(mesh):
    dp = mesh.shape["dp"]
    fsdp = mesh.shape["fsdp"]
    row = P(BOTH, None)
    flat = P(BOTH)
    in_specs = (row, row, flat, flat, flat, P(), P())
    out_specs = (row, row, flat, P(), flat, flat, flat)

    def per_device(*args):
        inputs, master = args[0], args[2]
        plan = Plan(dp, fsdp, master.shape[0], inputs.shape[0])
        return build(plan)(*args)

    return jax.shard_map(
        per_device, mesh=mesh, in_specs=in_specs, out_specs=out_specs, check_vma=False
    )
```
